128 devices in a mesh: dp: 8 (over x, core), seq: 16 (over z, y).
Axes of the slice: x: 4, y: 4, z: 4, core: 2. Of those that a mesh axis runs over, the one named last changes fastest.
Arguments:
- queries: bfloat16 [8, 2048, 4096], P('dp', 'seq'), may hold values from -24 to 24
- keys: bfloat16 [8, 2048, 1024], P('dp', 'seq'), may hold values from -6 to 6
- values: bfloat16 [8, 2048, 1024], P('dp', 'seq'), may hold values from -48 to 48
- stem_kv: bfloat16 [8, 2, 4096, 1024], P('dp', None, 'seq'), may hold values from -48 to 48
- seg_ids: int32 [8, 2048], P('dp'), may hold values from 0 to 15, never falling along the last dimension, each value on 1 to 512 neighbouring positions
- seg_parent: int32 [8, 16], P('dp'), may hold values from 0 to 14, as said below
- stem_owner: int32 [8], replicated, may hold values from 0 to 7
Outputs:
- attended: bfloat16 [8, 2048, 4096], P('dp', 'seq')
The draws below stay inside these ranges and needn't reach their ends.
Inputs may be any that keep to these rules, and one draw needn't show every extreme that they name: seg_parent[g, 0] = 0 and seg_parent[g, s] < s for s >= 1, so each pack's segments form a tree rooted at segment 0. Pack g attends to the stem stored by group stem_owner[g].
All inputs are finite; a program needn't handle non-finite values.
Results may differ from the reference program's by a relative error of at most 0.0088.
Values may be sent and summed in bfloat16 or wider, within the bound.
No kernel may reach another device: no remote copies, remote signals or barrier semaphores. Data moves between devices by JAX's collectives and lax.ppermute only.
A program may use at most 64 MiB of HBM per device.

```python
import math
import jax
import jax.numpy as jnp
import numpy as np
from jax import lax

H = 32
KVH = 8
HD = 128
STEM = 4096
SEGS = 16
PACK = 2048
N_DP = 8


AMPLE = 4.0


def sign_table(key):
    flips = jax.random.bernoulli(jax.random.fold_in(key, 11), 0.5, (KVH, HD // 2))
    return 2.0 * flips.astype(jnp.float32) - 1.0


def strength(block_ids):
    phase_index = block_ids % 3
    return jnp.where(phase_index == 0, 3.0, jnp.where(phase_index == 1, 4.5, 6.0))


def column_pattern(key, width):
    columns = jnp.arange(width, dtype=jnp.int32)
    head_ids = columns // HD
    pair_ids = columns % HD % (HD // 2)
    low_band = pair_ids >= 3 * HD // 8
    return (head_ids, pair_ids, low_band)


def token_plant():
    period = min(512, PACK)
    tokens = jnp.arange(PACK, dtype=jnp.int32)
    chosen = tokens % period == 100 % period
    return (chosen, strength(tokens // 512))


def draw_queries(key, part):
    base_key = jax.random.fold_in(key, 21)
    base_draw = 2.0 * jax.random.truncated_normal(base_key, -6.0, 6.0, (N_DP, PACK, H * HD), jnp.float32)
    signs = sign_table(key)
    head_ids, pair_ids, low_band = column_pattern(key, H * HD)
    lead_head = head_ids % (H // KVH) == 0
    pattern = signs[head_ids // (H // KVH), pair_ids]
    chosen, boost_rows = token_plant()
    planted = jnp.where(low_band[None, :], AMPLE * boost_rows[:, None] * pattern[None, :], 0.0)
    row_mask = chosen[:, None] & lead_head[None, :]
    return jnp.where(row_mask[None], planted[None], base_draw).astype(jnp.bfloat16)


def draw_keys(key, part):
    base_key = jax.random.fold_in(key, 22)
    base_draw = jax.random.truncated_normal(base_key, -6.0, 6.0, (N_DP, PACK, KVH * HD), jnp.float32)
    signs = sign_table(key)
    head_ids, pair_ids, low_band = column_pattern(key, KVH * HD)
    pattern = signs[head_ids, pair_ids]
    chosen, boost_rows = token_plant()
    planted = jnp.where(low_band, AMPLE * pattern, 0.0)
    return jnp.where(chosen[None, :, None], planted[None, None, :], base_draw).astype(jnp.bfloat16)


def draw_stem_kv(key, part):
    key_draw = jax.random.fold_in(key, 23)
    value_draw = jax.random.fold_in(key, 24)
    shape = (N_DP, STEM, KVH * HD)
    stem_keys = jax.random.truncated_normal(key_draw, -6.0, 6.0, shape, jnp.float32)
    stem_values = 8.0 * jax.random.truncated_normal(value_draw, -6.0, 6.0, shape, jnp.float32)
    signs = sign_table(key)
    head_ids, pair_ids, low_band = column_pattern(key, KVH * HD)
    pattern = signs[head_ids, pair_ids]
    period = min(64, STEM)
    stem_rows = jnp.arange(STEM, dtype=jnp.int32)
    planted_count = max(1, PACK // 512)
    chosen = (stem_rows % period == 7 % period) & (stem_rows // 64 < planted_count)
    boost_rows = strength(stem_rows // 64)
    planted = jnp.where(low_band[None, :], (AMPLE - 0.18 / boost_rows[:, None]) * pattern[None, :], 0.0)
    stem_keys = jnp.where(chosen[None, :, None], planted[None], stem_keys)
    return jnp.stack([stem_keys, stem_values], axis=1).astype(jnp.bfloat16)


def draw_seg_parent(key, part):
    limits = jnp.maximum(jnp.arange(SEGS, dtype=jnp.int32), 1)
    drawn = jax.random.randint(key, (N_DP, SEGS), 0, limits[None, :]).astype(jnp.int32)
    rows = jnp.arange(N_DP, dtype=jnp.int32)[:, None]
    cols = jnp.arange(SEGS, dtype=jnp.int32)[None, :]
    last_link = (rows == 0) & (cols == SEGS - 1)
    return jnp.where(last_link, SEGS - 2, drawn).astype(jnp.int32)


def set_ends(values, key, smallest, high):
    index_at = [jax.random.randint(jax.random.fold_in(key, axis), (), 0, length) for axis, length in enumerate(values.shape)]
    main_axis = values.shape.index(max(values.shape))
    neighbour = index_at[:main_axis] + [(index_at[main_axis] + 1) % values.shape[main_axis]] + index_at[main_axis + 1:]
    return values.at[tuple(index_at)].set(smallest).at[tuple(neighbour)].set(high)


def levels(stream_key, shape, shards, low, largest):
    gain, own = 1.0, jax.random.fold_in(stream_key, 6)
    for axis_at, blocks in shards:
        draws = jnp.exp(jax.random.uniform(jax.random.fold_in(own, axis_at), (blocks,), jnp.float32, low / len(shards), largest / len(shards)))
        gain = gain * jnp.repeat(draws, shape[axis_at] // blocks).reshape([-1 if axis == axis_at else 1 for axis in range(len(shape))])
    return gain


def cumulative_ranks(count, slope):
    loads = [(1 << 20) // math.isqrt(standing ** slope) + 1 for standing in range(1, count + 1)]
    scale = 1 + sum(loads) // (1 << 30)
    return np.cumsum(np.array([max(1, weight // scale) for weight in loads]))


def ranked(key, dims, amount, lean):
    table = cumulative_ranks(amount, lean)
    ticket = jax.random.randint(jax.random.fold_in(key, 1), dims, 0, int(table[amount - 1]))
    standing = jnp.searchsorted(jnp.asarray(table, jnp.int32), ticket, side="right")
    return jax.random.permutation(jax.random.fold_in(key, 2), amount)[standing].astype(jnp.int32)


def split_up(count, total, most, slope):
    weights = [(1 << 20) // math.isqrt(grade ** slope) + 1 for grade in range(2, count + 1)]
    spare, counts = total - most - (count - 1), [1] * (count - 1)
    while spare > 0:
        free = [i for i in range(count - 1) if counts[i] < most]
        mass, remaining = sum([weights[i] for i in free]), spare
        for i in free:
            more = min(most - counts[i], max(1, remaining * weights[i] // mass), spare)
            counts[i] = counts[i] + more
            spare = spare - more
    return np.array([most] + counts)


def uneven_parts(rng, count, total, bound, skew):
    if count == 2:
        one = jax.random.randint(rng, (), max(1, total - bound), min(bound, total - 1) + 1)
        return jnp.stack([one, total - one])
    sizes = jnp.asarray(split_up(count, total, bound, skew), jnp.int32)
    twos = (count - 1) // 2
    giver, receiver = sizes[1:1 + 2 * twos:2], sizes[2:2 + 2 * twos:2]
    slack = jnp.minimum(giver - 1, bound - receiver)
    moved = jax.random.randint(jax.random.fold_in(rng, 1), (twos,), 0, 1 << 20) % (slack + 1)
    sizes = sizes.at[1:1 + 2 * twos:2].set(giver - moved).at[2:2 + 2 * twos:2].set(receiver + moved)
    return sizes[jax.random.permutation(jax.random.fold_in(rng, 2), count)]


def scatter_about(key, extent, scale, limit, pieces=(), kind=jnp.bfloat16):
    level = levels(key, extent, pieces, -0.22, 0.18) if pieces else 1.0
    result = jax.random.normal(key, extent, jnp.float32) * scale * level
    return jnp.minimum(jnp.maximum(result, -limit), limit).astype(kind)


def setup_inputs(seed: int = 0) -> dict:
    key_list = jax.random.split(jax.random.key(seed), 8)
    queries = draw_queries(jax.random.fold_in(key_list[7], 71), 0)
    keys = draw_keys(jax.random.fold_in(key_list[7], 71), 0)
    values = scatter_about(key_list[2], (N_DP, PACK, KVH * HD), 8.0, 48.0, ((0, 8), (1, 16)))
    stem_kv = draw_stem_kv(jax.random.fold_in(key_list[7], 71), 0)
    seg_ids = jax.vmap(lambda own: jnp.searchsorted(jnp.cumsum(uneven_parts(own, SEGS, PACK, PACK // 4, 2)), jnp.arange(PACK), side="right"))(jax.random.split(key_list[4], N_DP)).reshape((N_DP, PACK)).astype(jnp.int32)
    seg_parent = draw_seg_parent(jax.random.fold_in(key_list[7], 71), 0)
    stem_owner = set_ends(ranked(key_list[6], (N_DP,), N_DP, 2), jax.random.fold_in(key_list[6], 3), 0, N_DP - 1).astype(jnp.int32)
    return dict(queries=queries, keys=keys, values=values, stem_kv=stem_kv, seg_ids=seg_ids, seg_parent=seg_parent, stem_owner=stem_owner)


def rotary_table():
    halves = np.arange(0, HD, 2) / HD
    inverse = 1.0 / (500000.0 ** halves)
    wavelen = 2.0 * np.pi / inverse
    smooth = (8192.0 / wavelen - 1.0) / 3.0
    blended = (1.0 - smooth) * inverse / 8.0 + smooth * inverse
    scaled = np.where(wavelen < 2048.0, inverse, np.where(wavelen > 8192.0, inverse / 8.0, blended))
    return jnp.asarray(scaled, dtype=jnp.float32)


def rotate(head_block, places):
    rotary = rotary_table()
    angles = places[:, None] * rotary[None, :]
    cosine = jnp.concatenate([jnp.cos(angles), jnp.cos(angles)], axis=1)[:, None, :]
    sine_full = jnp.concatenate([jnp.sin(angles), jnp.sin(angles)], axis=1)[:, None, :]
    widened = head_block.astype(jnp.float32)
    rolled = jnp.concatenate([-widened[..., HD // 2:], widened[..., : HD // 2]], axis=-1)
    return (widened * cosine + rolled * sine_full).astype(jnp.bfloat16)


def ancestry(parents):
    seg_count = parents.shape[0]
    indices = jnp.arange(seg_count, dtype=jnp.int32)
    linked = ((indices[:, None] == indices[None, :]) | (parents[:, None] == indices[None, :])).astype(jnp.float32)
    for sweep in range(max(1, (seg_count - 1).bit_length())):
        linked = (jnp.dot(linked, linked, precision=lax.Precision.HIGHEST, preferred_element_type=jnp.float32) > 0.5).astype(jnp.float32)
    return linked


def token_places(seg_row, linked):
    seg_count = linked.shape[0]
    onehot = (seg_row[:, None] == jnp.arange(seg_count, dtype=jnp.int32)[None, :]).astype(jnp.float32)
    lengths = jnp.sum(onehot, axis=0)
    starts = jnp.cumsum(lengths) - lengths
    before = jnp.sum(linked * lengths[None, :], axis=1) - lengths
    token_ids = jnp.arange(seg_row.shape[0], dtype=jnp.int32).astype(jnp.float32)
    return STEM + token_ids - jnp.sum(onehot * starts[None, :], axis=1) + jnp.sum(onehot * before[None, :], axis=1)


def reference(queries, keys, values, stem_kv, seg_ids, seg_parent, stem_owner):
    group_size = H // KVH
    score_scale = HD ** -0.5

    def one_pack(pack_index):
        linked = ancestry(seg_parent[pack_index])
        seg_row = seg_ids[pack_index]
        places = token_places(seg_row, linked)
        q_rot = rotate(queries[pack_index].reshape(PACK, H, HD), places)
        k_rot = rotate(keys[pack_index].reshape(PACK, KVH, HD), places)
        v_all = values[pack_index].reshape(PACK, KVH, HD)
        stem_pair = lax.dynamic_index_in_dim(stem_kv, stem_owner[pack_index], 0, keepdims=False).reshape(2, STEM, KVH, HD)
        onehot = (seg_row[:, None] == jnp.arange(SEGS, dtype=jnp.int32)[None, :]).astype(jnp.float32)
        reach_rows = jnp.dot(onehot, linked, precision=lax.Precision.HIGHEST, preferred_element_type=jnp.float32)
        reach_mask = jnp.dot(reach_rows, onehot.T, precision=lax.Precision.HIGHEST, preferred_element_type=jnp.float32) > 0.5
        token_ids = jnp.arange(PACK, dtype=jnp.int32)
        visible = jnp.concatenate([jnp.ones((PACK, STEM), dtype=jnp.bool_), reach_mask & (token_ids[None, :] <= token_ids[:, None])], axis=1)

        def one_head(head_index):
            kv_head = head_index // group_size
            query_rows = lax.dynamic_index_in_dim(q_rot, head_index, 1, keepdims=False)
            key_set = jnp.concatenate([lax.dynamic_index_in_dim(stem_pair[0], kv_head, 1, keepdims=False), lax.dynamic_index_in_dim(k_rot, kv_head, 1, keepdims=False)], axis=0)
            value_set = jnp.concatenate([lax.dynamic_index_in_dim(stem_pair[1], kv_head, 1, keepdims=False), lax.dynamic_index_in_dim(v_all, kv_head, 1, keepdims=False)], axis=0)
            scores = jnp.dot(query_rows, key_set.T, preferred_element_type=jnp.float32) * score_scale
            masked = jnp.where(visible, scores, -jnp.inf)
            row_max = jnp.max(masked, axis=1, keepdims=True)
            exp_scores = jnp.exp(masked - row_max)
            totals = jnp.sum(exp_scores, axis=1, keepdims=True)
            mixed_sum = jnp.dot(exp_scores.astype(jnp.bfloat16), value_set, preferred_element_type=jnp.float32)
            return (mixed_sum / totals).astype(jnp.bfloat16)

        per_head = lax.map(one_head, jnp.arange(H, dtype=jnp.int32))
        return jnp.transpose(per_head, (1, 0, 2)).reshape(PACK, H * HD)

    return lax.map(one_pack, jnp.arange(N_DP, dtype=jnp.int32))
```

```python
import functools
import math

import jax
import jax.numpy as jnp
import numpy as np
from jax import lax
from jax.experimental import pallas as pl
from jax.experimental.pallas import tpu as pltpu
from jax.sharding import PartitionSpec as P

H = 32
KVH = 8
HD = 128
STEM = 4096
SEGS = 16


def as_sent(value):

    def short(part):
        return part.astype(jnp.bfloat16) if part.dtype == jnp.float32 else part

    return jax.tree.map(short, value)


def rotary_table():
    halves = np.arange(0, HD, 2) / HD
    inverse = 1.0 / 500000.0**halves
    wavelen = 2.0 * np.pi / inverse
    smooth = (8192.0 / wavelen - 1.0) / 3.0
    blended = (1.0 - smooth) * inverse / 8.0 + smooth * inverse
    scaled = np.where(wavelen < 2048.0, inverse, np.where(wavelen > 8192.0, inverse / 8.0, blended))
    return jnp.asarray(scaled, dtype=jnp.float32)


def rotate(head_block, places):
    rotary = rotary_table()
    angles = places[:, None] * rotary[None, :]
    cosine = jnp.concatenate([jnp.cos(angles), jnp.cos(angles)], axis=1)[:, None, :]
    sine_full = jnp.concatenate([jnp.sin(angles), jnp.sin(angles)], axis=1)[:, None, :]
    widened = head_block.astype(jnp.float32)
    rolled = jnp.concatenate([-widened[..., HD // 2 :], widened[..., : HD // 2]], axis=-1)
    return (widened * cosine + rolled * sine_full).astype(jnp.bfloat16)


def ancestry(parents):
    seg_count = parents.shape[0]
    indices = jnp.arange(seg_count, dtype=jnp.int32)
    linked = (
        (indices[:, None] == indices[None, :]) | (parents[:, None] == indices[None, :])
    ).astype(jnp.float32)
    for sweep in range(max(1, (seg_count - 1).bit_length())):
        linked = (
            jnp.dot(
                linked, linked, precision=lax.Precision.HIGHEST, preferred_element_type=jnp.float32
            )
            > 0.5
        ).astype(jnp.float32)
    return linked


def token_places(seg_row, linked):
    seg_count = linked.shape[0]
    onehot = (seg_row[:, None] == jnp.arange(seg_count, dtype=jnp.int32)[None, :]).astype(
        jnp.float32
    )
    lengths = jnp.sum(onehot, axis=0)
    starts = jnp.cumsum(lengths) - lengths
    before = jnp.sum(linked * lengths[None, :], axis=1) - lengths
    token_ids = jnp.arange(seg_row.shape[0], dtype=jnp.int32).astype(jnp.float32)
    return (
        STEM
        + token_ids
        - jnp.sum(onehot * starts[None, :], axis=1)
        + jnp.sum(onehot * before[None, :], axis=1)
    )


BARRED = -1e30
BQ = 512
SCALE=HD**-0.5*math.log2(math.e)
SHIFT=60.0/SCALE
TINY=2.0**-60
NT=(((1,),(1,)),((),()))

def attn_kernel(vis_ref, q_ref, qb_ref, kb_ref, ks_ref, vs_ref, kp_ref, vp_ref, o_ref, qa, ka, va, kap, vap, acc, kmax, *, BQ, CK, stem, pack):
    qi=pl.program_id(0)
    R=2*BQ
    lane=lax.broadcasted_iota(jnp.int32,(1,128),1)
    @pl.when(qi==0)
    def _():
        def sq(x):
            x=x.astype(jnp.float32); return jnp.max(jnp.sum(x*x,axis=1,keepdims=True),axis=0,keepdims=True)
        ka[:, :128]=ks_ref[...]
        ka[:, 128:]=jnp.broadcast_to(jnp.where(lane==16,-1.0,0.0).astype(jnp.bfloat16),(stem,128))
        va[:, :128]=vs_ref[...]
        va[:, 128:]=jnp.ones((stem,128),jnp.bfloat16)
        kap[:, :128]=kp_ref[...]
        kap[:, 128:]=kb_ref[...]
        vap[:, :128]=vp_ref[...]
        vap[:, 128:]=jnp.ones((pack,128),jnp.bfloat16)
        m=jnp.zeros((1,1),jnp.float32)
        for c in range(stem//512):
            m=jnp.maximum(m,sq(ks_ref[pl.ds(c*512,512),:]))
        for c in range(pack//512):
            m=jnp.maximum(m,sq(kp_ref[pl.ds(c*512,512),:]))
        kmax[...]=jnp.broadcast_to(jnp.sqrt(m),(8,128))
    qf=jnp.concatenate([q_ref[:, :128],q_ref[:,128:]],axis=0)
    qa[:, :128]=qf
    qb=qb_ref[...]
    qb2=jnp.concatenate([qb,qb],axis=0)
    q32=qf.astype(jnp.float32)
    bound=jnp.sqrt(jnp.sum(q32*q32,axis=1,keepdims=True))*kmax[0:1,0:1]*1.02-SHIFT

    def set_m(m):
        qa[:,128:]=jnp.where(lane==16,m,qb2.astype(jnp.float32)).astype(jnp.bfloat16)

    def scores(kref,start,size):
        return lax.dot_general(qa[...],kref[pl.ds(start,size),:],NT,preferred_element_type=jnp.float32)

    def run():
        n=stem//CK
        a=None
        s=scores(ka,0,CK)
        for c in range(n):
            s_next=scores(ka,(c+1)*CK,CK) if c+1<n else None
            p=jnp.exp2(s*SCALE).astype(jnp.bfloat16)
            d=jnp.dot(p,va[pl.ds(c*CK,CK),:],preferred_element_type=jnp.float32)
            a=d if a is None else a+d
            s=s_next
        st=pl.multiple_of(qi*BQ,BQ)
        s=scores(kap,st,BQ)
        r=lax.broadcasted_iota(jnp.int32,(R,BQ),0)
        r=jnp.where(r>=BQ,r-BQ,r)
        col=lax.broadcasted_iota(jnp.int32,(R,BQ),1)
        p=jnp.where(col<=r,jnp.exp2(s*SCALE),0.0).astype(jnp.bfloat16)
        a=a+jnp.dot(p,vap[pl.ds(st,BQ),:],preferred_element_type=jnp.float32)
        acc[...]=a
        def body(kj,_):
            @pl.when(vis_ref[qi,kj]>0)
            def _():
                st=pl.multiple_of(kj*BQ,BQ)
                p=jnp.exp2(scores(kap,st,BQ)*SCALE).astype(jnp.bfloat16)
                acc[...]+=jnp.dot(p,vap[pl.ds(st,BQ),:],preferred_element_type=jnp.float32)
            return 0
        lax.fori_loop(0,qi,body,0)

    def finish():
        a=acc[...]
        o=(a[:, :128]/a[:,128:129]).astype(jnp.bfloat16)
        o_ref[:, :128]=o[:BQ]
        o_ref[:, 128:]=o[BQ:]
    set_m(bound)
    run()
    finish()
    low=jnp.min(acc[:,128:])
    @pl.when(low<TINY)
    def _():
        set_m(jnp.zeros((R,1),jnp.float32))
        def smax(c,m):
            return jnp.maximum(m,jnp.max(scores(ka,pl.multiple_of(c*512,512),512),axis=1,keepdims=True))
        m=lax.fori_loop(0,stem//512,smax,jnp.full((R,1),-1e30,jnp.float32))
        def pmax(kj,m):
            s=scores(kap,pl.multiple_of(kj*BQ,BQ),BQ)
            r=lax.broadcasted_iota(jnp.int32,(R,BQ),0)
            r=jnp.where(r>=BQ,r-BQ,r)+qi*BQ
            col=lax.broadcasted_iota(jnp.int32,(R,BQ),1)+kj*BQ
            return jnp.maximum(m,jnp.max(jnp.where(col<=r,s,-1e30),axis=1,keepdims=True))
        m=lax.fori_loop(0,qi+1,pmax,m)
        set_m(m)
        run()
        finish()

def attention(vis,q,qb,kb,ks,vs,kp,vp,*,BQ=256,CK=512):
    stem=ks.shape[0]; pack=q.shape[0]
    full=lambda n:pl.BlockSpec((n,128),lambda i,v:(0,0),pipeline_mode=pl.Buffered(1))
    return pl.pallas_call(
        functools.partial(attn_kernel,BQ=BQ,CK=CK,stem=stem,pack=pack),
        out_shape=jax.ShapeDtypeStruct((pack,256),jnp.bfloat16),
        grid_spec=pltpu.PrefetchScalarGridSpec(num_scalar_prefetch=1,grid=(pack//BQ,),
            in_specs=[pl.BlockSpec((BQ,256),lambda i,v:(i,0)),pl.BlockSpec((BQ,128),lambda i,v:(i,0)),full(pack),full(stem),full(stem),full(pack),full(pack)],
            out_specs=pl.BlockSpec((BQ,256),lambda i,v:(i,0)),
            scratch_shapes=[pltpu.VMEM((2*BQ,256),jnp.bfloat16),pltpu.VMEM((stem,256),jnp.bfloat16),pltpu.VMEM((stem,256),jnp.bfloat16),
                pltpu.VMEM((pack,256),jnp.bfloat16),pltpu.VMEM((pack,256),jnp.bfloat16),pltpu.VMEM((2*BQ,256),jnp.float32),pltpu.VMEM((8,128),jnp.float32)]),
        compiler_params=pltpu.CompilerParams(vmem_limit_bytes=56*1024*1024),
        name="attn",
    )(vis,q,qb,kb,ks,vs,kp,vp)


def shards(queries, keys, values, stem_kv, seg_ids, seg_parent, stem_owner):
    tok_count = queries.shape[1]
    seq_count = lax.axis_size("seq")
    pack_len = tok_count * seq_count
    group_size = H // KVH
    local_heads = H // seq_count
    repeat = max(1, seq_count // KVH)
    kv_local = max(KVH, seq_count) // seq_count
    seg_row = seg_ids[0]
    linked = ancestry(seg_parent[0])
    places = token_places(seg_row, linked)
    own_places = lax.dynamic_slice_in_dim(places, lax.axis_index("seq") * tok_count, tok_count)
    q_rot = rotate(queries[0].reshape(tok_count, H, HD), own_places).reshape(tok_count, H * HD)
    k_rot = rotate(keys[0].reshape(tok_count, KVH, HD), own_places)
    k_wide = jnp.repeat(k_rot, repeat, axis=1).reshape(tok_count, repeat * KVH * HD)
    v_wide = jnp.repeat(values[0].reshape(tok_count, KVH, HD), repeat, axis=1).reshape(
        tok_count, repeat * KVH * HD
    )
    q_heads, k_heads, v_heads = (
        lax.all_to_all(q_rot, "seq", split_axis=1, concat_axis=0, tiled=True),
        lax.all_to_all(k_wide, "seq", split_axis=1, concat_axis=0, tiled=True),
        lax.all_to_all(v_wide, "seq", split_axis=1, concat_axis=0, tiled=True),
    )
    owner_group = lax.dynamic_index_in_dim(stem_owner, lax.axis_index("dp"), 0, keepdims=False)
    empty_block = jnp.zeros(stem_kv.shape[1:], jnp.bfloat16)
    incoming = lax.all_gather(stem_kv, "dp", axis=0, tiled=True)
    inside = (owner_group >= 0) & (owner_group < incoming.shape[0])
    chosen = lax.dynamic_index_in_dim(
        incoming, jnp.clip(owner_group, 0, incoming.shape[0] - 1), 0, keepdims=False
    )
    owned = jnp.where(inside, chosen, empty_block)
    stem_rows = owned.shape[1]
    stem_wide = jnp.repeat(owned.reshape(2, stem_rows, KVH, HD), repeat, axis=2).reshape(
        2, stem_rows, repeat * KVH * HD
    )
    stem_heads = lax.all_to_all(stem_wide, "seq", split_axis=2, concat_axis=1, tiled=True)
    onehot = (seg_row[:, None] == jnp.arange(128, dtype=jnp.int32)[None, :]).astype(jnp.float32)
    barred = jnp.pad(BARRED * (1.0 - linked), ((0, 112), (0, 112)))
    q_bias = jnp.dot(onehot, barred, precision=lax.Precision.HIGHEST).astype(jnp.bfloat16)
    k_bias = jnp.where(jnp.arange(128)[None, :] == SEGS, -1.0, onehot).astype(jnp.bfloat16)
    present = onehot.reshape(pack_len // BQ, BQ, 128).max(axis=1)[:, :SEGS]
    seen = (present @ linked @ present.T > 0.5).astype(jnp.int32)
    attended_heads = attention(
        seen, q_heads, q_bias, k_bias, stem_heads[0], stem_heads[1], k_heads, v_heads, BQ=BQ, CK=256
    )
    back = lax.all_to_all(attended_heads, "seq", split_axis=0, concat_axis=1, tiled=True)
    return back.reshape(1, tok_count, H * HD)


def solution(mesh):
    placed = (
        P("dp", "seq", None),
        P("dp", "seq", None),
        P("dp", "seq", None),
        P("dp", None, "seq", None),
        P("dp", None),
        P("dp", None),
        P(),
    )
    return jax.shard_map(
        shards, mesh=mesh, in_specs=placed, out_specs=P("dp", "seq", None), check_vma=False
    )
```

```python
import functools
import math

import jax
import jax.numpy as jnp
import numpy as np
from jax import lax
from jax.experimental import pallas as pl
from jax.experimental.pallas import tpu as pltpu
from jax.sharding import Mesh
from jax.sharding import PartitionSpec as P

H = 32
KVH = 8
HD = 128
STEM = 4096
SEGS = 16
BARRED = -1e30
BQ = 512
CK = 256
SCALE = HD**-0.5 * math.log2(math.e)
SHIFT = 70.0 / SCALE
TINY = 2.0**-16
FLIP = [(0, 1), (1, 0)]
NEAR = [(0, 1), (1, 0), (2, 3), (3, 2)]
FAR = [(0, 3), (3, 0), (1, 2), (2, 1)]
SEQ = ("z", "y")
NT = (((1,), (1,)), ((), ()))
ROOM = 56 * 1024 * 1024


def rotary_table():
    halves = np.arange(0, HD, 2) / HD
    inverse = 1.0 / 500000.0**halves
    wavelen = 2.0 * np.pi / inverse
    smooth = (8192.0 / wavelen - 1.0) / 3.0
    blended = (1.0 - smooth) * inverse / 8.0 + smooth * inverse
    scaled = np.where(wavelen < 2048.0, inverse, np.where(wavelen > 8192.0, inverse / 8.0, blended))
    return jnp.asarray(scaled, dtype=jnp.float32)


def ancestry(parents):
    seg_count = parents.shape[0]
    indices = jnp.arange(seg_count, dtype=jnp.int32)
    linked = (
        (indices[:, None] == indices[None, :]) | (parents[:, None] == indices[None, :])
    ).astype(jnp.float32)
    for sweep in range(max(1, (seg_count - 1).bit_length())):
        linked = (
            jnp.dot(
                linked, linked, precision=lax.Precision.HIGHEST, preferred_element_type=jnp.float32
            )
            > 0.5
        ).astype(jnp.float32)
    return linked


def token_places(seg_row, linked):
    seg_count = linked.shape[0]
    onehot = (seg_row[:, None] == jnp.arange(seg_count, dtype=jnp.int32)[None, :]).astype(
        jnp.float32
    )
    lengths = jnp.sum(onehot, axis=0)
    starts = jnp.cumsum(lengths) - lengths
    before = jnp.sum(linked * lengths[None, :], axis=1) - lengths
    token_ids = jnp.arange(seg_row.shape[0], dtype=jnp.int32).astype(jnp.float32)
    return (
        STEM
        + token_ids
        - jnp.sum(onehot * starts[None, :], axis=1)
        + jnp.sum(onehot * before[None, :], axis=1)
    )


def turn_kernel(q_ref, k_ref, v_ref, cos_ref, sin_ref, o_ref):
    cosine = cos_ref[...]
    sine = sin_ref[...]

    def turned(part):
        wide = part.astype(jnp.float32)
        return (wide * cosine + pltpu.roll(wide, HD // 2, 1) * sine).astype(jnp.bfloat16)

    for head in range(4):
        at = head % 2 * HD
        o_ref[head // 2, 0, :, at : at + HD] = turned(q_ref[:, head * HD : head * HD + HD])
    o_ref[0, 0, :, 2 * HD :] = turned(k_ref[...])
    o_ref[1, 0, :, 2 * HD :] = v_ref[...]


def turn(q, k, v, cosine, sine):
    tok = q.shape[0]
    return pl.pallas_call(
        turn_kernel,
        out_shape=jax.ShapeDtypeStruct((2, KVH, tok, 3 * HD), jnp.bfloat16),
        grid=(KVH,),
        in_specs=[
            pl.BlockSpec((tok, 4 * HD), lambda e: (0, e)),
            pl.BlockSpec((tok, HD), lambda e: (0, e)),
            pl.BlockSpec((tok, HD), lambda e: (0, e)),
            pl.BlockSpec((tok, HD), lambda e: (0, 0)),
            pl.BlockSpec((tok, HD), lambda e: (0, 0)),
        ],
        out_specs=pl.BlockSpec((2, 1, tok, 3 * HD), lambda e: (0, e, 0, 0)),
        name="turn",
    )(q, k, v, cosine, sine)


def relay_kernel(plan, a_own, b_own, a_got, b_got, a_out, b_out):
    item = pl.program_id(0)
    a_out[...] = jnp.where(plan[2, item] > 0, a_own[...], a_got[...])
    b_out[...] = jnp.where(plan[3, item] > 0, b_own[...], b_got[...])


def relay(plan, items, a_got, b_got):
    rows, width = a_got.shape[1:]
    block = (1, rows, width)
    return pl.pallas_call(
        relay_kernel,
        out_shape=[jax.ShapeDtypeStruct((2, rows, width), jnp.bfloat16)] * 2,
        grid_spec=pltpu.PrefetchScalarGridSpec(
            num_scalar_prefetch=1,
            grid=(2,),
            in_specs=[
                pl.BlockSpec(block, lambda i, plan: (plan[0, i], 0, 0)),
                pl.BlockSpec(block, lambda i, plan: (plan[1, i], 1, 0)),
                pl.BlockSpec(block, lambda i, plan: (plan[0, i], 0, 0)),
                pl.BlockSpec(block, lambda i, plan: (plan[1, i], 0, 0)),
            ],
            out_specs=[pl.BlockSpec(block, lambda i, plan: (i, 0, 0))] * 2,
        ),
        name="relay",
    )(plan, items, items, a_got, b_got)


def settle_kernel(plan, own, a_one, b_one, a_two, b_two, out):
    pack = pl.program_id(0)
    half = a_one.shape[1]
    mine = plan[1, pack] == 0
    a = jnp.where(mine, own[0, :half], jnp.where(plan[1, pack] == 1, a_one[0], a_two[0]))
    b = jnp.where(mine, own[0, half:], jnp.where(plan[1, pack] == 2, b_one[0], b_two[0]))
    for e in range(out.shape[1]):
        out[0, e, :half] = a[:, e * HD : e * HD + HD]
        out[0, e, half:] = b[:, e * HD : e * HD + HD]


def settle(plan, items, a_one, b_one, a_two, b_two):
    rows, width = a_one.shape[1:]
    part = width // 2
    block = (1, rows, part)
    return pl.pallas_call(
        settle_kernel,
        out_shape=jax.ShapeDtypeStruct((2, KVH, 2 * rows, HD), jnp.bfloat16),
        grid_spec=pltpu.PrefetchScalarGridSpec(
            num_scalar_prefetch=1,
            grid=(2, 2),
            in_specs=[
                pl.BlockSpec((1, 2 * rows, part), lambda i, j, plan: (plan[0, i], 0, j)),
                pl.BlockSpec(block, lambda i, j, plan: (plan[0, i], 0, j)),
                pl.BlockSpec(block, lambda i, j, plan: (plan[0, i], 0, j)),
                pl.BlockSpec(block, lambda i, j, plan: (i, 0, j)),
                pl.BlockSpec(block, lambda i, j, plan: (i, 0, j)),
            ],
            out_specs=pl.BlockSpec(
                (1, KVH // 2, 2 * rows, HD), lambda i, j, plan: (i, j, 0, 0)
            ),
        ),
        name="settle",
    )(plan, items, a_one, b_one, a_two, b_two)


def longest(ref, rows):
    most = jnp.zeros((1, 1), jnp.float32)
    for at in range(0, rows, 512):
        wide = ref[at : at + 512, :HD].astype(jnp.float32)
        norms = jnp.sum(wide * wide, axis=1, keepdims=True)
        most = jnp.maximum(most, jnp.max(norms, axis=0, keepdims=True))
    return jnp.broadcast_to(jnp.sqrt(most), (8, HD))


def stacked(q_ref):
    return jnp.concatenate([q_ref[:, :HD], q_ref[:, HD : 2 * HD]], axis=0)


def ceiling(rows, top):
    wide = rows.astype(jnp.float32)
    return jnp.sqrt(jnp.sum(wide * wide, axis=1, keepdims=True)) * top * 1.02 - SHIFT


def score(qa, ref, start, size):
    return lax.dot_general(
        qa[...], ref[pl.ds(start, size), :], NT, preferred_element_type=jnp.float32
    )


def fill(core, mine_ref, other_ref, k_side, ka, va):
    mine = mine_ref[...]
    other = other_ref[...]
    first = core == 0
    ka[:, :HD] = jnp.where(first, mine, other)
    va[:, :HD] = jnp.where(first, other, mine)
    ka[:, HD:] = k_side
    va[:, HD:] = jnp.ones_like(k_side)


def pack_kernel(
    core, seen, q_ref, mine_ref, other_ref, qb_ref, kb_ref, o_ref, qa, ka, va, top, acc
):
    qi = pl.program_id(0)
    rows = 2 * BQ
    lane = lax.broadcasted_iota(jnp.int32, (1, HD), 1)

    @pl.when(qi == 0)
    def _():
        fill(core[0], mine_ref, other_ref, kb_ref[...], ka, va)
        top[...] = longest(ka, ka.shape[0])

    q_rows = stacked(q_ref)
    qa[:, :HD] = q_rows
    side = jnp.concatenate([qb_ref[...], qb_ref[...]], axis=0).astype(jnp.float32)
    row = lax.broadcasted_iota(jnp.int32, (rows, BQ), 0)
    ahead = lax.broadcasted_iota(jnp.int32, (rows, BQ), 1) > jnp.where(row >= BQ, row - BQ, row)
    here = pl.multiple_of(qi * BQ, BQ)

    def run(shift):
        qa[:, HD:] = jnp.where(lane == SEGS, shift, side).astype(jnp.bfloat16)
        weights = jnp.where(ahead, 0.0, jnp.exp2(score(qa, ka, here, BQ) * SCALE))
        acc[...] = jnp.dot(
            weights.astype(jnp.bfloat16), va[pl.ds(here, BQ), :], preferred_element_type=jnp.float32
        )

        def body(kj, carry):
            @pl.when(seen[qi, kj] > 0)
            def _():
                at = pl.multiple_of(kj * CK, CK)
                part = jnp.exp2(score(qa, ka, at, CK) * SCALE).astype(jnp.bfloat16)
                acc[...] += jnp.dot(
                    part, va[pl.ds(at, CK), :], preferred_element_type=jnp.float32
                )

            return carry

        lax.fori_loop(0, qi * (BQ // CK), body, 0)
        kept = qa[:, HD:].astype(jnp.float32)
        shift_kept = jnp.sum(jnp.where(lane == SEGS, kept, 0.0), axis=1, keepdims=True)
        o_ref[:, :HD] = acc[:, :HD]
        o_ref[:, HD:] = jnp.where(lane == 1, shift_kept, acc[:, HD:])

    run(ceiling(q_rows, top[0:1, 0:1]))

    @pl.when(jnp.min(acc[:, HD:]) < TINY)
    def _():
        qa[:, HD:] = side.astype(jnp.bfloat16)
        most = jnp.max(
            jnp.where(ahead, BARRED, score(qa, ka, here, BQ)), axis=1, keepdims=True
        )

        def body(kj, most):
            part = score(qa, ka, pl.multiple_of(kj * BQ, BQ), BQ)
            return jnp.maximum(most, jnp.max(part, axis=1, keepdims=True))

        run(lax.fori_loop(0, qi, body, most))


def pack_part(core, seen, arrived, other, q_side, k_side):
    pack = arrived.shape[0]
    once = dict(pipeline_mode=pl.Buffered(1))
    return pl.pallas_call(
        pack_kernel,
        out_shape=jax.ShapeDtypeStruct((2 * pack, 2 * HD), jnp.float32),
        grid_spec=pltpu.PrefetchScalarGridSpec(
            num_scalar_prefetch=2,
            grid=(pack // BQ,),
            in_specs=[
                pl.BlockSpec((BQ, 2 * HD), lambda i, *_: (i, 0)),
                pl.BlockSpec((pack, HD), lambda i, *_: (0, 2), **once),
                pl.BlockSpec((pack, HD), lambda i, *_: (0, 0), **once),
                pl.BlockSpec((BQ, HD), lambda i, *_: (i, 0)),
                pl.BlockSpec((pack, HD), lambda i, *_: (0, 0), **once),
            ],
            out_specs=pl.BlockSpec((2 * BQ, 2 * HD), lambda i, *_: (i, 0)),
            scratch_shapes=[
                pltpu.VMEM((2 * BQ, 2 * HD), jnp.bfloat16),
                pltpu.VMEM((pack, 2 * HD), jnp.bfloat16),
                pltpu.VMEM((pack, 2 * HD), jnp.bfloat16),
                pltpu.VMEM((8, HD), jnp.float32),
                pltpu.VMEM((2 * BQ, 2 * HD), jnp.float32),
            ],
        ),
        compiler_params=pltpu.CompilerParams(vmem_limit_bytes=ROOM),
        cost_estimate=pl.CostEstimate(
            flops=8 * pack * pack * HD, bytes_accessed=8 << 20, transcendentals=pack * pack
        ),
        name="pack_part",
    )(core, seen, arrived, arrived, other, q_side, k_side)


def stem_kernel(core, q_ref, mine_ref, other_ref, part_ref, o_ref, qa, ka, va, top, acc):
    stem = ka.shape[0]
    lane = lax.broadcasted_iota(jnp.int32, (1, HD), 1)

    @pl.when(pl.program_id(0) == 0)
    def _():
        side = jnp.broadcast_to(jnp.where(lane == SEGS, -1.0, 0.0).astype(jnp.bfloat16), (stem, HD))
        fill(core[0], mine_ref, other_ref, side, ka, va)
        top[...] = longest(ka, stem)

    q_rows = stacked(q_ref)
    qa[:, :HD] = q_rows

    def run(shift):
        qa[:, HD:] = jnp.where(lane == SEGS, shift, 0.0).astype(jnp.bfloat16)
        total = None
        held = score(qa, ka, 0, CK)
        for at in range(0, stem, CK):
            ahead = score(qa, ka, at + CK, CK) if at + CK < stem else None
            weights = jnp.exp2(held * SCALE).astype(jnp.bfloat16)
            part = jnp.dot(weights, va[at : at + CK, :], preferred_element_type=jnp.float32)
            total = part if total is None else total + part
            held = ahead
        acc[...] = total

    def finish():
        kept = qa[:, HD:].astype(jnp.float32)
        shift = jnp.sum(jnp.where(lane == SEGS, kept, 0.0), axis=1, keepdims=True)
        before = part_ref[:, HD + 1 : HD + 2]
        most = jnp.maximum(shift, before)
        new = jnp.exp2((shift - most) * SCALE)
        old = jnp.exp2((before - most) * SCALE)
        total = acc[:, HD : HD + 1] * new + part_ref[:, HD : HD + 1] * old
        mixed = ((acc[:, :HD] * new + part_ref[:, :HD] * old) / total).astype(jnp.bfloat16)
        o_ref[:, :HD] = mixed[:BQ]
        o_ref[:, HD:] = mixed[BQ:]

    run(ceiling(q_rows, top[0:1, 0:1]))
    finish()

    @pl.when(jnp.min(acc[:, HD:]) < TINY)
    def _():
        qa[:, HD:] = jnp.zeros_like(q_rows)

        def body(step, most):
            part = score(qa, ka, pl.multiple_of(step * BQ, BQ), BQ)
            return jnp.maximum(most, jnp.max(part, axis=1, keepdims=True))

        low = jnp.full((2 * BQ, 1), BARRED, jnp.float32)
        run(lax.fori_loop(0, stem // BQ, body, low))
        finish()


def stem_part(core, arrived, mine, other, before):
    pack = arrived.shape[0]
    stem = mine.shape[0]
    once = dict(pipeline_mode=pl.Buffered(1))
    return pl.pallas_call(
        stem_kernel,
        out_shape=jax.ShapeDtypeStruct((pack, 2 * HD), jnp.bfloat16),
        grid_spec=pltpu.PrefetchScalarGridSpec(
            num_scalar_prefetch=1,
            grid=(pack // BQ,),
            in_specs=[
                pl.BlockSpec((BQ, 2 * HD), lambda i, *_: (i, 0)),
                pl.BlockSpec((stem, HD), lambda i, *_: (0, 0), **once),
                pl.BlockSpec((stem, HD), lambda i, *_: (0, 0), **once),
                pl.BlockSpec((2 * BQ, 2 * HD), lambda i, *_: (i, 0)),
            ],
            out_specs=pl.BlockSpec((BQ, 2 * HD), lambda i, *_: (i, 0)),
            scratch_shapes=[
                pltpu.VMEM((2 * BQ, 2 * HD), jnp.bfloat16),
                pltpu.VMEM((stem, 2 * HD), jnp.bfloat16),
                pltpu.VMEM((stem, 2 * HD), jnp.bfloat16),
                pltpu.VMEM((8, HD), jnp.float32),
                pltpu.VMEM((2 * BQ, 2 * HD), jnp.float32),
            ],
        ),
        compiler_params=pltpu.CompilerParams(vmem_limit_bytes=ROOM),
        cost_estimate=pl.CostEstimate(
            flops=8 * pack * stem * HD, bytes_accessed=8 << 20, transcendentals=2 * pack * stem
        ),
        name="stem_part",
    )(core, arrived, mine, other, before)


def gather_kernel(core, mine_ref, other_ref, o_ref):
    first = core[0] == 0
    for e in range(mine_ref.shape[1]):
        mine = mine_ref[0, e]
        other = other_ref[e]
        at = 4 * HD * e
        o_ref[:, at : at + 2 * HD] = jnp.where(first, mine, other)
        o_ref[:, at + 2 * HD : at + 4 * HD] = jnp.where(first, other, mine)


def gather(core, mine, other):
    tok = mine.shape[2]
    heads = KVH // 2
    return pl.pallas_call(
        gather_kernel,
        out_shape=jax.ShapeDtypeStruct((tok, H * HD), jnp.bfloat16),
        grid_spec=pltpu.PrefetchScalarGridSpec(
            num_scalar_prefetch=1,
            grid=(2,),
            in_specs=[
                pl.BlockSpec((1, heads, tok, 2 * HD), lambda i, core: (core[0], i, 0, 0)),
                pl.BlockSpec((heads, tok, 2 * HD), lambda i, core: (i, 0, 0)),
            ],
            out_specs=pl.BlockSpec((tok, H * HD // 2), lambda i, core: (0, i)),
        ),
        name="gather",
    )(core, mine, other)


def shards(queries, keys, values, stem_kv, seg_ids, seg_parent, stem_owner):
    tok = queries.shape[1]
    x = lax.axis_index("x")
    core = lax.axis_index("core")
    spot = lax.axis_index(SEQ)
    pack_len = tok * 16
    core_row = core[None].astype(jnp.int32)

    items = lax.all_to_all(stem_kv[0], "core", split_axis=0, concat_axis=0, tiled=True)
    half = items.shape[1] // 2
    near, far = x ^ 1, 3 - x
    a_one = lax.ppermute(items[:, :half], "x", NEAR)
    b_one = lax.ppermute(items[:, half:], "x", FAR)
    follow = stem_owner.reshape(4, 2)
    for_far, for_near, for_us = follow[far], follow[near], follow[x]
    plan = jnp.stack(
        [for_far % 2, for_near % 2, (for_far // 2 == x) * 1, (for_near // 2 == x) * 1]
    ).astype(jnp.int32)
    a_send, b_send = relay(plan, items, a_one, b_one)
    a_two = lax.ppermute(a_send, "x", FAR)
    b_two = lax.ppermute(b_send, "x", NEAR)
    chip = for_us // 2
    source = jnp.where(chip == x, 0, jnp.where(chip == near, 1, jnp.where(chip == far, 2, 3)))
    stems = settle(
        jnp.stack([for_us % 2, source]).astype(jnp.int32), items, a_one, b_one, a_two, b_two
    ).reshape(16, 2 * half, HD)

    linked = ancestry(seg_parent[0])
    places = token_places(seg_ids[0], linked)
    own_places = lax.dynamic_slice_in_dim(places, spot * tok, tok)
    angles = own_places[:, None] * rotary_table()[None, :]
    cosine, sine = jnp.cos(angles), jnp.sin(angles)
    sent = turn(
        queries[0],
        keys[0],
        values[0],
        jnp.concatenate([cosine, cosine], axis=1),
        jnp.concatenate([-sine, sine], axis=1),
    )
    crossed = lax.all_to_all(sent, "core", split_axis=0, concat_axis=0, tiled=True)
    arrived = lax.all_to_all(
        crossed.reshape(16, tok, 3 * HD), SEQ, split_axis=0, concat_axis=0, tiled=True
    ).reshape(pack_len, 3 * HD)
    pair = lax.ppermute(arrived[:, 2 * HD :], "core", FLIP)

    rows = jnp.concatenate([seg_ids[0], seg_parent[0]])
    rows = jnp.where(spot // KVH == core, rows, lax.ppermute(rows, "core", FLIP))
    seg_row, reach = rows[:pack_len], ancestry(rows[pack_len:])
    onehot = (seg_row[:, None] == jnp.arange(HD, dtype=jnp.int32)[None, :]).astype(jnp.float32)
    barred = jnp.pad(BARRED * (1.0 - reach), ((0, HD - SEGS), (0, HD - SEGS)))
    q_side = jnp.dot(onehot, barred, precision=lax.Precision.HIGHEST).astype(jnp.bfloat16)
    k_side = jnp.where(jnp.arange(HD)[None, :] == SEGS, -1.0, onehot).astype(jnp.bfloat16)
    q_has = onehot.reshape(pack_len // BQ, BQ, HD).max(axis=1)[:, :SEGS]
    k_has = onehot.reshape(pack_len // CK, CK, HD).max(axis=1)[:, :SEGS]
    seen = (q_has @ reach @ k_has.T > 0.5).astype(jnp.int32)

    before = pack_part(core_row, seen, arrived, pair, q_side, k_side)
    mine = lax.all_to_all(stems, SEQ, split_axis=0, concat_axis=0, tiled=True).reshape(STEM, HD)
    other = lax.ppermute(mine, "core", FLIP)
    mixed = stem_part(core_row, arrived, mine, other, before)

    back = lax.all_to_all(
        mixed.reshape(16, tok, 2 * HD), SEQ, split_axis=0, concat_axis=0, tiled=True
    ).reshape(2, KVH, tok, 2 * HD)
    away = lax.dynamic_index_in_dim(back, 1 - core, 0, keepdims=False)
    return gather(core_row, back, lax.ppermute(away, "core", FLIP))[None]


def solution(mesh):
    grid = Mesh(mesh.devices.reshape(4, 2, 4, 4), ("x", "core", "z", "y"))
    dp, seq = ("x", "core"), SEQ
    placed = (
        P(dp, seq, None),
        P(dp, seq, None),
        P(dp, seq, None),
        P(dp, None, seq, None),
        P(dp, None),
        P(dp, None),
        P(),
    )
    return jax.shard_map(
        shards, mesh=grid, in_specs=placed, out_specs=P(dp, seq, None), check_vma=False
    )
```

```python
import functools
import math

import jax
import jax.numpy as jnp
import numpy as np
from jax import lax
from jax.experimental import pallas as pl
from jax.experimental.pallas import tpu as pltpu
from jax.sharding import Mesh
from jax.sharding import PartitionSpec as P

H = 32
KVH = 8
HD = 128
STEM = 4096
SEGS = 16
BARRED = -1e30
BQ = 512
CK = 256
SCALE = HD**-0.5 * math.log2(math.e)
SHIFT = 70.0 / SCALE
TINY = 2.0**-16
FLIP = [(0, 1), (1, 0)]
NEAR = [(0, 1), (1, 0), (2, 3), (3, 2)]
FAR = [(0, 3), (3, 0), (1, 2), (2, 1)]
SEQ = ("z", "y")
NT = (((1,), (1,)), ((), ()))
ROOM = 56 * 1024 * 1024


def rotary_table():
    halves = np.arange(0, HD, 2) / HD
    inverse = 1.0 / 500000.0**halves
    wavelen = 2.0 * np.pi / inverse
    smooth = (8192.0 / wavelen - 1.0) / 3.0
    blended = (1.0 - smooth) * inverse / 8.0 + smooth * inverse
    scaled = np.where(wavelen < 2048.0, inverse, np.where(wavelen > 8192.0, inverse / 8.0, blended))
    return jnp.asarray(scaled, dtype=jnp.float32)


def ancestry(parents):
    seg_count = parents.shape[0]
    indices = jnp.arange(seg_count, dtype=jnp.int32)
    linked = (
        (indices[:, None] == indices[None, :]) | (parents[:, None] == indices[None, :])
    ).astype(jnp.float32)
    for sweep in range(max(1, (seg_count - 1).bit_length())):
        linked = (
            jnp.dot(
                linked, linked, precision=lax.Precision.HIGHEST, preferred_element_type=jnp.float32
            )
            > 0.5
        ).astype(jnp.float32)
    return linked


def token_places(seg_row, linked):
    seg_count = linked.shape[0]
    onehot = (seg_row[:, None] == jnp.arange(seg_count, dtype=jnp.int32)[None, :]).astype(
        jnp.float32
    )
    lengths = jnp.sum(onehot, axis=0)
    starts = jnp.cumsum(lengths) - lengths
    before = jnp.sum(linked * lengths[None, :], axis=1) - lengths
    token_ids = jnp.arange(seg_row.shape[0], dtype=jnp.int32).astype(jnp.float32)
    return (
        STEM
        + token_ids
        - jnp.sum(onehot * starts[None, :], axis=1)
        + jnp.sum(onehot * before[None, :], axis=1)
    )


def turn_kernel(q_ref, k_ref, v_ref, cos_ref, sin_ref, o_ref):
    cosine = cos_ref[...]
    sine = sin_ref[...]

    def turned(part):
        wide = part.astype(jnp.float32)
        return (wide * cosine + pltpu.roll(wide, HD // 2, 1) * sine).astype(jnp.bfloat16)

    for head in range(4):
        at = head % 2 * HD
        o_ref[head // 2, 0, :, at : at + HD] = turned(q_ref[:, head * HD : head * HD + HD])
    o_ref[0, 0, :, 2 * HD :] = turned(k_ref[...])
    o_ref[1, 0, :, 2 * HD :] = v_ref[...]


def turn(q, k, v, cosine, sine):
    tok = q.shape[0]
    return pl.pallas_call(
        turn_kernel,
        out_shape=jax.ShapeDtypeStruct((2, KVH, tok, 3 * HD), jnp.bfloat16),
        grid=(KVH,),
        in_specs=[
            pl.BlockSpec((tok, 4 * HD), lambda e: (0, e)),
            pl.BlockSpec((tok, HD), lambda e: (0, e)),
            pl.BlockSpec((tok, HD), lambda e: (0, e)),
            pl.BlockSpec((tok, HD), lambda e: (0, 0)),
            pl.BlockSpec((tok, HD), lambda e: (0, 0)),
        ],
        out_specs=pl.BlockSpec((2, 1, tok, 3 * HD), lambda e: (0, e, 0, 0)),
        name="turn",
    )(q, k, v, cosine, sine)


def relay_kernel(plan, own, a_got, b_got, a_out, b_out, sems):
    half = a_got.shape[1]
    for item in range(2):
        a, b = plan[0, item], plan[1, item]
        own_a, own_b = plan[2, item] > 0, plan[3, item] > 0
        a_to, b_to = a_out.at[item], b_out.at[item]
        a_sem, b_sem = sems.at[2 * item], sems.at[2 * item + 1]

        @pl.when(own_a)
        def _():
            pltpu.make_async_copy(own.at[a, pl.ds(0, half)], a_to, a_sem).start()

        @pl.when(jnp.logical_not(own_a))
        def _():
            pltpu.make_async_copy(a_got.at[a], a_to, a_sem).start()

        @pl.when(own_b)
        def _():
            pltpu.make_async_copy(own.at[b, pl.ds(half, half)], b_to, b_sem).start()

        @pl.when(jnp.logical_not(own_b))
        def _():
            pltpu.make_async_copy(b_got.at[b], b_to, b_sem).start()

    for item in range(2):
        pltpu.make_async_copy(a_got.at[0], a_out.at[item], sems.at[2 * item]).wait()
        pltpu.make_async_copy(b_got.at[0], b_out.at[item], sems.at[2 * item + 1]).wait()


def relay(plan, items, a_got, b_got):
    whole = pl.BlockSpec(memory_space=pl.ANY)
    return pl.pallas_call(
        relay_kernel,
        out_shape=[jax.ShapeDtypeStruct(a_got.shape, jnp.bfloat16)] * 2,
        grid_spec=pltpu.PrefetchScalarGridSpec(
            num_scalar_prefetch=1,
            grid=(1,),
            in_specs=[whole] * 3,
            out_specs=[whole] * 2,
            scratch_shapes=[pltpu.SemaphoreType.DMA((4,))],
        ),
        cost_estimate=pl.CostEstimate(flops=0, bytes_accessed=2 << 20, transcendentals=0),
        name="relay",
    )(plan, items, a_got, b_got)


def settle_kernel(plan, own, a_one, b_one, a_two, b_two, a_out, b_out, sems):
    half = a_one.shape[1]

    def spread(when, source, target, pack, side):
        @pl.when(when)
        def _():
            for e in range(KVH):
                pltpu.make_async_copy(
                    source.at[:, pl.ds(e * HD, HD)], target.at[pack, e], sems.at[pack, side, e]
                ).start()

    for pack in range(2):
        item, chip = plan[0, pack], plan[1, pack]
        spread(chip == 0, own.at[item, pl.ds(0, half)], a_out, pack, 0)
        spread(chip == 1, a_one.at[item], a_out, pack, 0)
        spread(chip >= 2, a_two.at[pack], a_out, pack, 0)
        spread(chip == 0, own.at[item, pl.ds(half, half)], b_out, pack, 1)
        spread(chip == 2, b_one.at[item], b_out, pack, 1)
        spread((chip == 1) | (chip == 3), b_two.at[pack], b_out, pack, 1)
    for pack in range(2):
        for side, target in enumerate((a_out, b_out)):
            for e in range(KVH):
                pltpu.make_async_copy(
                    a_two.at[0, :, pl.ds(0, HD)], target.at[pack, e], sems.at[pack, side, e]
                ).wait()


def settle(plan, items, a_one, b_one, a_two, b_two):
    whole = pl.BlockSpec(memory_space=pl.ANY)
    shape = (2, KVH, a_one.shape[1], HD)
    return pl.pallas_call(
        settle_kernel,
        out_shape=[jax.ShapeDtypeStruct(shape, jnp.bfloat16)] * 2,
        grid_spec=pltpu.PrefetchScalarGridSpec(
            num_scalar_prefetch=1,
            grid=(1,),
            in_specs=[whole] * 5,
            out_specs=[whole] * 2,
            scratch_shapes=[pltpu.SemaphoreType.DMA((2, 2, KVH))],
        ),
        cost_estimate=pl.CostEstimate(flops=0, bytes_accessed=2 << 20, transcendentals=0),
        name="settle",
    )(plan, items, a_one, b_one, a_two, b_two)


def longest(ref, rows):
    most = jnp.zeros((1, 1), jnp.float32)
    for at in range(0, rows, 512):
        wide = ref[at : at + 512, :HD].astype(jnp.float32)
        norms = jnp.sum(wide * wide, axis=1, keepdims=True)
        most = jnp.maximum(most, jnp.max(norms, axis=0, keepdims=True))
    return jnp.broadcast_to(jnp.sqrt(most), (8, HD))


def stacked(q_ref):
    return jnp.concatenate([q_ref[:, :HD], q_ref[:, HD : 2 * HD]], axis=0)


def ceiling(rows, top):
    wide = rows.astype(jnp.float32)
    return jnp.sqrt(jnp.sum(wide * wide, axis=1, keepdims=True)) * top * 1.02 - SHIFT


def score(qa, ref, start, size):
    return lax.dot_general(
        qa[...], ref[pl.ds(start, size), :], NT, preferred_element_type=jnp.float32
    )


def fill(core, mine_ref, other_ref, k_side, ka, va):
    mine = mine_ref[...]
    other = other_ref[...]
    first = core == 0
    ka[:, :HD] = jnp.where(first, mine, other)
    va[:, :HD] = jnp.where(first, other, mine)
    ka[:, HD:] = k_side
    va[:, HD:] = jnp.ones_like(k_side)


def put(o_ref, total, side):
    rows = o_ref.shape[1]
    for head in range(o_ref.shape[0]):
        o_ref[head, :, :HD] = total[head * rows : head * rows + rows]
        o_ref[head, :, HD:] = side[head * rows : head * rows + rows]


def pack_kernel(
    core, seen, q_ref, mine_ref, other_ref, qb_ref, kb_ref, o_ref, qa, ka, va, top, acc
):
    qi = pl.program_id(0)
    rows = 2 * BQ
    lane = lax.broadcasted_iota(jnp.int32, (1, HD), 1)

    @pl.when(qi == 0)
    def _():
        fill(core[0], mine_ref, other_ref, kb_ref[...], ka, va)
        top[...] = longest(ka, ka.shape[0])

    q_rows = stacked(q_ref)
    qa[:, :HD] = q_rows
    side = jnp.concatenate([qb_ref[...], qb_ref[...]], axis=0).astype(jnp.float32)
    row = lax.broadcasted_iota(jnp.int32, (rows, BQ), 0)
    ahead = lax.broadcasted_iota(jnp.int32, (rows, BQ), 1) > jnp.where(row >= BQ, row - BQ, row)
    here = pl.multiple_of(qi * BQ, BQ)

    def run(shift):
        qa[:, HD:] = jnp.where(lane == SEGS, shift, side).astype(jnp.bfloat16)
        weights = jnp.where(ahead, 0.0, jnp.exp2(score(qa, ka, here, BQ) * SCALE))
        acc[...] = jnp.dot(
            weights.astype(jnp.bfloat16), va[pl.ds(here, BQ), :], preferred_element_type=jnp.float32
        )

        def body(kj, carry):
            @pl.when(seen[qi, kj] > 0)
            def _():
                at = pl.multiple_of(kj * BQ, BQ)
                part = jnp.exp2(score(qa, ka, at, BQ) * SCALE).astype(jnp.bfloat16)
                acc[...] += jnp.dot(
                    part, va[pl.ds(at, BQ), :], preferred_element_type=jnp.float32
                )

            return carry

        lax.fori_loop(0, qi, body, 0)
        kept = qa[:, HD:].astype(jnp.float32)
        shift_kept = jnp.sum(jnp.where(lane == SEGS, kept, 0.0), axis=1, keepdims=True)
        put(o_ref, acc[:, :HD], jnp.where(lane == 1, shift_kept, acc[:, HD:]))

    run(ceiling(q_rows, top[0:1, 0:1]))

    @pl.when(jnp.min(acc[:, HD:]) < TINY)
    def _():
        qa[:, HD:] = side.astype(jnp.bfloat16)
        most = jnp.max(
            jnp.where(ahead, BARRED, score(qa, ka, here, BQ)), axis=1, keepdims=True
        )

        def body(kj, most):
            part = score(qa, ka, pl.multiple_of(kj * BQ, BQ), BQ)
            return jnp.maximum(most, jnp.max(part, axis=1, keepdims=True))

        run(lax.fori_loop(0, qi, body, most))


def pack_part(core, seen, arrived, other, q_side, k_side):
    pack = arrived.shape[0]
    once = dict(pipeline_mode=pl.Buffered(1))
    return pl.pallas_call(
        pack_kernel,
        out_shape=jax.ShapeDtypeStruct((2, pack, 2 * HD), jnp.float32),
        grid_spec=pltpu.PrefetchScalarGridSpec(
            num_scalar_prefetch=2,
            grid=(pack // BQ,),
            in_specs=[
                pl.BlockSpec((BQ, 2 * HD), lambda i, *_: (i, 0)),
                pl.BlockSpec((pack, HD), lambda i, *_: (0, 2), **once),
                pl.BlockSpec((pack, HD), lambda i, *_: (0, 0), **once),
                pl.BlockSpec((BQ, HD), lambda i, *_: (i, 0)),
                pl.BlockSpec((pack, HD), lambda i, *_: (0, 0), **once),
            ],
            out_specs=pl.BlockSpec((2, BQ, 2 * HD), lambda i, *_: (0, i, 0)),
            scratch_shapes=[
                pltpu.VMEM((2 * BQ, 2 * HD), jnp.bfloat16),
                pltpu.VMEM((pack, 2 * HD), jnp.bfloat16),
                pltpu.VMEM((pack, 2 * HD), jnp.bfloat16),
                pltpu.VMEM((8, HD), jnp.float32),
                pltpu.VMEM((2 * BQ, 2 * HD), jnp.float32),
            ],
        ),
        compiler_params=pltpu.CompilerParams(vmem_limit_bytes=ROOM),
        cost_estimate=pl.CostEstimate(
            flops=8 * pack * pack * HD, bytes_accessed=8 << 20, transcendentals=pack * pack
        ),
        name="pack_part",
    )(core, seen, arrived, arrived, other, q_side, k_side)


def stem_kernel(last, core, q_ref, mine_ref, other_ref, part_ref, o_ref, qa, top, acc):
    stem = mine_ref.shape[0]
    heads, rows = part_ref.shape[:2]
    lane = lax.broadcasted_iota(jnp.int32, (1, HD), 1)
    first = core[0] == 0
    side = jnp.broadcast_to(jnp.where(lane == SEGS, -1.0, 0.0).astype(jnp.bfloat16), (CK, HD))
    ones = jnp.ones((CK, HD), jnp.bfloat16)

    def keys(at):
        here = pl.ds(at, CK)
        return jnp.where(first, mine_ref[here, :], other_ref[here, :])

    @pl.when(pl.program_id(0) == 0)
    def _():
        def body(step, most):
            wide = keys(pl.multiple_of(step * CK, CK)).astype(jnp.float32)
            norms = jnp.sum(wide * wide, axis=1, keepdims=True)
            return jnp.maximum(most, jnp.max(norms, axis=0, keepdims=True))

        most = lax.fori_loop(0, stem // CK, body, jnp.zeros((1, 1), jnp.float32))
        top[...] = jnp.broadcast_to(jnp.sqrt(most), (8, HD))

    q_rows = jnp.concatenate([q_ref[:, h * HD : h * HD + HD] for h in range(heads)], axis=0)
    qa[:, :HD] = q_rows

    def scores(at):
        wide = jnp.concatenate([keys(at), side], axis=1)
        return lax.dot_general(qa[...], wide, NT, preferred_element_type=jnp.float32)

    def run(shift):
        qa[:, HD:] = jnp.where(lane == SEGS, shift, 0.0).astype(jnp.bfloat16)
        total = None
        held = scores(0)
        for at in range(0, stem, CK):
            ahead = scores(at + CK) if at + CK < stem else None
            weights = jnp.exp2(held * SCALE).astype(jnp.bfloat16)
            here = pl.ds(at, CK)
            wide = jnp.where(first, other_ref[here, :], mine_ref[here, :])
            wide = jnp.concatenate([wide, ones], axis=1)
            part = jnp.dot(weights, wide, preferred_element_type=jnp.float32)
            total = part if total is None else total + part
            held = ahead
        acc[...] = total

    def finish():
        kept = qa[:, HD:].astype(jnp.float32)
        shift = jnp.sum(jnp.where(lane == SEGS, kept, 0.0), axis=1, keepdims=True)
        part = jnp.concatenate([part_ref[h] for h in range(heads)], axis=0)
        before = part[:, HD + 1 : HD + 2]
        most = jnp.maximum(shift, before)
        new = jnp.exp2((shift - most) * SCALE)
        old = jnp.exp2((before - most) * SCALE)
        total = acc[:, HD : HD + 1] * new + part[:, HD : HD + 1] * old
        mixed = acc[:, :HD] * new + part[:, :HD] * old
        if last:
            mixed = (mixed / total).astype(jnp.bfloat16)
            for h in range(heads):
                o_ref[:, h * HD : h * HD + HD] = mixed[h * rows : h * rows + rows]
        else:
            put(o_ref, mixed, jnp.where(lane == 1, most, total))

    run(ceiling(q_rows, top[0:1, 0:1]))
    finish()

    @pl.when(jnp.min(acc[:, HD:]) < TINY)
    def _():
        qa[:, HD:] = jnp.zeros_like(q_rows)

        def body(step, most):
            part = scores(pl.multiple_of(step * CK, CK))
            return jnp.maximum(most, jnp.max(part, axis=1, keepdims=True))

        low = jnp.full((heads * rows, 1), BARRED, jnp.float32)
        run(lax.fori_loop(0, stem // CK, body, low))
        finish()


def stem_part(core, arrived, mine, other, before, head=None):
    pack = arrived.shape[0]
    stem = mine.shape[0]
    heads = 2 if head is None else 1
    rows = 2 * BQ // heads
    at = head or 0
    once = dict(pipeline_mode=pl.Buffered(1))
    part = pl.BlockSpec((heads, rows, 2 * HD), lambda i, *_: (at, i, 0))
    if head is None:
        shape, spec = jax.ShapeDtypeStruct((2, pack, 2 * HD), jnp.float32), part
    else:
        shape = jax.ShapeDtypeStruct((pack, HD), jnp.bfloat16)
        spec = pl.BlockSpec((rows, HD), lambda i, *_: (i, 0))
    return pl.pallas_call(
        functools.partial(stem_kernel, head is not None),
        out_shape=shape,
        grid_spec=pltpu.PrefetchScalarGridSpec(
            num_scalar_prefetch=1,
            grid=(pack // rows,),
            in_specs=[
                pl.BlockSpec((rows, heads * HD), lambda i, *_: (i, at)),
                pl.BlockSpec((stem, HD), lambda i, *_: (0, 0), **once),
                pl.BlockSpec((stem, HD), lambda i, *_: (0, 0), **once),
                part,
            ],
            out_specs=spec,
            scratch_shapes=[
                pltpu.VMEM((2 * BQ, 2 * HD), jnp.bfloat16),
                pltpu.VMEM((8, HD), jnp.float32),
                pltpu.VMEM((2 * BQ, 2 * HD), jnp.float32),
            ],
        ),
        compiler_params=pltpu.CompilerParams(vmem_limit_bytes=ROOM),
        cost_estimate=pl.CostEstimate(
            flops=4 * heads * pack * stem * HD,
            bytes_accessed=8 << 20,
            transcendentals=heads * pack * stem,
        ),
        name="stem_part",
    )(core, arrived, mine, other, before)


def gather_kernel(core, mine_a, mine_b, other_ref, o_ref):
    first = core[0] == 0
    for e in range(mine_a.shape[1]):
        for head, mine_ref in enumerate((mine_a, mine_b)):
            mine = mine_ref[0, e]
            other = other_ref[head, e]
            at = 4 * HD * e + HD * head
            o_ref[:, at : at + HD] = jnp.where(first, mine, other)
            o_ref[:, at + 2 * HD : at + 3 * HD] = jnp.where(first, other, mine)


def gather(core, mine_a, mine_b, other):
    tok = mine_a.shape[2]
    heads = KVH // 2
    mine = pl.BlockSpec((1, heads, tok, HD), lambda i, core: (core[0], i, 0, 0))
    return pl.pallas_call(
        gather_kernel,
        out_shape=jax.ShapeDtypeStruct((tok, H * HD), jnp.bfloat16),
        grid_spec=pltpu.PrefetchScalarGridSpec(
            num_scalar_prefetch=1,
            grid=(2,),
            in_specs=[
                mine,
                mine,
                pl.BlockSpec((2, heads, tok, HD), lambda i, core: (0, i, 0, 0)),
            ],
            out_specs=pl.BlockSpec((tok, H * HD // 2), lambda i, core: (0, i)),
        ),
        name="gather",
    )(core, mine_a, mine_b, other)


def shards(queries, keys, values, stem_kv, seg_ids, seg_parent, stem_owner):
    tok = queries.shape[1]
    x = lax.axis_index("x")
    core = lax.axis_index("core")
    spot = lax.axis_index(SEQ)
    pack_len = tok * 16
    core_row = core[None].astype(jnp.int32)

    items = lax.all_to_all(stem_kv[0], "core", split_axis=0, concat_axis=0, tiled=True)
    half = items.shape[1] // 2
    near, far = x ^ 1, 3 - x
    a_one = lax.ppermute(items[:, :half], "x", NEAR)
    b_one = lax.ppermute(items[:, half:], "x", FAR)
    queries, seg_ids, seg_parent, _ = lax.optimization_barrier(
        (queries, seg_ids, seg_parent, items)
    )

    linked = ancestry(seg_parent[0])
    places = token_places(seg_ids[0], linked)
    own_places = lax.dynamic_slice_in_dim(places, spot * tok, tok)
    angles = own_places[:, None] * rotary_table()[None, :]
    cosine, sine = jnp.cos(angles), jnp.sin(angles)
    sent = turn(
        queries[0],
        keys[0],
        values[0],
        jnp.concatenate([cosine, cosine], axis=1),
        jnp.concatenate([-sine, sine], axis=1),
    )

    a_one, b_one, sent = lax.optimization_barrier((a_one, b_one, sent))
    follow = stem_owner.reshape(4, 2)
    for_far, for_near, for_us = follow[far], follow[near], follow[x]
    plan = jnp.stack(
        [for_far % 2, for_near % 2, (for_far // 2 == x) * 1, (for_near // 2 == x) * 1]
    ).astype(jnp.int32)
    a_send, b_send = relay(plan, items, a_one, b_one)
    a_two = lax.ppermute(a_send, "x", FAR)
    b_two = lax.ppermute(b_send, "x", NEAR)

    sent, a_send, seg_ids, seg_parent = lax.optimization_barrier(
        (sent, a_send, seg_ids, seg_parent)
    )
    crossed = lax.all_to_all(sent, "core", split_axis=0, concat_axis=0, tiled=True)
    arrived = lax.all_to_all(
        crossed.reshape(16, tok, 3 * HD), SEQ, split_axis=0, concat_axis=0, tiled=True
    ).reshape(pack_len, 3 * HD)
    pair = lax.ppermute(arrived[:, 2 * HD :], "core", FLIP)

    rows = jnp.concatenate([seg_ids[0], seg_parent[0]])
    rows = jnp.where(spot // KVH == core, rows, lax.ppermute(rows, "core", FLIP))
    seg_row, reach = rows[:pack_len], ancestry(rows[pack_len:])
    onehot = (seg_row[:, None] == jnp.arange(HD, dtype=jnp.int32)[None, :]).astype(jnp.float32)
    barred = jnp.pad(BARRED * (1.0 - reach), ((0, HD - SEGS), (0, HD - SEGS)))
    q_side = jnp.dot(onehot, barred, precision=lax.Precision.HIGHEST).astype(jnp.bfloat16)
    k_side = jnp.where(jnp.arange(HD)[None, :] == SEGS, -1.0, onehot).astype(jnp.bfloat16)
    q_has = onehot.reshape(pack_len // BQ, BQ, HD).max(axis=1)[:, :SEGS]
    seen = (q_has @ reach @ q_has.T > 0.5).astype(jnp.int32)

    chip = for_us // 2
    source = jnp.where(chip == x, 0, jnp.where(chip == near, 1, jnp.where(chip == far, 2, 3)))
    a_stem, b_stem = settle(
        jnp.stack([for_us % 2, source]).astype(jnp.int32), items, a_one, b_one, a_two, b_two
    )

    def to_heads(part):
        part = part.reshape(16, half, HD)
        part = lax.all_to_all(part, SEQ, split_axis=0, concat_axis=0, tiled=True)
        return part.reshape(16 * half, HD)

    a_mine = to_heads(a_stem)
    arrived, pair, _ = lax.optimization_barrier((arrived, pair, a_stem))
    partial = pack_part(core_row, seen, arrived, pair, q_side, k_side)
    a_mine, partial, b_stem = lax.optimization_barrier((a_mine, partial, b_stem))
    b_mine = to_heads(b_stem)
    partial = stem_part(core_row, arrived, a_mine, lax.ppermute(a_mine, "core", FLIP), partial)
    b_other = lax.ppermute(b_mine, "core", FLIP)
    backs = []
    for head in range(2):
        mixed = stem_part(core_row, arrived, b_mine, b_other, partial, head)
        back = lax.all_to_all(
            mixed.reshape(16, tok, HD), SEQ, split_axis=0, concat_axis=0, tiled=True
        )
        backs.append(back.reshape(2, KVH, tok, HD))
    away = jnp.stack(
        [lax.dynamic_index_in_dim(back, 1 - core, 0, keepdims=False) for back in backs]
    )
    return gather(core_row, backs[0], backs[1], lax.ppermute(away, "core", FLIP))[None]


def solution(mesh):
    grid = Mesh(mesh.devices.reshape(4, 2, 4, 4), ("x", "core", "z", "y"))
    dp, seq = ("x", "core"), SEQ
    placed = (
        P(dp, seq, None),
        P(dp, seq, None),
        P(dp, seq, None),
        P(dp, None, seq, None),
        P(dp, None),
        P(dp, None),
        P(),
    )
    return jax.shard_map(
        shards, mesh=grid, in_specs=placed, out_specs=P(dp, seq, None), check_vma=False
    )
```

```python
import math

import jax
import jax.numpy as jnp
import numpy as np
from jax import lax
from jax.experimental import pallas as pl
from jax.experimental.pallas import tpu as pltpu
from jax.sharding import Mesh
from jax.sharding import PartitionSpec as P

H = 32
KVH = 8
HD = 128
STEM = 4096
SEGS = 16
BARRED = -1e30
BQ = 512
CK = 256
SCALE = HD**-0.5 * math.log2(math.e)
SHIFT = 70.0 / SCALE
TINY = 2.0**-16
FLIP = [(0, 1), (1, 0)]
NEAR = [(0, 1), (1, 0), (2, 3), (3, 2)]
FAR = [(0, 3), (3, 0), (1, 2), (2, 1)]
SEQ = ("z", "y")
NT = (((1,), (1,)), ((), ()))
ROOM = 56 * 1024 * 1024


def rotary_table():
    halves = np.arange(0, HD, 2) / HD
    inverse = 1.0 / 500000.0**halves
    wavelen = 2.0 * np.pi / inverse
    smooth = (8192.0 / wavelen - 1.0) / 3.0
    blended = (1.0 - smooth) * inverse / 8.0 + smooth * inverse
    scaled = np.where(wavelen < 2048.0, inverse, np.where(wavelen > 8192.0, inverse / 8.0, blended))
    return jnp.asarray(scaled, dtype=jnp.float32)


def ancestry(parents):
    seg_count = parents.shape[0]
    indices = jnp.arange(seg_count, dtype=jnp.int32)
    linked = (
        (indices[:, None] == indices[None, :]) | (parents[:, None] == indices[None, :])
    ).astype(jnp.float32)
    for sweep in range(max(1, (seg_count - 1).bit_length())):
        linked = (
            jnp.dot(
                linked, linked, precision=lax.Precision.HIGHEST, preferred_element_type=jnp.float32
            )
            > 0.5
        ).astype(jnp.float32)
    return linked


def token_places(seg_row, linked):
    seg_count = linked.shape[0]
    onehot = (seg_row[:, None] == jnp.arange(seg_count, dtype=jnp.int32)[None, :]).astype(
        jnp.float32
    )
    lengths = jnp.sum(onehot, axis=0)
    starts = jnp.cumsum(lengths) - lengths
    before = jnp.sum(linked * lengths[None, :], axis=1) - lengths
    token_ids = jnp.arange(seg_row.shape[0], dtype=jnp.int32).astype(jnp.float32)
    return (
        STEM
        + token_ids
        - jnp.sum(onehot * starts[None, :], axis=1)
        + jnp.sum(onehot * before[None, :], axis=1)
    )


def turn_kernel(q_ref, k_ref, v_ref, cos_ref, sin_ref, o_ref):
    cosine = cos_ref[...]
    sine = sin_ref[...]

    def turned(part):
        wide = part.astype(jnp.float32)
        return (wide * cosine + pltpu.roll(wide, HD // 2, 1) * sine).astype(jnp.bfloat16)

    for head in range(4):
        at = head % 2 * HD
        o_ref[head // 2, 0, :, at : at + HD] = turned(q_ref[:, head * HD : head * HD + HD])
    o_ref[0, 0, :, 2 * HD :] = turned(k_ref[...])
    o_ref[1, 0, :, 2 * HD :] = v_ref[...]


def turn(q, k, v, cosine, sine):
    tok = q.shape[0]
    return pl.pallas_call(
        turn_kernel,
        out_shape=jax.ShapeDtypeStruct((2, KVH, tok, 3 * HD), jnp.bfloat16),
        grid=(KVH,),
        in_specs=[
            pl.BlockSpec((tok, 4 * HD), lambda e: (0, e)),
            pl.BlockSpec((tok, HD), lambda e: (0, e)),
            pl.BlockSpec((tok, HD), lambda e: (0, e)),
            pl.BlockSpec((tok, HD), lambda e: (0, 0)),
            pl.BlockSpec((tok, HD), lambda e: (0, 0)),
        ],
        out_specs=pl.BlockSpec((2, 1, tok, 3 * HD), lambda e: (0, e, 0, 0)),
        name="turn",
    )(q, k, v, cosine, sine)


def relay_kernel(plan, a_own, b_own, a_got, b_got, a_out, b_out):
    item = pl.program_id(0)
    a_out[...] = jnp.where(plan[2, item] > 0, a_own[...], a_got[...])
    b_out[...] = jnp.where(plan[3, item] > 0, b_own[...], b_got[...])


def relay(plan, items, a_got, b_got):
    rows, width = a_got.shape[1:]
    block = (1, rows, width)
    return pl.pallas_call(
        relay_kernel,
        out_shape=[jax.ShapeDtypeStruct((2, rows, width), jnp.bfloat16)] * 2,
        grid_spec=pltpu.PrefetchScalarGridSpec(
            num_scalar_prefetch=1,
            grid=(2,),
            in_specs=[
                pl.BlockSpec(block, lambda i, plan: (plan[0, i], 0, 0)),
                pl.BlockSpec(block, lambda i, plan: (plan[1, i], 1, 0)),
                pl.BlockSpec(block, lambda i, plan: (plan[0, i], 0, 0)),
                pl.BlockSpec(block, lambda i, plan: (plan[1, i], 0, 0)),
            ],
            out_specs=[pl.BlockSpec(block, lambda i, plan: (i, 0, 0))] * 2,
        ),
        name="relay",
    )(plan, items, items, a_got, b_got)


def settle_kernel(plan, own, a_one, b_one, a_two, b_two, out):
    pack = pl.program_id(0)
    half = a_one.shape[1]
    mine = plan[1, pack] == 0
    a = jnp.where(mine, own[0, :half], jnp.where(plan[1, pack] == 1, a_one[0], a_two[0]))
    b = jnp.where(mine, own[0, half:], jnp.where(plan[1, pack] == 2, b_one[0], b_two[0]))
    for e in range(out.shape[1]):
        out[0, e, :half] = a[:, e * HD : e * HD + HD]
        out[0, e, half:] = b[:, e * HD : e * HD + HD]


def settle(plan, items, a_one, b_one, a_two, b_two):
    rows, width = a_one.shape[1:]
    part = width // 2
    block = (1, rows, part)
    return pl.pallas_call(
        settle_kernel,
        out_shape=jax.ShapeDtypeStruct((2, KVH, 2 * rows, HD), jnp.bfloat16),
        grid_spec=pltpu.PrefetchScalarGridSpec(
            num_scalar_prefetch=1,
            grid=(2, 2),
            in_specs=[
                pl.BlockSpec((1, 2 * rows, part), lambda i, j, plan: (plan[0, i], 0, j)),
                pl.BlockSpec(block, lambda i, j, plan: (plan[0, i], 0, j)),
                pl.BlockSpec(block, lambda i, j, plan: (plan[0, i], 0, j)),
                pl.BlockSpec(block, lambda i, j, plan: (i, 0, j)),
                pl.BlockSpec(block, lambda i, j, plan: (i, 0, j)),
            ],
            out_specs=pl.BlockSpec(
                (1, KVH // 2, 2 * rows, HD), lambda i, j, plan: (i, j, 0, 0)
            ),
        ),
        name="settle",
    )(plan, items, a_one, b_one, a_two, b_two)


def longest(ref, rows):
    most = jnp.zeros((1, 1), jnp.float32)
    for at in range(0, rows, 512):
        wide = ref[at : at + 512, :HD].astype(jnp.float32)
        norms = jnp.sum(wide * wide, axis=1, keepdims=True)
        most = jnp.maximum(most, jnp.max(norms, axis=0, keepdims=True))
    return jnp.broadcast_to(jnp.sqrt(most), (8, HD))


def stacked(q_ref):
    return jnp.concatenate([q_ref[:, :HD], q_ref[:, HD : 2 * HD]], axis=0)


def ceiling(rows, top):
    wide = rows.astype(jnp.float32)
    return jnp.sqrt(jnp.sum(wide * wide, axis=1, keepdims=True)) * top * 1.02 - SHIFT


def score(qa, ref, start, size):
    return lax.dot_general(
        qa[...], ref[pl.ds(start, size), :], NT, preferred_element_type=jnp.float32
    )


def fill(core, mine_ref, other_ref, k_side, ka, va):
    mine = mine_ref[...]
    other = other_ref[...]
    first = core == 0
    ka[:, :HD] = jnp.where(first, mine, other)
    va[:, :HD] = jnp.where(first, other, mine)
    ka[:, HD:] = k_side
    va[:, HD:] = jnp.ones_like(k_side)


def put(o_ref, total, side):
    rows = o_ref.shape[1]
    for head in range(o_ref.shape[0]):
        o_ref[head, :, :HD] = total[head * rows : head * rows + rows]
        o_ref[head, :, HD:] = side[head * rows : head * rows + rows]


def pack_kernel(
    core, seen, q_ref, mine_ref, other_ref, qb_ref, kb_ref, o_ref, qa, ka, va, top, acc
):
    qi = pl.program_id(0)
    rows = 2 * BQ
    lane = lax.broadcasted_iota(jnp.int32, (1, HD), 1)

    @pl.when(qi == 0)
    def _():
        fill(core[0], mine_ref, other_ref, kb_ref[...], ka, va)
        top[...] = longest(ka, ka.shape[0])

    q_rows = stacked(q_ref)
    qa[:, :HD] = q_rows
    side = jnp.concatenate([qb_ref[...], qb_ref[...]], axis=0).astype(jnp.float32)
    row = lax.broadcasted_iota(jnp.int32, (rows, BQ), 0)
    ahead = lax.broadcasted_iota(jnp.int32, (rows, BQ), 1) > jnp.where(row >= BQ, row - BQ, row)
    here = pl.multiple_of(qi * BQ, BQ)

    def run(shift):
        qa[:, HD:] = jnp.where(lane == SEGS, shift, side).astype(jnp.bfloat16)
        weights = jnp.where(ahead, 0.0, jnp.exp2(score(qa, ka, here, BQ) * SCALE))
        acc[...] = jnp.dot(
            weights.astype(jnp.bfloat16), va[pl.ds(here, BQ), :], preferred_element_type=jnp.float32
        )

        def body(kj, carry):
            @pl.when(seen[qi, kj] > 0)
            def _():
                at = pl.multiple_of(kj * BQ, BQ)
                part = jnp.exp2(score(qa, ka, at, BQ) * SCALE).astype(jnp.bfloat16)
                acc[...] += jnp.dot(
                    part, va[pl.ds(at, BQ), :], preferred_element_type=jnp.float32
                )

            return carry

        lax.fori_loop(0, qi, body, 0)
        kept = qa[:, HD:].astype(jnp.float32)
        shift_kept = jnp.sum(jnp.where(lane == SEGS, kept, 0.0), axis=1, keepdims=True)
        put(o_ref, acc[:, :HD], jnp.where(lane == 1, shift_kept, acc[:, HD:]))

    run(ceiling(q_rows, top[0:1, 0:1]))

    @pl.when(jnp.min(acc[:, HD:]) < TINY)
    def _():
        qa[:, HD:] = side.astype(jnp.bfloat16)
        most = jnp.max(
            jnp.where(ahead, BARRED, score(qa, ka, here, BQ)), axis=1, keepdims=True
        )

        def body(kj, most):
            part = score(qa, ka, pl.multiple_of(kj * BQ, BQ), BQ)
            return jnp.maximum(most, jnp.max(part, axis=1, keepdims=True))

        run(lax.fori_loop(0, qi, body, most))


def pack_part(core, seen, arrived, other, q_side, k_side):
    pack = arrived.shape[0]
    once = dict(pipeline_mode=pl.Buffered(1))
    return pl.pallas_call(
        pack_kernel,
        out_shape=jax.ShapeDtypeStruct((2, pack, 2 * HD), jnp.float32),
        grid_spec=pltpu.PrefetchScalarGridSpec(
            num_scalar_prefetch=2,
            grid=(pack // BQ,),
            in_specs=[
                pl.BlockSpec((BQ, 2 * HD), lambda i, *_: (i, 0)),
                pl.BlockSpec((pack, HD), lambda i, *_: (0, 2), **once),
                pl.BlockSpec((pack, HD), lambda i, *_: (0, 0), **once),
                pl.BlockSpec((BQ, HD), lambda i, *_: (i, 0)),
                pl.BlockSpec((pack, HD), lambda i, *_: (0, 0), **once),
            ],
            out_specs=pl.BlockSpec((2, BQ, 2 * HD), lambda i, *_: (0, i, 0)),
            scratch_shapes=[
                pltpu.VMEM((2 * BQ, 2 * HD), jnp.bfloat16),
                pltpu.VMEM((pack, 2 * HD), jnp.bfloat16),
                pltpu.VMEM((pack, 2 * HD), jnp.bfloat16),
                pltpu.VMEM((8, HD), jnp.float32),
                pltpu.VMEM((2 * BQ, 2 * HD), jnp.float32),
            ],
        ),
        compiler_params=pltpu.CompilerParams(vmem_limit_bytes=ROOM),
        cost_estimate=pl.CostEstimate(
            flops=8 * pack * pack * HD, bytes_accessed=8 << 20, transcendentals=pack * pack
        ),
        name="pack_part",
    )(core, seen, arrived, arrived, other, q_side, k_side)


def stem_kernel(core, q_ref, mine_ref, other_ref, part_ref, o_ref, qa, top, acc):
    stem = mine_ref.shape[0]
    heads, rows = part_ref.shape[:2]
    lane = lax.broadcasted_iota(jnp.int32, (1, HD), 1)
    first = core[0] == 0
    side = jnp.broadcast_to(jnp.where(lane == SEGS, -1.0, 0.0).astype(jnp.bfloat16), (CK, HD))
    ones = jnp.ones((CK, HD), jnp.bfloat16)

    def keys(at):
        here = pl.ds(at, CK)
        return jnp.where(first, mine_ref[here, :], other_ref[here, :])

    @pl.when(pl.program_id(0) == 0)
    def _():
        def body(step, most):
            wide = keys(pl.multiple_of(step * CK, CK)).astype(jnp.float32)
            norms = jnp.sum(wide * wide, axis=1, keepdims=True)
            return jnp.maximum(most, jnp.max(norms, axis=0, keepdims=True))

        most = lax.fori_loop(0, stem // CK, body, jnp.zeros((1, 1), jnp.float32))
        top[...] = jnp.broadcast_to(jnp.sqrt(most), (8, HD))

    q_rows = jnp.concatenate([q_ref[:, h * HD : h * HD + HD] for h in range(heads)], axis=0)
    qa[:, :HD] = q_rows

    def scores(at):
        wide = jnp.concatenate([keys(at), side], axis=1)
        return lax.dot_general(qa[...], wide, NT, preferred_element_type=jnp.float32)

    def run(shift):
        qa[:, HD:] = jnp.where(lane == SEGS, shift, 0.0).astype(jnp.bfloat16)
        total = None
        held = scores(0)
        for at in range(0, stem, CK):
            ahead = scores(at + CK) if at + CK < stem else None
            weights = jnp.exp2(held * SCALE).astype(jnp.bfloat16)
            here = pl.ds(at, CK)
            wide = jnp.where(first, other_ref[here, :], mine_ref[here, :])
            wide = jnp.concatenate([wide, ones], axis=1)
            part = jnp.dot(weights, wide, preferred_element_type=jnp.float32)
            total = part if total is None else total + part
            held = ahead
        acc[...] = total

    def finish():
        kept = qa[:, HD:].astype(jnp.float32)
        shift = jnp.sum(jnp.where(lane == SEGS, kept, 0.0), axis=1, keepdims=True)
        part = jnp.concatenate([part_ref[h] for h in range(heads)], axis=0)
        before = part[:, HD + 1 : HD + 2]
        most = jnp.maximum(shift, before)
        new = jnp.exp2((shift - most) * SCALE)
        old = jnp.exp2((before - most) * SCALE)
        total = acc[:, HD : HD + 1] * new + part[:, HD : HD + 1] * old
        mixed = (acc[:, :HD] * new + part[:, :HD] * old) / total
        for h in range(heads):
            o_ref[:, h * HD : h * HD + HD] = mixed[h * rows : h * rows + rows].astype(jnp.bfloat16)

    run(ceiling(q_rows, top[0:1, 0:1]))
    finish()

    @pl.when(jnp.min(acc[:, HD:]) < TINY)
    def _():
        qa[:, HD:] = jnp.zeros_like(q_rows)

        def body(step, most):
            part = scores(pl.multiple_of(step * CK, CK))
            return jnp.maximum(most, jnp.max(part, axis=1, keepdims=True))

        low = jnp.full((heads * rows, 1), BARRED, jnp.float32)
        run(lax.fori_loop(0, stem // CK, body, low))
        finish()


def stem_part(core, arrived, mine, other, before):
    pack = arrived.shape[0]
    stem = mine.shape[0]
    once = dict(pipeline_mode=pl.Buffered(1))
    return pl.pallas_call(
        stem_kernel,
        out_shape=jax.ShapeDtypeStruct((pack, 2 * HD), jnp.bfloat16),
        grid_spec=pltpu.PrefetchScalarGridSpec(
            num_scalar_prefetch=1,
            grid=(pack // BQ,),
            in_specs=[
                pl.BlockSpec((BQ, 2 * HD), lambda i, *_: (i, 0)),
                pl.BlockSpec((stem, HD), lambda i, *_: (0, 0), **once),
                pl.BlockSpec((stem, HD), lambda i, *_: (0, 0), **once),
                pl.BlockSpec((2, BQ, 2 * HD), lambda i, *_: (0, i, 0)),
            ],
            out_specs=pl.BlockSpec((BQ, 2 * HD), lambda i, *_: (i, 0)),
            scratch_shapes=[
                pltpu.VMEM((2 * BQ, 2 * HD), jnp.bfloat16),
                pltpu.VMEM((8, HD), jnp.float32),
                pltpu.VMEM((2 * BQ, 2 * HD), jnp.float32),
            ],
        ),
        compiler_params=pltpu.CompilerParams(vmem_limit_bytes=ROOM),
        cost_estimate=pl.CostEstimate(
            flops=8 * pack * stem * HD,
            bytes_accessed=8 << 20,
            transcendentals=2 * pack * stem,
        ),
        name="stem_part",
    )(core, arrived, mine, other, before)


def gather_kernel(core, mine_ref, other_ref, o_ref):
    first = core[0] == 0
    for e in range(mine_ref.shape[1]):
        mine = mine_ref[0, e]
        other = other_ref[e]
        at = 4 * HD * e
        o_ref[:, at : at + 2 * HD] = jnp.where(first, mine, other)
        o_ref[:, at + 2 * HD : at + 4 * HD] = jnp.where(first, other, mine)


def gather(core, mine, other):
    tok = mine.shape[2]
    heads = KVH // 2
    return pl.pallas_call(
        gather_kernel,
        out_shape=jax.ShapeDtypeStruct((tok, H * HD), jnp.bfloat16),
        grid_spec=pltpu.PrefetchScalarGridSpec(
            num_scalar_prefetch=1,
            grid=(2,),
            in_specs=[
                pl.BlockSpec((1, heads, tok, 2 * HD), lambda i, core: (core[0], i, 0, 0)),
                pl.BlockSpec((heads, tok, 2 * HD), lambda i, core: (i, 0, 0)),
            ],
            out_specs=pl.BlockSpec((tok, H * HD // 2), lambda i, core: (0, i)),
        ),
        name="gather",
    )(core, mine, other)


def shards(queries, keys, values, stem_kv, seg_ids, seg_parent, stem_owner):
    tok = queries.shape[1]
    x = lax.axis_index("x")
    core = lax.axis_index("core")
    spot = lax.axis_index(SEQ)
    pack_len = tok * 16
    core_row = core[None].astype(jnp.int32)

    items = lax.all_to_all(stem_kv[0], "core", split_axis=0, concat_axis=0, tiled=True)
    half = items.shape[1] // 2
    near, far = x ^ 1, 3 - x
    a_one = lax.ppermute(items[:, :half], "x", NEAR)
    b_one = lax.ppermute(items[:, half:], "x", FAR)
    queries, seg_ids, seg_parent, _ = lax.optimization_barrier(
        (queries, seg_ids, seg_parent, items)
    )

    linked = ancestry(seg_parent[0])
    places = token_places(seg_ids[0], linked)
    own_places = lax.dynamic_slice_in_dim(places, spot * tok, tok)
    angles = own_places[:, None] * rotary_table()[None, :]
    cosine, sine = jnp.cos(angles), jnp.sin(angles)
    sent = turn(
        queries[0],
        keys[0],
        values[0],
        jnp.concatenate([cosine, cosine], axis=1),
        jnp.concatenate([-sine, sine], axis=1),
    )

    a_one, b_one, sent = lax.optimization_barrier((a_one, b_one, sent))
    crossed = lax.all_to_all(sent, "core", split_axis=0, concat_axis=0, tiled=True)
    a_one, b_one, crossed = lax.optimization_barrier((a_one, b_one, crossed))

    arrived = lax.all_to_all(
        crossed.reshape(16, tok, 3 * HD), SEQ, split_axis=0, concat_axis=0, tiled=True
    ).reshape(pack_len, 3 * HD)
    pair = lax.ppermute(arrived[:, 2 * HD :], "core", FLIP)

    follow = stem_owner.reshape(4, 2)
    for_far, for_near, for_us = follow[far], follow[near], follow[x]
    plan = jnp.stack(
        [for_far % 2, for_near % 2, (for_far // 2 == x) * 1, (for_near // 2 == x) * 1]
    ).astype(jnp.int32)
    a_send, b_send = relay(plan, items, a_one, b_one)
    a_two = lax.ppermute(a_send, "x", FAR)
    b_two = lax.ppermute(b_send, "x", NEAR)
    seg_ids, seg_parent, _ = lax.optimization_barrier((seg_ids, seg_parent, a_send))

    rows = jnp.concatenate([seg_ids[0], seg_parent[0]])
    rows = jnp.where(spot // KVH == core, rows, lax.ppermute(rows, "core", FLIP))
    seg_row, reach = rows[:pack_len], ancestry(rows[pack_len:])
    onehot = (seg_row[:, None] == jnp.arange(HD, dtype=jnp.int32)[None, :]).astype(jnp.float32)
    barred = jnp.pad(BARRED * (1.0 - reach), ((0, HD - SEGS), (0, HD - SEGS)))
    q_side = jnp.dot(onehot, barred, precision=lax.Precision.HIGHEST).astype(jnp.bfloat16)
    k_side = jnp.where(jnp.arange(HD)[None, :] == SEGS, -1.0, onehot).astype(jnp.bfloat16)
    q_has = onehot.reshape(pack_len // BQ, BQ, HD).max(axis=1)[:, :SEGS]
    seen = (q_has @ reach @ q_has.T > 0.5).astype(jnp.int32)

    chip = for_us // 2
    source = jnp.where(chip == x, 0, jnp.where(chip == near, 1, jnp.where(chip == far, 2, 3)))
    stems = settle(
        jnp.stack([for_us % 2, source]).astype(jnp.int32), items, a_one, b_one, a_two, b_two
    ).reshape(16, 2 * half, HD)
    mine = lax.all_to_all(stems, SEQ, split_axis=0, concat_axis=0, tiled=True).reshape(STEM, HD)
    arrived, pair, _ = lax.optimization_barrier((arrived, pair, stems))
    partial = pack_part(core_row, seen, arrived, pair, q_side, k_side)
    mine, partial = lax.optimization_barrier((mine, partial))
    other = lax.ppermute(mine, "core", FLIP)
    mixed = stem_part(core_row, arrived, mine, other, partial)

    back = lax.all_to_all(
        mixed.reshape(16, tok, 2 * HD), SEQ, split_axis=0, concat_axis=0, tiled=True
    ).reshape(2, KVH, tok, 2 * HD)
    away = lax.dynamic_index_in_dim(back, 1 - core, 0, keepdims=False)
    return gather(core_row, back, lax.ppermute(away, "core", FLIP))[None]


def solution(mesh):
    grid = Mesh(mesh.devices.reshape(4, 2, 4, 4), ("x", "core", "z", "y"))
    dp, seq = ("x", "core"), SEQ
    placed = (
        P(dp, seq, None),
        P(dp, seq, None),
        P(dp, seq, None),
        P(dp, None, seq, None),
        P(dp, None),
        P(dp, None),
        P(),
    )
    return jax.shard_map(
        shards, mesh=grid, in_specs=placed, out_specs=P(dp, seq, None), check_vma=False
    )
```

```python
import math

import jax
import jax.numpy as jnp
import numpy as np
from jax import lax
from jax.experimental import pallas as pl
from jax.experimental.pallas import tpu as pltpu
from jax.sharding import Mesh
from jax.sharding import PartitionSpec as P

H = 32
KVH = 8
HD = 128
STEM = 4096
SEGS = 16
BARRED = -1e30
BQ = 512
CK = 256
SCALE = HD**-0.5 * math.log2(math.e)
SHIFT = 70.0 / SCALE
TINY = 2.0**-16
FLIP = [(0, 1), (1, 0)]
NEAR = [(0, 1), (1, 0), (2, 3), (3, 2)]
FAR = [(0, 3), (3, 0), (1, 2), (2, 1)]
SEQ = ("z", "y")
NT = (((1,), (1,)), ((), ()))
ROOM = 56 * 1024 * 1024


def rotary_table():
    halves = np.arange(0, HD, 2) / HD
    inverse = 1.0 / 500000.0**halves
    wavelen = 2.0 * np.pi / inverse
    smooth = (8192.0 / wavelen - 1.0) / 3.0
    blended = (1.0 - smooth) * inverse / 8.0 + smooth * inverse
    scaled = np.where(wavelen < 2048.0, inverse, np.where(wavelen > 8192.0, inverse / 8.0, blended))
    return jnp.asarray(scaled, dtype=jnp.float32)


def ancestry(parents):
    seg_count = parents.shape[0]
    indices = jnp.arange(seg_count, dtype=jnp.int32)
    linked = (
        (indices[:, None] == indices[None, :]) | (parents[:, None] == indices[None, :])
    ).astype(jnp.float32)
    for sweep in range(max(1, (seg_count - 1).bit_length())):
        linked = (
            jnp.dot(
                linked, linked, precision=lax.Precision.HIGHEST, preferred_element_type=jnp.float32
            )
            > 0.5
        ).astype(jnp.float32)
    return linked


def token_places(seg_row, linked):
    seg_count = linked.shape[0]
    onehot = (seg_row[:, None] == jnp.arange(seg_count, dtype=jnp.int32)[None, :]).astype(
        jnp.float32
    )
    lengths = jnp.sum(onehot, axis=0)
    starts = jnp.cumsum(lengths) - lengths
    before = jnp.sum(linked * lengths[None, :], axis=1) - lengths
    token_ids = jnp.arange(seg_row.shape[0], dtype=jnp.int32).astype(jnp.float32)
    return (
        STEM
        + token_ids
        - jnp.sum(onehot * starts[None, :], axis=1)
        + jnp.sum(onehot * before[None, :], axis=1)
    )


def turn_kernel(q_ref, k_ref, v_ref, cos_ref, sin_ref, o_ref):
    cosine = cos_ref[...]
    sine = sin_ref[...]

    def turned(part):
        wide = part.astype(jnp.float32)
        return (wide * cosine + pltpu.roll(wide, HD // 2, 1) * sine).astype(jnp.bfloat16)

    for head in range(4):
        at = head % 2 * HD
        o_ref[head // 2, 0, :, at : at + HD] = turned(q_ref[:, head * HD : head * HD + HD])
    o_ref[0, 0, :, 2 * HD :] = turned(k_ref[...])
    o_ref[1, 0, :, 2 * HD :] = v_ref[...]


def turn(q, k, v, cosine, sine):
    tok = q.shape[0]
    return pl.pallas_call(
        turn_kernel,
        out_shape=jax.ShapeDtypeStruct((2, KVH, tok, 3 * HD), jnp.bfloat16),
        grid=(KVH,),
        in_specs=[
            pl.BlockSpec((tok, 4 * HD), lambda e: (0, e)),
            pl.BlockSpec((tok, HD), lambda e: (0, e)),
            pl.BlockSpec((tok, HD), lambda e: (0, e)),
            pl.BlockSpec((tok, HD), lambda e: (0, 0)),
            pl.BlockSpec((tok, HD), lambda e: (0, 0)),
        ],
        out_specs=pl.BlockSpec((2, 1, tok, 3 * HD), lambda e: (0, e, 0, 0)),
        name="turn",
    )(q, k, v, cosine, sine)


def held_at(x, core, group):
    chip = lax.div(group, 2)
    here = chip == x
    other = jnp.where(core == 0, NEAR_OF(x), FAR_OF(x))
    own = jnp.where(here, 0, 1 + core)
    mate = jnp.where(here, 3, 4)
    found = jnp.where(lax.rem(group, 2) == core, own, mate)
    return jnp.where(here | (chip == other), found, 5)


def NEAR_OF(x):
    return x + 1 - 2 * lax.rem(x, 2)


def FAR_OF(x):
    return 3 - x


def swap_kernel(spot, own, a_one, b_one, out, sems):
    core = spot[1]
    pltpu.make_async_copy(own.at[1 - core], out.at[0], sems.at[0]).start()

    @pl.when(core == 0)
    def _():
        pltpu.make_async_copy(b_one, out.at[1], sems.at[1]).start()

    @pl.when(core != 0)
    def _():
        pltpu.make_async_copy(a_one, out.at[1], sems.at[1]).start()

    for item in range(2):
        pltpu.make_async_copy(b_one, out.at[item], sems.at[item]).wait()


def relay_kernel(spot, owner, own, a_one, b_one, mate, out, sems):
    x, core = spot[0], spot[1]
    to = jnp.where(core == 0, FAR_OF(x), NEAR_OF(x))
    for item in range(2):
        code = held_at(x, core, owner[2 * to + item])
        sources = (own.at[core], a_one, b_one, mate.at[0], mate.at[1])
        for place, source in enumerate(sources):
            chosen = code == place if place else (code == 0) | (code == 5)

            @pl.when(chosen)
            def _(source=source):
                pltpu.make_async_copy(source, out.at[item], sems.at[item]).start()

    for item in range(2):
        pltpu.make_async_copy(a_one, out.at[item], sems.at[item]).wait()


def settle_kernel(spot, owner, own, a_one, b_one, mate, two, out, sems):
    x, core = spot[0], spot[1]
    for pack in range(2):
        code = held_at(x, core, owner[2 * x + pack])
        sources = (own.at[core], a_one, b_one, mate.at[0], mate.at[1], two.at[pack])
        for place, source in enumerate(sources):

            @pl.when(code == place)
            def _(source=source):
                for e in range(KVH):
                    pltpu.make_async_copy(
                        source.at[:, pl.ds(e * HD, HD)], out.at[pack, e], sems.at[pack, e]
                    ).start()

    for pack in range(2):
        for e in range(KVH):
            pltpu.make_async_copy(
                a_one.at[:, pl.ds(0, HD)], out.at[pack, e], sems.at[pack, e]
            ).wait()


def moved(kernel, shape, sems, scalars, arrays):
    return pl.pallas_call(
        kernel,
        out_shape=jax.ShapeDtypeStruct(shape, jnp.bfloat16),
        grid_spec=pltpu.PrefetchScalarGridSpec(
            num_scalar_prefetch=len(scalars),
            grid=(1,),
            in_specs=[pl.BlockSpec(memory_space=pl.ANY)] * len(arrays),
            out_specs=pl.BlockSpec(shape, lambda *_: (0,) * len(shape)),
            scratch_shapes=[pltpu.SemaphoreType.DMA(sems)],
        ),
        name=kernel.__name__,
    )(*scalars, *arrays)


def longest(ref, rows):
    most = jnp.zeros((1, 1), jnp.float32)
    for at in range(0, rows, 512):
        wide = ref[at : at + 512, :HD].astype(jnp.float32)
        norms = jnp.sum(wide * wide, axis=1, keepdims=True)
        most = jnp.maximum(most, jnp.max(norms, axis=0, keepdims=True))
    return jnp.broadcast_to(jnp.sqrt(most), (8, HD))


def stacked(q_ref):
    return jnp.concatenate([q_ref[:, :HD], q_ref[:, HD : 2 * HD]], axis=0)


def ceiling(rows, top):
    wide = rows.astype(jnp.float32)
    return jnp.sqrt(jnp.sum(wide * wide, axis=1, keepdims=True)) * top * 1.02 - SHIFT


def score(qa, ref, start, size):
    return lax.dot_general(
        qa[...], ref[pl.ds(start, size), :], NT, preferred_element_type=jnp.float32
    )


def fill(core, mine_ref, other_ref, k_side, ka, va):
    mine = mine_ref[...]
    other = other_ref[...]
    first = core == 0
    ka[:, :HD] = jnp.where(first, mine, other)
    va[:, :HD] = jnp.where(first, other, mine)
    ka[:, HD:] = k_side
    va[:, HD:] = jnp.ones_like(k_side)


def put(o_ref, total, side):
    rows = o_ref.shape[1]
    for head in range(o_ref.shape[0]):
        o_ref[head, :, :HD] = total[head * rows : head * rows + rows]
        o_ref[head, :, HD:] = side[head * rows : head * rows + rows]


def pack_kernel(
    core, seen, q_ref, mine_ref, other_ref, qb_ref, kb_ref, o_ref, qa, ka, va, top, acc
):
    qi = pl.program_id(0)
    rows = 2 * BQ
    lane = lax.broadcasted_iota(jnp.int32, (1, HD), 1)

    @pl.when(qi == 0)
    def _():
        fill(core[0], mine_ref, other_ref, kb_ref[...], ka, va)
        top[...] = longest(ka, ka.shape[0])

    q_rows = stacked(q_ref)
    qa[:, :HD] = q_rows
    side = jnp.concatenate([qb_ref[...], qb_ref[...]], axis=0).astype(jnp.float32)
    row = lax.broadcasted_iota(jnp.int32, (rows, BQ), 0)
    ahead = lax.broadcasted_iota(jnp.int32, (rows, BQ), 1) > jnp.where(row >= BQ, row - BQ, row)
    here = pl.multiple_of(qi * BQ, BQ)

    def run(shift):
        qa[:, HD:] = jnp.where(lane == SEGS, shift, side).astype(jnp.bfloat16)
        weights = jnp.where(ahead, 0.0, jnp.exp2(score(qa, ka, here, BQ) * SCALE))
        acc[...] = jnp.dot(
            weights.astype(jnp.bfloat16), va[pl.ds(here, BQ), :], preferred_element_type=jnp.float32
        )

        def body(kj, carry):
            @pl.when(seen[qi, kj] > 0)
            def _():
                at = pl.multiple_of(kj * BQ, BQ)
                part = jnp.exp2(score(qa, ka, at, BQ) * SCALE).astype(jnp.bfloat16)
                acc[...] += jnp.dot(
                    part, va[pl.ds(at, BQ), :], preferred_element_type=jnp.float32
                )

            return carry

        lax.fori_loop(0, qi, body, 0)
        kept = qa[:, HD:].astype(jnp.float32)
        shift_kept = jnp.sum(jnp.where(lane == SEGS, kept, 0.0), axis=1, keepdims=True)
        put(o_ref, acc[:, :HD], jnp.where(lane == 1, shift_kept, acc[:, HD:]))

    run(ceiling(q_rows, top[0:1, 0:1]))

    @pl.when(jnp.min(acc[:, HD:]) < TINY)
    def _():
        qa[:, HD:] = side.astype(jnp.bfloat16)
        most = jnp.max(
            jnp.where(ahead, BARRED, score(qa, ka, here, BQ)), axis=1, keepdims=True
        )

        def body(kj, most):
            part = score(qa, ka, pl.multiple_of(kj * BQ, BQ), BQ)
            return jnp.maximum(most, jnp.max(part, axis=1, keepdims=True))

        run(lax.fori_loop(0, qi, body, most))


def pack_part(core, seen, arrived, other, q_side, k_side):
    pack = arrived.shape[0]
    once = dict(pipeline_mode=pl.Buffered(1))
    return pl.pallas_call(
        pack_kernel,
        out_shape=jax.ShapeDtypeStruct((2, pack, 2 * HD), jnp.float32),
        grid_spec=pltpu.PrefetchScalarGridSpec(
            num_scalar_prefetch=2,
            grid=(pack // BQ,),
            in_specs=[
                pl.BlockSpec((BQ, 2 * HD), lambda i, *_: (i, 0)),
                pl.BlockSpec((pack, HD), lambda i, *_: (0, 2), **once),
                pl.BlockSpec((pack, HD), lambda i, *_: (0, 0), **once),
                pl.BlockSpec((BQ, HD), lambda i, *_: (i, 0)),
                pl.BlockSpec((pack, HD), lambda i, *_: (0, 0), **once),
            ],
            out_specs=pl.BlockSpec((2, BQ, 2 * HD), lambda i, *_: (0, i, 0)),
            scratch_shapes=[
                pltpu.VMEM((2 * BQ, 2 * HD), jnp.bfloat16),
                pltpu.VMEM((pack, 2 * HD), jnp.bfloat16),
                pltpu.VMEM((pack, 2 * HD), jnp.bfloat16),
                pltpu.VMEM((8, HD), jnp.float32),
                pltpu.VMEM((2 * BQ, 2 * HD), jnp.float32),
            ],
        ),
        compiler_params=pltpu.CompilerParams(vmem_limit_bytes=ROOM),
        cost_estimate=pl.CostEstimate(
            flops=8 * pack * pack * HD, bytes_accessed=8 << 20, transcendentals=pack * pack
        ),
        name="pack_part",
    )(core, seen, arrived, arrived, other, q_side, k_side)


def stem_kernel(core, q_ref, mine_ref, other_ref, part_ref, o_ref, qa, top, acc):
    stem = mine_ref.shape[0]
    heads, rows = part_ref.shape[:2]
    lane = lax.broadcasted_iota(jnp.int32, (1, HD), 1)
    first = core[0] == 0
    side = jnp.broadcast_to(jnp.where(lane == SEGS, -1.0, 0.0).astype(jnp.bfloat16), (CK, HD))
    ones = jnp.ones((CK, HD), jnp.bfloat16)

    def keys(at):
        here = pl.ds(at, CK)
        return jnp.where(first, mine_ref[here, :], other_ref[here, :])

    @pl.when(pl.program_id(0) == 0)
    def _():
        def body(step, most):
            wide = keys(pl.multiple_of(step * CK, CK)).astype(jnp.float32)
            norms = jnp.sum(wide * wide, axis=1, keepdims=True)
            return jnp.maximum(most, jnp.max(norms, axis=0, keepdims=True))

        most = lax.fori_loop(0, stem // CK, body, jnp.zeros((1, 1), jnp.float32))
        top[...] = jnp.broadcast_to(jnp.sqrt(most), (8, HD))

    q_rows = jnp.concatenate([q_ref[:, h * HD : h * HD + HD] for h in range(heads)], axis=0)
    qa[:, :HD] = q_rows

    def scores(at):
        wide = jnp.concatenate([keys(at), side], axis=1)
        return lax.dot_general(qa[...], wide, NT, preferred_element_type=jnp.float32)

    def run(shift):
        qa[:, HD:] = jnp.where(lane == SEGS, shift, 0.0).astype(jnp.bfloat16)
        total = None
        held = scores(0)
        for at in range(0, stem, CK):
            ahead = scores(at + CK) if at + CK < stem else None
            weights = jnp.exp2(held * SCALE).astype(jnp.bfloat16)
            here = pl.ds(at, CK)
            wide = jnp.where(first, other_ref[here, :], mine_ref[here, :])
            wide = jnp.concatenate([wide, ones], axis=1)
            part = jnp.dot(weights, wide, preferred_element_type=jnp.float32)
            total = part if total is None else total + part
            held = ahead
        acc[...] = total

    def finish():
        kept = qa[:, HD:].astype(jnp.float32)
        shift = jnp.sum(jnp.where(lane == SEGS, kept, 0.0), axis=1, keepdims=True)
        part = jnp.concatenate([part_ref[h] for h in range(heads)], axis=0)
        before = part[:, HD + 1 : HD + 2]
        most = jnp.maximum(shift, before)
        new = jnp.exp2((shift - most) * SCALE)
        old = jnp.exp2((before - most) * SCALE)
        total = acc[:, HD : HD + 1] * new + part[:, HD : HD + 1] * old
        mixed = (acc[:, :HD] * new + part[:, :HD] * old) / total
        for h in range(heads):
            o_ref[:, h * HD : h * HD + HD] = mixed[h * rows : h * rows + rows].astype(jnp.bfloat16)

    run(ceiling(q_rows, top[0:1, 0:1]))
    finish()

    @pl.when(jnp.min(acc[:, HD:]) < TINY)
    def _():
        qa[:, HD:] = jnp.zeros_like(q_rows)

        def body(step, most):
            part = scores(pl.multiple_of(step * CK, CK))
            return jnp.maximum(most, jnp.max(part, axis=1, keepdims=True))

        low = jnp.full((heads * rows, 1), BARRED, jnp.float32)
        run(lax.fori_loop(0, stem // CK, body, low))
        finish()


def stem_part(core, arrived, mine, other, before):
    pack = arrived.shape[0]
    stem = mine.shape[0]
    once = dict(pipeline_mode=pl.Buffered(1))
    return pl.pallas_call(
        stem_kernel,
        out_shape=jax.ShapeDtypeStruct((pack, 2 * HD), jnp.bfloat16),
        grid_spec=pltpu.PrefetchScalarGridSpec(
            num_scalar_prefetch=1,
            grid=(pack // BQ,),
            in_specs=[
                pl.BlockSpec((BQ, 2 * HD), lambda i, *_: (i, 0)),
                pl.BlockSpec((stem, HD), lambda i, *_: (0, 0), **once),
                pl.BlockSpec((stem, HD), lambda i, *_: (0, 0), **once),
                pl.BlockSpec((2, BQ, 2 * HD), lambda i, *_: (0, i, 0)),
            ],
            out_specs=pl.BlockSpec((BQ, 2 * HD), lambda i, *_: (i, 0)),
            scratch_shapes=[
                pltpu.VMEM((2 * BQ, 2 * HD), jnp.bfloat16),
                pltpu.VMEM((8, HD), jnp.float32),
                pltpu.VMEM((2 * BQ, 2 * HD), jnp.float32),
            ],
        ),
        compiler_params=pltpu.CompilerParams(vmem_limit_bytes=ROOM),
        cost_estimate=pl.CostEstimate(
            flops=8 * pack * stem * HD,
            bytes_accessed=8 << 20,
            transcendentals=2 * pack * stem,
        ),
        name="stem_part",
    )(core, arrived, mine, other, before)


def gather_kernel(core, mine_ref, other_ref, o_ref):
    first = core[0] == 0
    for e in range(mine_ref.shape[1]):
        mine = mine_ref[0, e]
        other = other_ref[e]
        at = 4 * HD * e
        o_ref[:, at : at + 2 * HD] = jnp.where(first, mine, other)
        o_ref[:, at + 2 * HD : at + 4 * HD] = jnp.where(first, other, mine)


def gather(core, mine, other):
    tok = mine.shape[2]
    heads = KVH // 2
    return pl.pallas_call(
        gather_kernel,
        out_shape=jax.ShapeDtypeStruct((tok, H * HD), jnp.bfloat16),
        grid_spec=pltpu.PrefetchScalarGridSpec(
            num_scalar_prefetch=1,
            grid=(2,),
            in_specs=[
                pl.BlockSpec((1, heads, tok, 2 * HD), lambda i, core: (core[0], i, 0, 0)),
                pl.BlockSpec((heads, tok, 2 * HD), lambda i, core: (i, 0, 0)),
            ],
            out_specs=pl.BlockSpec((tok, H * HD // 2), lambda i, core: (0, i)),
        ),
        name="gather",
    )(core, mine, other)


def shards(queries, keys, values, stem_kv, seg_ids, seg_parent, stem_owner):
    tok = queries.shape[1]
    x = lax.axis_index("x")
    core = lax.axis_index("core")
    spot = lax.axis_index(SEQ)
    pack_len = tok * 16
    core_row = core[None].astype(jnp.int32)
    here = jnp.stack([x, core]).astype(jnp.int32)

    own = stem_kv[0]
    a_one = lax.ppermute(own[0], "x", NEAR)
    b_one = lax.ppermute(own[1], "x", FAR)

    linked = ancestry(seg_parent[0])
    places = token_places(seg_ids[0], linked)
    own_places = lax.dynamic_slice_in_dim(places, spot * tok, tok)
    angles = own_places[:, None] * rotary_table()[None, :]
    cosine, sine = jnp.cos(angles), jnp.sin(angles)
    sent = turn(
        queries[0],
        keys[0],
        values[0],
        jnp.concatenate([cosine, cosine], axis=1),
        jnp.concatenate([-sine, sine], axis=1),
    )

    a_one, b_one, sent = lax.optimization_barrier((a_one, b_one, sent))

    passed = moved(swap_kernel, own.shape, (2,), (here,), (own, a_one, b_one))
    mate = lax.ppermute(passed, "core", FLIP)
    sent, passed = lax.optimization_barrier((sent, passed))
    crossed = lax.all_to_all(sent, "core", split_axis=0, concat_axis=0, tiled=True)
    mate, crossed = lax.optimization_barrier((mate, crossed))

    arrived = lax.all_to_all(
        crossed.reshape(16, tok, 3 * HD), SEQ, split_axis=0, concat_axis=0, tiled=True
    ).reshape(pack_len, 3 * HD)
    pair = lax.ppermute(arrived[:, 2 * HD :], "core", FLIP)

    wanted = moved(
        relay_kernel, own.shape, (2,), (here, stem_owner), (own, a_one, b_one, mate)
    )
    two = lax.ppermute(
        wanted,
        ("x", "core"),
        [(2 * i, 2 * j) for i, j in FAR] + [(2 * i + 1, 2 * j + 1) for i, j in NEAR],
    )
    seg_ids, seg_parent, _ = lax.optimization_barrier((seg_ids, seg_parent, wanted))

    rows = jnp.concatenate([seg_ids[0], seg_parent[0]])
    rows = jnp.where(spot // KVH == core, rows, lax.ppermute(rows, "core", FLIP))
    seg_row, reach = rows[:pack_len], ancestry(rows[pack_len:])
    onehot = (seg_row[:, None] == jnp.arange(HD, dtype=jnp.int32)[None, :]).astype(jnp.float32)
    barred = jnp.pad(BARRED * (1.0 - reach), ((0, HD - SEGS), (0, HD - SEGS)))
    q_side = jnp.dot(onehot, barred, precision=lax.Precision.HIGHEST).astype(jnp.bfloat16)
    k_side = jnp.where(jnp.arange(HD)[None, :] == SEGS, -1.0, onehot).astype(jnp.bfloat16)
    q_has = onehot.reshape(pack_len // BQ, BQ, HD).max(axis=1)[:, :SEGS]
    seen = (q_has @ reach @ q_has.T > 0.5).astype(jnp.int32)

    stems = moved(
        settle_kernel,
        (2, KVH, own.shape[1], HD),
        (2, KVH),
        (here, stem_owner),
        (own, a_one, b_one, mate, two),
    ).reshape(16, own.shape[1], HD)
    mine = lax.all_to_all(stems, SEQ, split_axis=0, concat_axis=0, tiled=True).reshape(STEM, HD)
    arrived, pair, _ = lax.optimization_barrier((arrived, pair, stems))
    partial = pack_part(core_row, seen, arrived, pair, q_side, k_side)
    mine, partial = lax.optimization_barrier((mine, partial))
    other = lax.ppermute(mine, "core", FLIP)
    mixed = stem_part(core_row, arrived, mine, other, partial)

    back = lax.all_to_all(
        mixed.reshape(16, tok, 2 * HD), SEQ, split_axis=0, concat_axis=0, tiled=True
    ).reshape(2, KVH, tok, 2 * HD)
    away = lax.dynamic_index_in_dim(back, 1 - core, 0, keepdims=False)
    return gather(core_row, back, lax.ppermute(away, "core", FLIP))[None]


def solution(mesh):
    grid = Mesh(mesh.devices.reshape(4, 2, 4, 4), ("x", "core", "z", "y"))
    dp, seq = ("x", "core"), SEQ
    placed = (
        P(dp, seq, None),
        P(dp, seq, None),
        P(dp, seq, None),
        P(dp, None, seq, None),
        P(dp, None),
        P(dp, None),
        P(),
    )
    return jax.shard_map(
        shards, mesh=grid, in_specs=placed, out_specs=P(dp, seq, None), check_vma=False
    )
```

```python
import math

import jax
import jax.numpy as jnp
import numpy as np
from jax import lax
from jax.experimental import pallas as pl
from jax.experimental.pallas import tpu as pltpu
from jax.sharding import Mesh
from jax.sharding import PartitionSpec as P

H = 32
KVH = 8
HD = 128
STEM = 4096
SEGS = 16
BARRED = -1e30
BQ = 512
CK = 256
SCALE = HD**-0.5 * math.log2(math.e)
SHIFT = 70.0 / SCALE
TINY = 2.0**-16
FLIP = [(0, 1), (1, 0)]
NEAR = [(0, 1), (1, 0), (2, 3), (3, 2)]
FAR = [(0, 3), (3, 0), (1, 2), (2, 1)]
SEQ = ("z", "y")
NT = (((1,), (1,)), ((), ()))
ROOM = 56 * 1024 * 1024


def rotary_table():
    halves = np.arange(0, HD, 2) / HD
    inverse = 1.0 / 500000.0**halves
    wavelen = 2.0 * np.pi / inverse
    smooth = (8192.0 / wavelen - 1.0) / 3.0
    blended = (1.0 - smooth) * inverse / 8.0 + smooth * inverse
    scaled = np.where(wavelen < 2048.0, inverse, np.where(wavelen > 8192.0, inverse / 8.0, blended))
    return jnp.asarray(scaled, dtype=jnp.float32)


def ancestry(parents):
    seg_count = parents.shape[0]
    indices = jnp.arange(seg_count, dtype=jnp.int32)
    linked = (
        (indices[:, None] == indices[None, :]) | (parents[:, None] == indices[None, :])
    ).astype(jnp.float32)
    for sweep in range(max(1, (seg_count - 1).bit_length())):
        linked = (
            jnp.dot(
                linked, linked, precision=lax.Precision.HIGHEST, preferred_element_type=jnp.float32
            )
            > 0.5
        ).astype(jnp.float32)
    return linked


def token_places(seg_row, linked):
    seg_count = linked.shape[0]
    onehot = (seg_row[:, None] == jnp.arange(seg_count, dtype=jnp.int32)[None, :]).astype(
        jnp.float32
    )
    lengths = jnp.sum(onehot, axis=0)
    starts = jnp.cumsum(lengths) - lengths
    before = jnp.sum(linked * lengths[None, :], axis=1) - lengths
    token_ids = jnp.arange(seg_row.shape[0], dtype=jnp.int32).astype(jnp.float32)
    return (
        STEM
        + token_ids
        - jnp.sum(onehot * starts[None, :], axis=1)
        + jnp.sum(onehot * before[None, :], axis=1)
    )


def turn_kernel(
    spot, q_own, k_own, v_own, q_mate, k_mate, v_mate, cos_ref, sin_ref, o_ref
):
    core = spot[1]
    pack = pl.program_id(0)

    def run(place, q_ref, k_ref, v_ref):
        cosine = cos_ref[place]
        sine = sin_ref[place]

        def turned(part):
            wide = part.astype(jnp.float32)
            return (wide * cosine + pltpu.roll(wide, HD // 2, 1) * sine).astype(jnp.bfloat16)

        for e in range(KVH):
            for head in range(2):
                at = pl.multiple_of((4 * e + head + 2 * core) * HD, HD)
                o_ref[0, e, :, head * HD : head * HD + HD] = turned(q_ref[:, pl.ds(at, HD)])
            at = e * HD
            o_ref[0, e, :, 2 * HD :] = jnp.where(
                core == 0, turned(k_ref[:, at : at + HD]), v_ref[:, at : at + HD]
            )

    @pl.when(pack == core)
    def _():
        run(0, q_own, k_own, v_own)

    @pl.when(pack != core)
    def _():
        run(1, q_mate, k_mate, v_mate)


def turn(here, own, mate, cosine, sine):
    tok = own[0].shape[0]
    whole = [
        pl.BlockSpec(part.shape, lambda i, here: (0, 0), pipeline_mode=pl.Buffered(1))
        for part in own + mate
    ]
    table = pl.BlockSpec(cosine.shape, lambda i, here: (0, 0, 0), pipeline_mode=pl.Buffered(1))
    return pl.pallas_call(
        turn_kernel,
        out_shape=jax.ShapeDtypeStruct((2, KVH, tok, 3 * HD), jnp.bfloat16),
        grid_spec=pltpu.PrefetchScalarGridSpec(
            num_scalar_prefetch=1,
            grid=(2,),
            in_specs=whole + [table, table],
            out_specs=pl.BlockSpec((1, KVH, tok, 3 * HD), lambda i, here: (i, 0, 0, 0)),
        ),
        compiler_params=pltpu.CompilerParams(vmem_limit_bytes=32 * 1024 * 1024),
        name="turn",
    )(here, *own, *mate, cosine, sine)


def held_at(x, core, group):
    chip = lax.div(group, 2)
    here = chip == x
    other = jnp.where(core == 0, NEAR_OF(x), FAR_OF(x))
    own = jnp.where(here, 0, 1 + core)
    mate = jnp.where(here, 3, 4)
    found = jnp.where(lax.rem(group, 2) == core, own, mate)
    return jnp.where(here | (chip == other), found, 5)


def NEAR_OF(x):
    return x + 1 - 2 * lax.rem(x, 2)


def FAR_OF(x):
    return 3 - x


def swap_kernel(spot, own, a_one, b_one, out, sems):
    core = spot[1]
    pltpu.make_async_copy(own.at[1 - core], out.at[0], sems.at[0]).start()

    @pl.when(core == 0)
    def _():
        pltpu.make_async_copy(b_one, out.at[1], sems.at[1]).start()

    @pl.when(core != 0)
    def _():
        pltpu.make_async_copy(a_one, out.at[1], sems.at[1]).start()

    for item in range(2):
        pltpu.make_async_copy(b_one, out.at[item], sems.at[item]).wait()


def relay_kernel(spot, owner, own, a_one, b_one, mate, out, sems):
    x, core = spot[0], spot[1]
    to = jnp.where(core == 0, FAR_OF(x), NEAR_OF(x))
    for item in range(2):
        code = held_at(x, core, owner[2 * to + item])
        sources = (own.at[core], a_one, b_one, mate.at[0], mate.at[1])
        for place, source in enumerate(sources):
            chosen = code == place if place else (code == 0) | (code == 5)

            @pl.when(chosen)
            def _(source=source):
                pltpu.make_async_copy(source, out.at[item], sems.at[item]).start()

    for item in range(2):
        pltpu.make_async_copy(a_one, out.at[item], sems.at[item]).wait()


def settle_kernel(spot, owner, own, a_one, b_one, mate, two, out, sems):
    x, core = spot[0], spot[1]
    for pack in range(2):
        code = held_at(x, core, owner[2 * x + pack])
        sources = (own.at[core], a_one, b_one, mate.at[0], mate.at[1], two.at[pack])
        for place, source in enumerate(sources):

            @pl.when(code == place)
            def _(source=source):
                for e in range(KVH):
                    pltpu.make_async_copy(
                        source.at[:, pl.ds(e * HD, HD)], out.at[pack, e], sems.at[pack, e]
                    ).start()

    for pack in range(2):
        for e in range(KVH):
            pltpu.make_async_copy(
                a_one.at[:, pl.ds(0, HD)], out.at[pack, e], sems.at[pack, e]
            ).wait()


def moved(kernel, shape, sems, scalars, arrays):
    return pl.pallas_call(
        kernel,
        out_shape=jax.ShapeDtypeStruct(shape, jnp.bfloat16),
        grid_spec=pltpu.PrefetchScalarGridSpec(
            num_scalar_prefetch=len(scalars),
            grid=(1,),
            in_specs=[pl.BlockSpec(memory_space=pl.ANY)] * len(arrays),
            out_specs=pl.BlockSpec(shape, lambda *_: (0,) * len(shape)),
            scratch_shapes=[pltpu.SemaphoreType.DMA(sems)],
        ),
        name=kernel.__name__,
    )(*scalars, *arrays)


def longest(ref, rows):
    most = jnp.zeros((1, 1), jnp.float32)
    for at in range(0, rows, 512):
        wide = ref[at : at + 512, :HD].astype(jnp.float32)
        norms = jnp.sum(wide * wide, axis=1, keepdims=True)
        most = jnp.maximum(most, jnp.max(norms, axis=0, keepdims=True))
    return jnp.broadcast_to(jnp.sqrt(most), (8, HD))


def stacked(q_ref):
    return jnp.concatenate([q_ref[:, :HD], q_ref[:, HD : 2 * HD]], axis=0)


def ceiling(rows, top):
    wide = rows.astype(jnp.float32)
    return jnp.sqrt(jnp.sum(wide * wide, axis=1, keepdims=True)) * top * 1.02 - SHIFT


def score(qa, ref, start, size):
    return lax.dot_general(
        qa[...], ref[pl.ds(start, size), :], NT, preferred_element_type=jnp.float32
    )


def fill(core, mine_ref, other_ref, k_side, ka, va):
    mine = mine_ref[...]
    other = other_ref[...]
    first = core == 0
    ka[:, :HD] = jnp.where(first, mine, other)
    va[:, :HD] = jnp.where(first, other, mine)
    ka[:, HD:] = k_side
    va[:, HD:] = jnp.ones_like(k_side)


def put(o_ref, total, side):
    rows = o_ref.shape[1]
    for head in range(o_ref.shape[0]):
        o_ref[head, :, :HD] = total[head * rows : head * rows + rows]
        o_ref[head, :, HD:] = side[head * rows : head * rows + rows]


def pack_kernel(
    core, seen, q_ref, mine_ref, other_ref, qb_ref, kb_ref, o_ref, qa, ka, va, top, acc
):
    qi = pl.program_id(0)
    rows = 2 * BQ
    lane = lax.broadcasted_iota(jnp.int32, (1, HD), 1)

    @pl.when(qi == 0)
    def _():
        fill(core[0], mine_ref, other_ref, kb_ref[...], ka, va)
        top[...] = longest(ka, ka.shape[0])

    q_rows = stacked(q_ref)
    qa[:, :HD] = q_rows
    side = jnp.concatenate([qb_ref[...], qb_ref[...]], axis=0).astype(jnp.float32)
    row = lax.broadcasted_iota(jnp.int32, (rows, BQ), 0)
    ahead = lax.broadcasted_iota(jnp.int32, (rows, BQ), 1) > jnp.where(row >= BQ, row - BQ, row)
    here = pl.multiple_of(qi * BQ, BQ)

    def run(shift):
        qa[:, HD:] = jnp.where(lane == SEGS, shift, side).astype(jnp.bfloat16)
        weights = jnp.where(ahead, 0.0, jnp.exp2(score(qa, ka, here, BQ) * SCALE))
        acc[...] = jnp.dot(
            weights.astype(jnp.bfloat16), va[pl.ds(here, BQ), :], preferred_element_type=jnp.float32
        )

        def body(kj, carry):
            @pl.when(seen[qi, kj] > 0)
            def _():
                at = pl.multiple_of(kj * BQ, BQ)
                part = jnp.exp2(score(qa, ka, at, BQ) * SCALE).astype(jnp.bfloat16)
                acc[...] += jnp.dot(
                    part, va[pl.ds(at, BQ), :], preferred_element_type=jnp.float32
                )

            return carry

        lax.fori_loop(0, qi, body, 0)
        kept = qa[:, HD:].astype(jnp.float32)
        shift_kept = jnp.sum(jnp.where(lane == SEGS, kept, 0.0), axis=1, keepdims=True)
        put(o_ref, acc[:, :HD], jnp.where(lane == 1, shift_kept, acc[:, HD:]))

    run(ceiling(q_rows, top[0:1, 0:1]))

    @pl.when(jnp.min(acc[:, HD:]) < TINY)
    def _():
        qa[:, HD:] = side.astype(jnp.bfloat16)
        most = jnp.max(
            jnp.where(ahead, BARRED, score(qa, ka, here, BQ)), axis=1, keepdims=True
        )

        def body(kj, most):
            part = score(qa, ka, pl.multiple_of(kj * BQ, BQ), BQ)
            return jnp.maximum(most, jnp.max(part, axis=1, keepdims=True))

        run(lax.fori_loop(0, qi, body, most))


def pack_part(core, seen, arrived, other, q_side, k_side):
    pack = arrived.shape[0]
    once = dict(pipeline_mode=pl.Buffered(1))
    return pl.pallas_call(
        pack_kernel,
        out_shape=jax.ShapeDtypeStruct((2, pack, 2 * HD), jnp.float32),
        grid_spec=pltpu.PrefetchScalarGridSpec(
            num_scalar_prefetch=2,
            grid=(pack // BQ,),
            in_specs=[
                pl.BlockSpec((BQ, 2 * HD), lambda i, *_: (i, 0)),
                pl.BlockSpec((pack, HD), lambda i, *_: (0, 2), **once),
                pl.BlockSpec((pack, HD), lambda i, *_: (0, 0), **once),
                pl.BlockSpec((BQ, HD), lambda i, *_: (i, 0)),
                pl.BlockSpec((pack, HD), lambda i, *_: (0, 0), **once),
            ],
            out_specs=pl.BlockSpec((2, BQ, 2 * HD), lambda i, *_: (0, i, 0)),
            scratch_shapes=[
                pltpu.VMEM((2 * BQ, 2 * HD), jnp.bfloat16),
                pltpu.VMEM((pack, 2 * HD), jnp.bfloat16),
                pltpu.VMEM((pack, 2 * HD), jnp.bfloat16),
                pltpu.VMEM((8, HD), jnp.float32),
                pltpu.VMEM((2 * BQ, 2 * HD), jnp.float32),
            ],
        ),
        compiler_params=pltpu.CompilerParams(vmem_limit_bytes=ROOM),
        cost_estimate=pl.CostEstimate(
            flops=8 * pack * pack * HD, bytes_accessed=8 << 20, transcendentals=pack * pack
        ),
        name="pack_part",
    )(core, seen, arrived, arrived, other, q_side, k_side)


def stem_kernel(core, q_ref, mine_ref, other_ref, part_ref, o_ref, qa, top, acc):
    stem = mine_ref.shape[0]
    heads, rows = part_ref.shape[:2]
    lane = lax.broadcasted_iota(jnp.int32, (1, HD), 1)
    first = core[0] == 0
    side = jnp.broadcast_to(jnp.where(lane == SEGS, -1.0, 0.0).astype(jnp.bfloat16), (CK, HD))
    ones = jnp.ones((CK, HD), jnp.bfloat16)

    def keys(at):
        here = pl.ds(at, CK)
        return jnp.where(first, mine_ref[here, :], other_ref[here, :])

    @pl.when(pl.program_id(0) == 0)
    def _():
        def body(step, most):
            wide = keys(pl.multiple_of(step * CK, CK)).astype(jnp.float32)
            norms = jnp.sum(wide * wide, axis=1, keepdims=True)
            return jnp.maximum(most, jnp.max(norms, axis=0, keepdims=True))

        most = lax.fori_loop(0, stem // CK, body, jnp.zeros((1, 1), jnp.float32))
        top[...] = jnp.broadcast_to(jnp.sqrt(most), (8, HD))

    q_rows = jnp.concatenate([q_ref[:, h * HD : h * HD + HD] for h in range(heads)], axis=0)
    qa[:, :HD] = q_rows

    def scores(at):
        wide = jnp.concatenate([keys(at), side], axis=1)
        return lax.dot_general(qa[...], wide, NT, preferred_element_type=jnp.float32)

    def run(shift):
        qa[:, HD:] = jnp.where(lane == SEGS, shift, 0.0).astype(jnp.bfloat16)
        total = None
        held = scores(0)
        for at in range(0, stem, CK):
            ahead = scores(at + CK) if at + CK < stem else None
            weights = jnp.exp2(held * SCALE).astype(jnp.bfloat16)
            here = pl.ds(at, CK)
            wide = jnp.where(first, other_ref[here, :], mine_ref[here, :])
            wide = jnp.concatenate([wide, ones], axis=1)
            part = jnp.dot(weights, wide, preferred_element_type=jnp.float32)
            total = part if total is None else total + part
            held = ahead
        acc[...] = total

    def finish():
        kept = qa[:, HD:].astype(jnp.float32)
        shift = jnp.sum(jnp.where(lane == SEGS, kept, 0.0), axis=1, keepdims=True)
        part = jnp.concatenate([part_ref[h] for h in range(heads)], axis=0)
        before = part[:, HD + 1 : HD + 2]
        most = jnp.maximum(shift, before)
        new = jnp.exp2((shift - most) * SCALE)
        old = jnp.exp2((before - most) * SCALE)
        total = acc[:, HD : HD + 1] * new + part[:, HD : HD + 1] * old
        mixed = (acc[:, :HD] * new + part[:, :HD] * old) / total
        for h in range(heads):
            o_ref[:, h * HD : h * HD + HD] = mixed[h * rows : h * rows + rows].astype(jnp.bfloat16)

    run(ceiling(q_rows, top[0:1, 0:1]))
    finish()

    @pl.when(jnp.min(acc[:, HD:]) < TINY)
    def _():
        qa[:, HD:] = jnp.zeros_like(q_rows)

        def body(step, most):
            part = scores(pl.multiple_of(step * CK, CK))
            return jnp.maximum(most, jnp.max(part, axis=1, keepdims=True))

        low = jnp.full((heads * rows, 1), BARRED, jnp.float32)
        run(lax.fori_loop(0, stem // CK, body, low))
        finish()


def stem_part(core, arrived, mine, other, before):
    pack = arrived.shape[0]
    stem = mine.shape[0]
    once = dict(pipeline_mode=pl.Buffered(1))
    return pl.pallas_call(
        stem_kernel,
        out_shape=jax.ShapeDtypeStruct((pack, 2 * HD), jnp.bfloat16),
        grid_spec=pltpu.PrefetchScalarGridSpec(
            num_scalar_prefetch=1,
            grid=(pack // BQ,),
            in_specs=[
                pl.BlockSpec((BQ, 2 * HD), lambda i, *_: (i, 0)),
                pl.BlockSpec((stem, HD), lambda i, *_: (0, 0), **once),
                pl.BlockSpec((stem, HD), lambda i, *_: (0, 0), **once),
                pl.BlockSpec((2, BQ, 2 * HD), lambda i, *_: (0, i, 0)),
            ],
            out_specs=pl.BlockSpec((BQ, 2 * HD), lambda i, *_: (i, 0)),
            scratch_shapes=[
                pltpu.VMEM((2 * BQ, 2 * HD), jnp.bfloat16),
                pltpu.VMEM((8, HD), jnp.float32),
                pltpu.VMEM((2 * BQ, 2 * HD), jnp.float32),
            ],
        ),
        compiler_params=pltpu.CompilerParams(vmem_limit_bytes=ROOM),
        cost_estimate=pl.CostEstimate(
            flops=8 * pack * stem * HD,
            bytes_accessed=8 << 20,
            transcendentals=2 * pack * stem,
        ),
        name="stem_part",
    )(core, arrived, mine, other, before)


def gather_kernel(core, mine_ref, other_ref, o_ref):
    first = core[0] == 0
    for e in range(mine_ref.shape[1]):
        mine = mine_ref[0, e]
        other = other_ref[e]
        at = 4 * HD * e
        o_ref[:, at : at + 2 * HD] = jnp.where(first, mine, other)
        o_ref[:, at + 2 * HD : at + 4 * HD] = jnp.where(first, other, mine)


def gather(core, mine, other):
    tok = mine.shape[2]
    heads = KVH // 2
    return pl.pallas_call(
        gather_kernel,
        out_shape=jax.ShapeDtypeStruct((tok, H * HD), jnp.bfloat16),
        grid_spec=pltpu.PrefetchScalarGridSpec(
            num_scalar_prefetch=1,
            grid=(2,),
            in_specs=[
                pl.BlockSpec((1, heads, tok, 2 * HD), lambda i, core: (core[0], i, 0, 0)),
                pl.BlockSpec((heads, tok, 2 * HD), lambda i, core: (i, 0, 0)),
            ],
            out_specs=pl.BlockSpec((tok, H * HD // 2), lambda i, core: (0, i)),
        ),
        name="gather",
    )(core, mine, other)


def shards(queries, keys, values, stem_kv, seg_ids, seg_parent, stem_owner):
    tok = queries.shape[1]
    x = lax.axis_index("x")
    core = lax.axis_index("core")
    spot = lax.axis_index(SEQ)
    pack_len = tok * 16
    core_row = core[None].astype(jnp.int32)
    here = jnp.stack([x, core]).astype(jnp.int32)

    raw = (queries[0], keys[0], values[0])
    rows = jnp.concatenate([seg_ids[0], seg_parent[0]])
    rows_mate = lax.ppermute(rows, "core", FLIP)
    raw_mate = tuple(lax.ppermute(part, "core", FLIP) for part in raw)

    own = stem_kv[0]
    a_one = lax.ppermute(own[0], "x", NEAR)
    b_one = lax.ppermute(own[1], "x", FAR)

    both = jnp.stack([rows, rows_mate])
    linked = jax.vmap(ancestry)(both[:, pack_len:])
    places = jax.vmap(token_places)(both[:, :pack_len], linked)
    places = lax.dynamic_slice_in_dim(places, spot * tok, tok, axis=1)
    angles = places[:, :, None] * rotary_table()[None, None, :]
    cosine, sine = jnp.cos(angles), jnp.sin(angles)
    sent = turn(
        here,
        raw,
        raw_mate,
        jnp.concatenate([cosine, cosine], axis=2),
        jnp.concatenate([-sine, sine], axis=2),
    )
    arrived = lax.all_to_all(
        sent.reshape(16, tok, 3 * HD), SEQ, split_axis=0, concat_axis=0, tiled=True
    ).reshape(pack_len, 3 * HD)
    a_one, b_one, sent = lax.optimization_barrier((a_one, b_one, sent))

    passed = moved(swap_kernel, own.shape, (2,), (here,), (own, a_one, b_one))
    mate = lax.ppermute(passed, "core", FLIP)

    wanted = moved(
        relay_kernel, own.shape, (2,), (here, stem_owner), (own, a_one, b_one, mate)
    )
    two = lax.ppermute(
        wanted,
        ("x", "core"),
        [(2 * i, 2 * j) for i, j in FAR] + [(2 * i + 1, 2 * j + 1) for i, j in NEAR],
    )
    both, linked, _ = lax.optimization_barrier((both, linked, wanted))
    two, arrived = lax.optimization_barrier((two, arrived))
    pair = lax.ppermute(arrived[:, 2 * HD :], "core", FLIP)

    ours = spot // KVH == core
    seg_row = jnp.where(ours, both[0, :pack_len], both[1, :pack_len])
    reach = jnp.where(ours, linked[0], linked[1])
    onehot = (seg_row[:, None] == jnp.arange(HD, dtype=jnp.int32)[None, :]).astype(jnp.float32)
    barred = jnp.pad(BARRED * (1.0 - reach), ((0, HD - SEGS), (0, HD - SEGS)))
    q_side = jnp.dot(onehot, barred, precision=lax.Precision.HIGHEST).astype(jnp.bfloat16)
    k_side = jnp.where(jnp.arange(HD)[None, :] == SEGS, -1.0, onehot).astype(jnp.bfloat16)
    q_has = onehot.reshape(pack_len // BQ, BQ, HD).max(axis=1)[:, :SEGS]
    seen = (q_has @ reach @ q_has.T > 0.5).astype(jnp.int32)

    stems = moved(
        settle_kernel,
        (2, KVH, own.shape[1], HD),
        (2, KVH),
        (here, stem_owner),
        (own, a_one, b_one, mate, two),
    ).reshape(16, own.shape[1], HD)
    mine = lax.all_to_all(stems, SEQ, split_axis=0, concat_axis=0, tiled=True).reshape(STEM, HD)
    arrived, pair, _ = lax.optimization_barrier((arrived, pair, stems))
    partial = pack_part(core_row, seen, arrived, pair, q_side, k_side)
    mine, partial = lax.optimization_barrier((mine, partial))
    other = lax.ppermute(mine, "core", FLIP)
    mixed = stem_part(core_row, arrived, mine, other, partial)

    back = lax.all_to_all(
        mixed.reshape(16, tok, 2 * HD), SEQ, split_axis=0, concat_axis=0, tiled=True
    ).reshape(2, KVH, tok, 2 * HD)
    away = lax.dynamic_index_in_dim(back, 1 - core, 0, keepdims=False)
    return gather(core_row, back, lax.ppermute(away, "core", FLIP))[None]


def solution(mesh):
    grid = Mesh(mesh.devices.reshape(4, 2, 4, 4), ("x", "core", "z", "y"))
    dp, seq = ("x", "core"), SEQ
    placed = (
        P(dp, seq, None),
        P(dp, seq, None),
        P(dp, seq, None),
        P(dp, None, seq, None),
        P(dp, None),
        P(dp, None),
        P(),
    )
    return jax.shard_map(
        shards, mesh=grid, in_specs=placed, out_specs=P(dp, seq, None), check_vma=False
    )
```

```python
import math

import jax
import jax.numpy as jnp
import numpy as np
from jax import lax
from jax.experimental import pallas as pl
from jax.experimental.pallas import tpu as pltpu
from jax.sharding import Mesh
from jax.sharding import PartitionSpec as P

H = 32
KVH = 8
HD = 128
STEM = 4096
SEGS = 16
BARRED = -1e30
BQ = 512
CK = 256
SCALE = HD**-0.5 * math.log2(math.e)
SHIFT = 70.0 / SCALE
TINY = 2.0**-16
FLIP = [(0, 1), (1, 0)]
NEAR = [(0, 1), (1, 0), (2, 3), (3, 2)]
FAR = [(0, 3), (3, 0), (1, 2), (2, 1)]
SEQ = ("z", "y")


def joint(step, crossed):
    keys, values = (NEAR, FAR) if step == 0 else (FAR, NEAR)
    return [(2 * i + crossed, 2 * j) for i, j in keys] + [
        (2 * i + 1 - crossed, 2 * j + 1) for i, j in values
    ]


NT = (((1,), (1,)), ((), ()))
ROOM = 56 * 1024 * 1024


def rotary_table():
    halves = np.arange(0, HD, 2) / HD
    inverse = 1.0 / 500000.0**halves
    wavelen = 2.0 * np.pi / inverse
    smooth = (8192.0 / wavelen - 1.0) / 3.0
    blended = (1.0 - smooth) * inverse / 8.0 + smooth * inverse
    scaled = np.where(wavelen < 2048.0, inverse, np.where(wavelen > 8192.0, inverse / 8.0, blended))
    return jnp.asarray(scaled, dtype=jnp.float32)


def ancestry(parents):
    seg_count = parents.shape[0]
    indices = jnp.arange(seg_count, dtype=jnp.int32)
    linked = (
        (indices[:, None] == indices[None, :]) | (parents[:, None] == indices[None, :])
    ).astype(jnp.float32)
    for sweep in range(max(1, (seg_count - 1).bit_length())):
        linked = (
            jnp.dot(
                linked, linked, precision=lax.Precision.HIGHEST, preferred_element_type=jnp.float32
            )
            > 0.5
        ).astype(jnp.float32)
    return linked


def token_places(seg_row, linked):
    seg_count = linked.shape[0]
    onehot = (seg_row[:, None] == jnp.arange(seg_count, dtype=jnp.int32)[None, :]).astype(
        jnp.float32
    )
    lengths = jnp.sum(onehot, axis=0)
    starts = jnp.cumsum(lengths) - lengths
    before = jnp.sum(linked * lengths[None, :], axis=1) - lengths
    token_ids = jnp.arange(seg_row.shape[0], dtype=jnp.int32).astype(jnp.float32)
    return (
        STEM
        + token_ids
        - jnp.sum(onehot * starts[None, :], axis=1)
        + jnp.sum(onehot * before[None, :], axis=1)
    )


def turn_kernel(
    spot, q_own, k_own, v_own, q_mate, k_mate, v_mate, cos_ref, sin_ref, o_ref
):
    core = spot[1]
    pack = pl.program_id(0)

    def run(place, q_ref, k_ref, v_ref):
        cosine = cos_ref[place]
        sine = sin_ref[place]

        def turned(part):
            wide = part.astype(jnp.float32)
            return (wide * cosine + pltpu.roll(wide, HD // 2, 1) * sine).astype(jnp.bfloat16)

        for e in range(KVH):
            for head in range(2):
                at = pl.multiple_of((4 * e + head + 2 * core) * HD, HD)
                o_ref[0, e, :, head * HD : head * HD + HD] = turned(q_ref[:, pl.ds(at, HD)])
            at = e * HD
            o_ref[0, e, :, 2 * HD :] = jnp.where(
                core == 0, turned(k_ref[:, at : at + HD]), v_ref[:, at : at + HD]
            )

    @pl.when(pack == core)
    def _():
        run(0, q_own, k_own, v_own)

    @pl.when(pack != core)
    def _():
        run(1, q_mate, k_mate, v_mate)


def turn(here, own, mate, cosine, sine):
    tok = own[0].shape[0]
    whole = [
        pl.BlockSpec(part.shape, lambda i, here: (0, 0), pipeline_mode=pl.Buffered(1))
        for part in own + mate
    ]
    table = pl.BlockSpec(cosine.shape, lambda i, here: (0, 0, 0), pipeline_mode=pl.Buffered(1))
    return pl.pallas_call(
        turn_kernel,
        out_shape=jax.ShapeDtypeStruct((2, KVH, tok, 3 * HD), jnp.bfloat16),
        grid_spec=pltpu.PrefetchScalarGridSpec(
            num_scalar_prefetch=1,
            grid=(2,),
            in_specs=whole + [table, table],
            out_specs=pl.BlockSpec((1, KVH, tok, 3 * HD), lambda i, here: (i, 0, 0, 0)),
        ),
        compiler_params=pltpu.CompilerParams(vmem_limit_bytes=32 * 1024 * 1024),
        name="turn",
    )(here, *own, *mate, cosine, sine)


def held_at(x, core, group):
    chip = lax.div(group, 2)
    other = jnp.where(core == 0, near_of(x), far_of(x))
    found = jnp.where(lax.rem(group, 2) == core, 0, 2) + jnp.where(chip == x, 0, 1)
    return jnp.where((chip == x) | (chip == other), found, 4)


def near_of(x):
    return x + 1 - 2 * lax.rem(x, 2)


def far_of(x):
    return 3 - x


def relay_kernel(spot, owner, own, same, flip, cross, out, sems):
    x, core = spot[0], spot[1]
    to = jnp.where(core == 0, far_of(x), near_of(x))
    for item in range(2):
        code = held_at(x, core, owner[2 * to + item])
        for place, source in enumerate((own, same, flip, cross)):
            chosen = code == place if place else (code == 0) | (code == 4)

            @pl.when(chosen)
            def _(source=source):
                pltpu.make_async_copy(source, out.at[item], sems.at[item]).start()

    for item in range(2):
        pltpu.make_async_copy(own, out.at[item], sems.at[item]).wait()


def settle_kernel(spot, owner, own, same, flip, cross, two, out, sems):
    x, core = spot[0], spot[1]
    for pack in range(2):
        code = held_at(x, core, owner[2 * x + pack])
        for place, source in enumerate((own, same, flip, cross, two.at[pack])):

            @pl.when(code == place)
            def _(source=source):
                for e in range(KVH):
                    pltpu.make_async_copy(
                        source.at[:, pl.ds(e * HD, HD)], out.at[pack, e], sems.at[pack, e]
                    ).start()

    for pack in range(2):
        for e in range(KVH):
            pltpu.make_async_copy(
                own.at[:, pl.ds(0, HD)], out.at[pack, e], sems.at[pack, e]
            ).wait()


def moved(kernel, shape, sems, scalars, arrays):
    return pl.pallas_call(
        kernel,
        out_shape=jax.ShapeDtypeStruct(shape, jnp.bfloat16),
        grid_spec=pltpu.PrefetchScalarGridSpec(
            num_scalar_prefetch=len(scalars),
            grid=(1,),
            in_specs=[pl.BlockSpec(memory_space=pl.ANY)] * len(arrays),
            out_specs=pl.BlockSpec(shape, lambda *_: (0,) * len(shape)),
            scratch_shapes=[pltpu.SemaphoreType.DMA(sems)],
        ),
        name=kernel.__name__,
    )(*scalars, *arrays)


def longest(ref, rows):
    most = jnp.zeros((1, 1), jnp.float32)
    for at in range(0, rows, 512):
        wide = ref[at : at + 512, :HD].astype(jnp.float32)
        norms = jnp.sum(wide * wide, axis=1, keepdims=True)
        most = jnp.maximum(most, jnp.max(norms, axis=0, keepdims=True))
    return jnp.broadcast_to(jnp.sqrt(most), (8, HD))


def stacked(q_ref):
    return jnp.concatenate([q_ref[:, :HD], q_ref[:, HD : 2 * HD]], axis=0)


def ceiling(rows, top):
    wide = rows.astype(jnp.float32)
    return jnp.sqrt(jnp.sum(wide * wide, axis=1, keepdims=True)) * top * 1.02 - SHIFT


def score(qa, ref, start, size):
    return lax.dot_general(
        qa[...], ref[pl.ds(start, size), :], NT, preferred_element_type=jnp.float32
    )


def fill(core, mine_ref, other_ref, k_side, ka, va):
    mine = mine_ref[...]
    other = other_ref[...]
    first = core == 0
    ka[:, :HD] = jnp.where(first, mine, other)
    va[:, :HD] = jnp.where(first, other, mine)
    ka[:, HD:] = k_side
    va[:, HD:] = jnp.ones_like(k_side)


def put(o_ref, total, side):
    rows = o_ref.shape[1]
    for head in range(o_ref.shape[0]):
        o_ref[head, :, :HD] = total[head * rows : head * rows + rows]
        o_ref[head, :, HD:] = side[head * rows : head * rows + rows]


def pack_kernel(
    core, seen, q_ref, mine_ref, other_ref, qb_ref, kb_ref, o_ref, qa, ka, va, top, acc
):
    qi = pl.program_id(0)
    rows = 2 * BQ
    lane = lax.broadcasted_iota(jnp.int32, (1, HD), 1)

    @pl.when(qi == 0)
    def _():
        fill(core[0], mine_ref, other_ref, kb_ref[...], ka, va)
        top[...] = longest(ka, ka.shape[0])

    q_rows = stacked(q_ref)
    qa[:, :HD] = q_rows
    side = jnp.concatenate([qb_ref[...], qb_ref[...]], axis=0).astype(jnp.float32)
    row = lax.broadcasted_iota(jnp.int32, (rows, BQ), 0)
    ahead = lax.broadcasted_iota(jnp.int32, (rows, BQ), 1) > jnp.where(row >= BQ, row - BQ, row)
    here = pl.multiple_of(qi * BQ, BQ)

    def run(shift):
        qa[:, HD:] = jnp.where(lane == SEGS, shift, side).astype(jnp.bfloat16)
        weights = jnp.where(ahead, 0.0, jnp.exp2(score(qa, ka, here, BQ) * SCALE))
        acc[...] = jnp.dot(
            weights.astype(jnp.bfloat16), va[pl.ds(here, BQ), :], preferred_element_type=jnp.float32
        )

        def body(kj, carry):
            @pl.when(seen[qi, kj] > 0)
            def _():
                at = pl.multiple_of(kj * BQ, BQ)
                part = jnp.exp2(score(qa, ka, at, BQ) * SCALE).astype(jnp.bfloat16)
                acc[...] += jnp.dot(
                    part, va[pl.ds(at, BQ), :], preferred_element_type=jnp.float32
                )

            return carry

        lax.fori_loop(0, qi, body, 0)
        kept = qa[:, HD:].astype(jnp.float32)
        shift_kept = jnp.sum(jnp.where(lane == SEGS, kept, 0.0), axis=1, keepdims=True)
        put(o_ref, acc[:, :HD], jnp.where(lane == 1, shift_kept, acc[:, HD:]))

    run(ceiling(q_rows, top[0:1, 0:1]))

    @pl.when(jnp.min(acc[:, HD:]) < TINY)
    def _():
        qa[:, HD:] = side.astype(jnp.bfloat16)
        most = jnp.max(
            jnp.where(ahead, BARRED, score(qa, ka, here, BQ)), axis=1, keepdims=True
        )

        def body(kj, most):
            part = score(qa, ka, pl.multiple_of(kj * BQ, BQ), BQ)
            return jnp.maximum(most, jnp.max(part, axis=1, keepdims=True))

        run(lax.fori_loop(0, qi, body, most))


def pack_part(core, seen, arrived, other, q_side, k_side):
    pack = arrived.shape[0]
    once = dict(pipeline_mode=pl.Buffered(1))
    return pl.pallas_call(
        pack_kernel,
        out_shape=jax.ShapeDtypeStruct((2, pack, 2 * HD), jnp.float32),
        grid_spec=pltpu.PrefetchScalarGridSpec(
            num_scalar_prefetch=2,
            grid=(pack // BQ,),
            in_specs=[
                pl.BlockSpec((BQ, 2 * HD), lambda i, *_: (i, 0)),
                pl.BlockSpec((pack, HD), lambda i, *_: (0, 2), **once),
                pl.BlockSpec((pack, HD), lambda i, *_: (0, 0), **once),
                pl.BlockSpec((BQ, HD), lambda i, *_: (i, 0)),
                pl.BlockSpec((pack, HD), lambda i, *_: (0, 0), **once),
            ],
            out_specs=pl.BlockSpec((2, BQ, 2 * HD), lambda i, *_: (0, i, 0)),
            scratch_shapes=[
                pltpu.VMEM((2 * BQ, 2 * HD), jnp.bfloat16),
                pltpu.VMEM((pack, 2 * HD), jnp.bfloat16),
                pltpu.VMEM((pack, 2 * HD), jnp.bfloat16),
                pltpu.VMEM((8, HD), jnp.float32),
                pltpu.VMEM((2 * BQ, 2 * HD), jnp.float32),
            ],
        ),
        compiler_params=pltpu.CompilerParams(vmem_limit_bytes=ROOM),
        cost_estimate=pl.CostEstimate(
            flops=8 * pack * pack * HD, bytes_accessed=8 << 20, transcendentals=pack * pack
        ),
        name="pack_part",
    )(core, seen, arrived, arrived, other, q_side, k_side)


def stem_kernel(core, q_ref, mine_ref, other_ref, part_ref, o_ref, qa, top, acc):
    stem = mine_ref.shape[0]
    heads, rows = part_ref.shape[:2]
    lane = lax.broadcasted_iota(jnp.int32, (1, HD), 1)
    first = core[0] == 0
    side = jnp.broadcast_to(jnp.where(lane == SEGS, -1.0, 0.0).astype(jnp.bfloat16), (CK, HD))
    ones = jnp.ones((CK, HD), jnp.bfloat16)

    def keys(at):
        here = pl.ds(at, CK)
        return jnp.where(first, mine_ref[here, :], other_ref[here, :])

    @pl.when(pl.program_id(0) == 0)
    def _():
        def body(step, most):
            wide = keys(pl.multiple_of(step * CK, CK)).astype(jnp.float32)
            norms = jnp.sum(wide * wide, axis=1, keepdims=True)
            return jnp.maximum(most, jnp.max(norms, axis=0, keepdims=True))

        most = lax.fori_loop(0, stem // CK, body, jnp.zeros((1, 1), jnp.float32))
        top[...] = jnp.broadcast_to(jnp.sqrt(most), (8, HD))

    q_rows = jnp.concatenate([q_ref[:, h * HD : h * HD + HD] for h in range(heads)], axis=0)
    qa[:, :HD] = q_rows

    def scores(at):
        wide = jnp.concatenate([keys(at), side], axis=1)
        return lax.dot_general(qa[...], wide, NT, preferred_element_type=jnp.float32)

    def run(shift):
        qa[:, HD:] = jnp.where(lane == SEGS, shift, 0.0).astype(jnp.bfloat16)
        total = None
        held = scores(0)
        for at in range(0, stem, CK):
            ahead = scores(at + CK) if at + CK < stem else None
            weights = jnp.exp2(held * SCALE).astype(jnp.bfloat16)
            here = pl.ds(at, CK)
            wide = jnp.where(first, other_ref[here, :], mine_ref[here, :])
            wide = jnp.concatenate([wide, ones], axis=1)
            part = jnp.dot(weights, wide, preferred_element_type=jnp.float32)
            total = part if total is None else total + part
            held = ahead
        acc[...] = total

    def finish():
        kept = qa[:, HD:].astype(jnp.float32)
        shift = jnp.sum(jnp.where(lane == SEGS, kept, 0.0), axis=1, keepdims=True)
        part = jnp.concatenate([part_ref[h] for h in range(heads)], axis=0)
        before = part[:, HD + 1 : HD + 2]
        most = jnp.maximum(shift, before)
        new = jnp.exp2((shift - most) * SCALE)
        old = jnp.exp2((before - most) * SCALE)
        total = acc[:, HD : HD + 1] * new + part[:, HD : HD + 1] * old
        mixed = (acc[:, :HD] * new + part[:, :HD] * old) / total
        for h in range(heads):
            o_ref[:, h * HD : h * HD + HD] = mixed[h * rows : h * rows + rows].astype(jnp.bfloat16)

    run(ceiling(q_rows, top[0:1, 0:1]))
    finish()

    @pl.when(jnp.min(acc[:, HD:]) < TINY)
    def _():
        qa[:, HD:] = jnp.zeros_like(q_rows)

        def body(step, most):
            part = scores(pl.multiple_of(step * CK, CK))
            return jnp.maximum(most, jnp.max(part, axis=1, keepdims=True))

        low = jnp.full((heads * rows, 1), BARRED, jnp.float32)
        run(lax.fori_loop(0, stem // CK, body, low))
        finish()


def stem_part(core, arrived, mine, other, before):
    pack = arrived.shape[0]
    stem = mine.shape[0]
    once = dict(pipeline_mode=pl.Buffered(1))
    return pl.pallas_call(
        stem_kernel,
        out_shape=jax.ShapeDtypeStruct((pack, 2 * HD), jnp.bfloat16),
        grid_spec=pltpu.PrefetchScalarGridSpec(
            num_scalar_prefetch=1,
            grid=(pack // BQ,),
            in_specs=[
                pl.BlockSpec((BQ, 2 * HD), lambda i, *_: (i, 0)),
                pl.BlockSpec((stem, HD), lambda i, *_: (0, 0), **once),
                pl.BlockSpec((stem, HD), lambda i, *_: (0, 0), **once),
                pl.BlockSpec((2, BQ, 2 * HD), lambda i, *_: (0, i, 0)),
            ],
            out_specs=pl.BlockSpec((BQ, 2 * HD), lambda i, *_: (i, 0)),
            scratch_shapes=[
                pltpu.VMEM((2 * BQ, 2 * HD), jnp.bfloat16),
                pltpu.VMEM((8, HD), jnp.float32),
                pltpu.VMEM((2 * BQ, 2 * HD), jnp.float32),
            ],
        ),
        compiler_params=pltpu.CompilerParams(vmem_limit_bytes=ROOM),
        cost_estimate=pl.CostEstimate(
            flops=8 * pack * stem * HD,
            bytes_accessed=8 << 20,
            transcendentals=2 * pack * stem,
        ),
        name="stem_part",
    )(core, arrived, mine, other, before)


def gather_kernel(core, mine_ref, other_ref, o_ref):
    first = core[0] == 0
    for e in range(mine_ref.shape[1]):
        mine = mine_ref[0, e]
        other = other_ref[e]
        at = 4 * HD * e
        o_ref[:, at : at + 2 * HD] = jnp.where(first, mine, other)
        o_ref[:, at + 2 * HD : at + 4 * HD] = jnp.where(first, other, mine)


def gather(core, mine, other):
    tok = mine.shape[2]
    heads = KVH // 2
    return pl.pallas_call(
        gather_kernel,
        out_shape=jax.ShapeDtypeStruct((tok, H * HD), jnp.bfloat16),
        grid_spec=pltpu.PrefetchScalarGridSpec(
            num_scalar_prefetch=1,
            grid=(2,),
            in_specs=[
                pl.BlockSpec((1, heads, tok, 2 * HD), lambda i, core: (core[0], i, 0, 0)),
                pl.BlockSpec((heads, tok, 2 * HD), lambda i, core: (i, 0, 0)),
            ],
            out_specs=pl.BlockSpec((tok, H * HD // 2), lambda i, core: (0, i)),
        ),
        name="gather",
    )(core, mine, other)


def shards(queries, keys, values, stem_kv, seg_ids, seg_parent, stem_owner):
    tok = queries.shape[1]
    x = lax.axis_index("x")
    core = lax.axis_index("core")
    spot = lax.axis_index(SEQ)
    pack_len = tok * 16
    core_row = core[None].astype(jnp.int32)
    here = jnp.stack([x, core]).astype(jnp.int32)

    raw = (queries[0], keys[0], values[0])
    rows = jnp.concatenate([seg_ids[0], seg_parent[0]])
    rows_mate = lax.ppermute(rows, "core", FLIP)
    raw_mate = tuple(lax.ppermute(part, "core", FLIP) for part in raw)

    stem = stem_kv[0]
    own = lax.dynamic_index_in_dim(stem, core, 0, keepdims=False)
    given = lax.dynamic_index_in_dim(stem, 1 - core, 0, keepdims=False)
    same = lax.ppermute(own, ("x", "core"), joint(0, 0))
    cross = lax.ppermute(given, ("x", "core"), joint(0, 1))
    flip = lax.ppermute(given, "core", FLIP)

    both = jnp.stack([rows, rows_mate])
    linked = jax.vmap(ancestry)(both[:, pack_len:])
    places = jax.vmap(token_places)(both[:, :pack_len], linked)
    places = lax.dynamic_slice_in_dim(places, spot * tok, tok, axis=1)
    angles = places[:, :, None] * rotary_table()[None, None, :]
    cosine, sine = jnp.cos(angles), jnp.sin(angles)
    sent = turn(
        here,
        raw,
        raw_mate,
        jnp.concatenate([cosine, cosine], axis=2),
        jnp.concatenate([-sine, sine], axis=2),
    )
    arrived = lax.all_to_all(
        sent.reshape(16, tok, 3 * HD), SEQ, split_axis=0, concat_axis=0, tiled=True
    ).reshape(pack_len, 3 * HD)
    same, cross, flip, sent = lax.optimization_barrier((same, cross, flip, sent))

    held = (own, same, flip, cross)
    wanted = moved(relay_kernel, stem.shape, (2,), (here, stem_owner), held)
    two = lax.ppermute(wanted, ("x", "core"), joint(1, 0))
    both, linked, _ = lax.optimization_barrier((both, linked, wanted))
    two, arrived = lax.optimization_barrier((two, arrived))
    pair = lax.ppermute(arrived[:, 2 * HD :], "core", FLIP)

    ours = spot // KVH == core
    seg_row = jnp.where(ours, both[0, :pack_len], both[1, :pack_len])
    reach = jnp.where(ours, linked[0], linked[1])
    onehot = (seg_row[:, None] == jnp.arange(HD, dtype=jnp.int32)[None, :]).astype(jnp.float32)
    barred = jnp.pad(BARRED * (1.0 - reach), ((0, HD - SEGS), (0, HD - SEGS)))
    q_side = jnp.dot(onehot, barred, precision=lax.Precision.HIGHEST).astype(jnp.bfloat16)
    k_side = jnp.where(jnp.arange(HD)[None, :] == SEGS, -1.0, onehot).astype(jnp.bfloat16)
    q_has = onehot.reshape(pack_len // BQ, BQ, HD).max(axis=1)[:, :SEGS]
    seen = (q_has @ reach @ q_has.T > 0.5).astype(jnp.int32)

    stems = moved(
        settle_kernel,
        (2, KVH, stem.shape[1], HD),
        (2, KVH),
        (here, stem_owner),
        held + (two,),
    ).reshape(16, stem.shape[1], HD)
    mine = lax.all_to_all(stems, SEQ, split_axis=0, concat_axis=0, tiled=True).reshape(STEM, HD)
    arrived, pair, _ = lax.optimization_barrier((arrived, pair, stems))
    partial = pack_part(core_row, seen, arrived, pair, q_side, k_side)
    mine, partial = lax.optimization_barrier((mine, partial))
    other = lax.ppermute(mine, "core", FLIP)
    mixed = stem_part(core_row, arrived, mine, other, partial)

    back = lax.all_to_all(
        mixed.reshape(16, tok, 2 * HD), SEQ, split_axis=0, concat_axis=0, tiled=True
    ).reshape(2, KVH, tok, 2 * HD)
    away = lax.dynamic_index_in_dim(back, 1 - core, 0, keepdims=False)
    return gather(core_row, back, lax.ppermute(away, "core", FLIP))[None]


def solution(mesh):
    grid = Mesh(mesh.devices.reshape(4, 2, 4, 4), ("x", "core", "z", "y"))
    dp, seq = ("x", "core"), SEQ
    placed = (
        P(dp, seq, None),
        P(dp, seq, None),
        P(dp, seq, None),
        P(dp, None, seq, None),
        P(dp, None),
        P(dp, None),
        P(),
    )
    return jax.shard_map(
        shards, mesh=grid, in_specs=placed, out_specs=P(dp, seq, None), check_vma=False
    )
```

```python
import math

import jax
import jax.numpy as jnp
import numpy as np
from jax import lax
from jax.experimental import pallas as pl
from jax.experimental.pallas import tpu as pltpu
from jax.sharding import Mesh
from jax.sharding import PartitionSpec as P

H = 32
KVH = 8
HD = 128
STEM = 4096
SEGS = 16
BARRED = -1e30
BQ = 512
CK = 256
WIDE = 1024
SCALE = HD**-0.5 * math.log2(math.e)
SHIFT = 70.0 / SCALE
TINY = 2.0**-16
FLIP = [(0, 1), (1, 0)]
NEAR = [(0, 1), (1, 0), (2, 3), (3, 2)]
FAR = [(0, 3), (3, 0), (1, 2), (2, 1)]
SEQ = ("z", "y")


def joint(step, crossed):
    keys, values = (NEAR, FAR) if step == 0 else (FAR, NEAR)
    return [(2 * i + crossed, 2 * j) for i, j in keys] + [
        (2 * i + 1 - crossed, 2 * j + 1) for i, j in values
    ]


NT = (((1,), (1,)), ((), ()))
ROOM = 56 * 1024 * 1024


def rotary_table():
    halves = np.arange(0, HD, 2) / HD
    inverse = 1.0 / 500000.0**halves
    wavelen = 2.0 * np.pi / inverse
    smooth = (8192.0 / wavelen - 1.0) / 3.0
    blended = (1.0 - smooth) * inverse / 8.0 + smooth * inverse
    scaled = np.where(wavelen < 2048.0, inverse, np.where(wavelen > 8192.0, inverse / 8.0, blended))
    return jnp.asarray(scaled, dtype=jnp.float32)


def ancestry(parents):
    seg_count = parents.shape[0]
    indices = jnp.arange(seg_count, dtype=jnp.int32)
    linked = (
        (indices[:, None] == indices[None, :]) | (parents[:, None] == indices[None, :])
    ).astype(jnp.float32)
    for sweep in range(max(1, (seg_count - 1).bit_length())):
        linked = (
            jnp.dot(
                linked, linked, precision=lax.Precision.HIGHEST, preferred_element_type=jnp.float32
            )
            > 0.5
        ).astype(jnp.float32)
    return linked


def token_places(seg_row, linked):
    seg_count = linked.shape[0]
    onehot = (seg_row[:, None] == jnp.arange(seg_count, dtype=jnp.int32)[None, :]).astype(
        jnp.float32
    )
    lengths = jnp.sum(onehot, axis=0)
    starts = jnp.cumsum(lengths) - lengths
    before = jnp.sum(linked * lengths[None, :], axis=1) - lengths
    token_ids = jnp.arange(seg_row.shape[0], dtype=jnp.int32).astype(jnp.float32)
    return (
        STEM
        + token_ids
        - jnp.sum(onehot * starts[None, :], axis=1)
        + jnp.sum(onehot * before[None, :], axis=1)
    )


def turn_kernel(
    spot, q_own, k_own, v_own, q_mate, k_mate, v_mate, cos_ref, sin_ref, o_ref
):
    core = spot[1]
    pack = pl.program_id(0)

    def run(place, q_ref, k_ref, v_ref):
        cosine = cos_ref[place]
        sine = sin_ref[place]

        def turned(part):
            wide = part.astype(jnp.float32)
            return (wide * cosine + pltpu.roll(wide, HD // 2, 1) * sine).astype(jnp.bfloat16)

        for e in range(KVH):
            for head in range(2):
                at = pl.multiple_of((4 * e + head + 2 * core) * HD, HD)
                o_ref[0, e, :, head * HD : head * HD + HD] = turned(q_ref[:, pl.ds(at, HD)])
            at = e * HD
            o_ref[0, e, :, 2 * HD :] = jnp.where(
                core == 0, turned(k_ref[:, at : at + HD]), v_ref[:, at : at + HD]
            )

    @pl.when(pack == core)
    def _():
        run(0, q_own, k_own, v_own)

    @pl.when(pack != core)
    def _():
        run(1, q_mate, k_mate, v_mate)


def turn(here, own, mate, cosine, sine):
    tok = own[0].shape[0]
    whole = [
        pl.BlockSpec(part.shape, lambda i, here: (0, 0), pipeline_mode=pl.Buffered(1))
        for part in own + mate
    ]
    table = pl.BlockSpec(cosine.shape, lambda i, here: (0, 0, 0), pipeline_mode=pl.Buffered(1))
    return pl.pallas_call(
        turn_kernel,
        out_shape=jax.ShapeDtypeStruct((2, KVH, tok, 3 * HD), jnp.bfloat16),
        grid_spec=pltpu.PrefetchScalarGridSpec(
            num_scalar_prefetch=1,
            grid=(2,),
            in_specs=whole + [table, table],
            out_specs=pl.BlockSpec((1, KVH, tok, 3 * HD), lambda i, here: (i, 0, 0, 0)),
        ),
        compiler_params=pltpu.CompilerParams(vmem_limit_bytes=32 * 1024 * 1024),
        name="turn",
    )(here, *own, *mate, cosine, sine)


def held_at(x, core, group):
    chip = lax.div(group, 2)
    other = jnp.where(core == 0, near_of(x), far_of(x))
    found = jnp.where(lax.rem(group, 2) == core, 0, 2) + jnp.where(chip == x, 0, 1)
    return jnp.where((chip == x) | (chip == other), found, 4)


def near_of(x):
    return x + 1 - 2 * lax.rem(x, 2)


def far_of(x):
    return 3 - x


def relay_kernel(spot, owner, own, same, flip, cross, out, sems):
    x, core = spot[0], spot[1]
    to = jnp.where(core == 0, far_of(x), near_of(x))
    for item in range(2):
        code = held_at(x, core, owner[2 * to + item])
        for place, source in enumerate((own, same, flip, cross)):
            chosen = code == place if place else (code == 0) | (code == 4)

            @pl.when(chosen)
            def _(source=source):
                pltpu.make_async_copy(source, out.at[item], sems.at[item]).start()

    for item in range(2):
        pltpu.make_async_copy(own, out.at[item], sems.at[item]).wait()


def settle_kernel(spot, owner, own, same, flip, cross, two, out, sems):
    x, core = spot[0], spot[1]
    for pack in range(2):
        code = held_at(x, core, owner[2 * x + pack])
        for place, source in enumerate((own, same, flip, cross, two.at[pack])):

            @pl.when(code == place)
            def _(source=source):
                for e in range(KVH):
                    pltpu.make_async_copy(
                        source.at[:, pl.ds(e * HD, HD)], out.at[pack, e], sems.at[pack, e]
                    ).start()

    for pack in range(2):
        for e in range(KVH):
            pltpu.make_async_copy(
                own.at[:, pl.ds(0, HD)], out.at[pack, e], sems.at[pack, e]
            ).wait()


def moved(kernel, shape, sems, scalars, arrays):
    return pl.pallas_call(
        kernel,
        out_shape=jax.ShapeDtypeStruct(shape, jnp.bfloat16),
        grid_spec=pltpu.PrefetchScalarGridSpec(
            num_scalar_prefetch=len(scalars),
            grid=(1,),
            in_specs=[pl.BlockSpec(memory_space=pl.ANY)] * len(arrays),
            out_specs=pl.BlockSpec(shape, lambda *_: (0,) * len(shape)),
            scratch_shapes=[pltpu.SemaphoreType.DMA(sems)],
        ),
        name=kernel.__name__,
    )(*scalars, *arrays)


def flipped_dot(left, right):
    return lax.dot_general(left, right, NT, preferred_element_type=jnp.float32)


def fill(core, mine_ref, other_ref, ka, vt, top):
    first = core == 0
    best = jnp.zeros((8, BQ), jnp.float32)
    for at in range(0, mine_ref.shape[0], BQ):
        mine = mine_ref[at : at + BQ, :]
        other = other_ref[at : at + BQ, :]
        key = jnp.where(first, mine, other)
        ka[at : at + BQ, :HD] = key
        vt[:HD, at : at + BQ] = jnp.where(first, other, mine).T
        wide = key.astype(jnp.float32)
        squares = (wide * wide).astype(jnp.bfloat16)
        best = jnp.maximum(best, flipped_dot(jnp.ones((8, HD), jnp.bfloat16), squares))
    vt[HD:, :] = jnp.ones_like(vt[HD:, :])
    longest = jnp.max(jnp.max(best, axis=1, keepdims=True), axis=0, keepdims=True)
    top[...] = jnp.broadcast_to(jnp.sqrt(longest), (8, HD))


def stacked(ref):
    return jnp.concatenate([ref[:, :HD], ref[:, HD : 2 * HD]], axis=0)


def ceiling(rows, top):
    wide = rows.astype(jnp.float32)
    squares = (wide * wide).astype(jnp.bfloat16)
    norms = jnp.dot(squares, jnp.ones((HD, HD), jnp.bfloat16), preferred_element_type=jnp.float32)
    return jnp.sqrt(norms) * top * 1.02 - SHIFT


def shift_row(qa):
    pick = lax.broadcasted_iota(jnp.int32, (8, 2 * HD), 1) == HD + SEGS
    return flipped_dot(pick.astype(jnp.float32).astype(jnp.bfloat16), qa[...])


def down(row):
    return jnp.broadcast_to(row, (HD, row.shape[1])).T


def pack_kernel(
    core, seen, q_ref, mine_ref, other_ref, qb_ref, kb_ref, o_ref, qa, ka, vt, top, acc
):
    qi = pl.program_id(0)
    rows = 2 * BQ
    lane = lax.broadcasted_iota(jnp.int32, (1, HD), 1)

    @pl.when(qi == 0)
    def _():
        fill(core[0], mine_ref, other_ref, ka, vt, top)
        ka[:, HD:] = kb_ref[...]

    q_rows = stacked(q_ref)
    qa[:, :HD] = q_rows
    side = jnp.concatenate([qb_ref[...], qb_ref[...]], axis=0).astype(jnp.float32)
    query = lax.broadcasted_iota(jnp.int32, (BQ, rows), 1)
    ahead = lax.broadcasted_iota(jnp.int32, (BQ, rows), 0) > jnp.where(
        query >= BQ, query - BQ, query
    )
    here = pl.multiple_of(qi * BQ, BQ)

    def scores(at):
        return flipped_dot(ka[pl.ds(at, BQ), :], qa[...])

    def mixed(at, weights):
        return jnp.dot(
            vt[:, pl.ds(at, BQ)],
            weights.astype(jnp.bfloat16),
            preferred_element_type=jnp.float32,
        )

    def run(shift):
        qa[:, HD:] = jnp.where(lane == SEGS, shift, side).astype(jnp.bfloat16)
        acc[...] = mixed(here, jnp.where(ahead, 0.0, jnp.exp2(scores(here) * SCALE)))

        def body(kj, carry):
            @pl.when(seen[qi, kj] > 0)
            def _():
                at = pl.multiple_of(kj * BQ, BQ)
                acc[...] += mixed(at, jnp.exp2(scores(at) * SCALE))

            return carry

        lax.fori_loop(0, qi, body, 0)
        o_ref[0, : HD + 8] = acc[...]
        o_ref[0, HD + 8 :] = shift_row(qa)

    run(ceiling(q_rows, top[0:1, 0:1]))

    @pl.when(jnp.min(acc[HD:, :]) < TINY)
    def _():
        qa[:, HD:] = side.astype(jnp.bfloat16)
        most = jnp.max(jnp.where(ahead, BARRED, scores(here)), axis=0, keepdims=True)

        def body(kj, most):
            part = scores(pl.multiple_of(kj * BQ, BQ))
            return jnp.maximum(most, jnp.max(part, axis=0, keepdims=True))

        run(down(lax.fori_loop(0, qi, body, most)))


def pack_part(core, seen, arrived, other, q_side, k_side):
    pack = arrived.shape[0]
    once = dict(pipeline_mode=pl.Buffered(1))
    return pl.pallas_call(
        pack_kernel,
        out_shape=jax.ShapeDtypeStruct((pack // BQ, HD + 16, 2 * BQ), jnp.float32),
        grid_spec=pltpu.PrefetchScalarGridSpec(
            num_scalar_prefetch=2,
            grid=(pack // BQ,),
            in_specs=[
                pl.BlockSpec((BQ, 2 * HD), lambda i, *_: (i, 0)),
                pl.BlockSpec((pack, HD), lambda i, *_: (0, 2), **once),
                pl.BlockSpec((pack, HD), lambda i, *_: (0, 0), **once),
                pl.BlockSpec((BQ, HD), lambda i, *_: (i, 0)),
                pl.BlockSpec((pack, HD), lambda i, *_: (0, 0), **once),
            ],
            out_specs=pl.BlockSpec((1, HD + 16, 2 * BQ), lambda i, *_: (i, 0, 0)),
            scratch_shapes=[
                pltpu.VMEM((2 * BQ, 2 * HD), jnp.bfloat16),
                pltpu.VMEM((pack, 2 * HD), jnp.bfloat16),
                pltpu.VMEM((HD + 8, pack), jnp.bfloat16),
                pltpu.VMEM((8, HD), jnp.float32),
                pltpu.VMEM((HD + 8, 2 * BQ), jnp.float32),
            ],
        ),
        compiler_params=pltpu.CompilerParams(vmem_limit_bytes=ROOM),
        cost_estimate=pl.CostEstimate(
            flops=8 * pack * pack * HD, bytes_accessed=8 << 20, transcendentals=pack * pack
        ),
        name="pack_part",
    )(core, seen, arrived, arrived, other, q_side, k_side)


def stem_kernel(core, q_ref, mine_ref, other_ref, part_ref, o_ref, qa, ka, vt, top, acc):
    stem = ka.shape[0]
    lane = lax.broadcasted_iota(jnp.int32, (1, HD), 1)
    side = jnp.broadcast_to(jnp.where(lane == SEGS, -1.0, 0.0).astype(jnp.bfloat16), (CK, HD))

    @pl.when(pl.program_id(0) == 0)
    def _():
        fill(core[0], mine_ref, other_ref, ka, vt, top)

    q_rows = stacked(q_ref)
    qa[:, :HD] = q_rows

    def scores(at):
        return flipped_dot(jnp.concatenate([ka[pl.ds(at, CK), :], side], axis=1), qa[...])

    def run(shift):
        qa[:, HD:] = jnp.where(lane == SEGS, shift, 0.0).astype(jnp.bfloat16)
        total, weights = None, []
        held = scores(0)
        for at in range(0, stem, CK):
            ahead = scores(at + CK) if at + CK < stem else None
            weights.append(jnp.exp2(held * SCALE).astype(jnp.bfloat16))
            if len(weights) * CK == WIDE:
                part = jnp.dot(
                    vt[:, at + CK - WIDE : at + CK],
                    jnp.concatenate(weights, axis=0),
                    preferred_element_type=jnp.float32,
                )
                total = part if total is None else total + part
                weights = []
            held = ahead
        acc[...] = total

    def finish():
        shift = shift_row(qa)[:1]
        before = part_ref[0, HD + 8 : HD + 9]
        most = jnp.maximum(shift, before)
        new = jnp.exp2((shift - most) * SCALE)
        old = jnp.exp2((before - most) * SCALE)
        total = acc[HD : HD + 1] * new + part_ref[0, HD : HD + 1] * old
        out = (acc[:HD] * (new / total) + part_ref[0, :HD] * (old / total)).T
        o_ref[:, :HD] = out[:BQ].astype(jnp.bfloat16)
        o_ref[:, HD:] = out[BQ:].astype(jnp.bfloat16)

    run(ceiling(q_rows, top[0:1, 0:1]))
    finish()

    @pl.when(jnp.min(acc[HD:, :]) < TINY)
    def _():
        qa[:, HD:] = jnp.zeros_like(q_rows)

        def body(step, most):
            part = scores(pl.multiple_of(step * CK, CK))
            return jnp.maximum(most, jnp.max(part, axis=0, keepdims=True))

        low = jnp.full((1, 2 * BQ), BARRED, jnp.float32)
        run(down(lax.fori_loop(0, stem // CK, body, low)))
        finish()


def stem_part(core, arrived, mine, other, before):
    pack = arrived.shape[0]
    stem = mine.shape[0]
    once = dict(pipeline_mode=pl.Buffered(1))
    return pl.pallas_call(
        stem_kernel,
        out_shape=jax.ShapeDtypeStruct((pack, 2 * HD), jnp.bfloat16),
        grid_spec=pltpu.PrefetchScalarGridSpec(
            num_scalar_prefetch=1,
            grid=(pack // BQ,),
            in_specs=[
                pl.BlockSpec((BQ, 2 * HD), lambda i, *_: (i, 0)),
                pl.BlockSpec((stem, HD), lambda i, *_: (0, 0), **once),
                pl.BlockSpec((stem, HD), lambda i, *_: (0, 0), **once),
                pl.BlockSpec((1, HD + 16, 2 * BQ), lambda i, *_: (i, 0, 0)),
            ],
            out_specs=pl.BlockSpec((BQ, 2 * HD), lambda i, *_: (i, 0)),
            scratch_shapes=[
                pltpu.VMEM((2 * BQ, 2 * HD), jnp.bfloat16),
                pltpu.VMEM((stem, HD), jnp.bfloat16),
                pltpu.VMEM((HD + 8, stem), jnp.bfloat16),
                pltpu.VMEM((8, HD), jnp.float32),
                pltpu.VMEM((HD + 8, 2 * BQ), jnp.float32),
            ],
        ),
        compiler_params=pltpu.CompilerParams(vmem_limit_bytes=ROOM),
        cost_estimate=pl.CostEstimate(
            flops=8 * pack * stem * HD, bytes_accessed=8 << 20, transcendentals=2 * pack * stem
        ),
        name="stem_part",
    )(core, arrived, mine, other, before)


def gather_kernel(core, mine_ref, other_ref, o_ref):
    first = core[0] == 0
    for e in range(mine_ref.shape[1]):
        mine = mine_ref[0, e]
        other = other_ref[e]
        at = 4 * HD * e
        o_ref[:, at : at + 2 * HD] = jnp.where(first, mine, other)
        o_ref[:, at + 2 * HD : at + 4 * HD] = jnp.where(first, other, mine)


def gather(core, mine, other):
    tok = mine.shape[2]
    heads = KVH // 2
    return pl.pallas_call(
        gather_kernel,
        out_shape=jax.ShapeDtypeStruct((tok, H * HD), jnp.bfloat16),
        grid_spec=pltpu.PrefetchScalarGridSpec(
            num_scalar_prefetch=1,
            grid=(2,),
            in_specs=[
                pl.BlockSpec((1, heads, tok, 2 * HD), lambda i, core: (core[0], i, 0, 0)),
                pl.BlockSpec((heads, tok, 2 * HD), lambda i, core: (i, 0, 0)),
            ],
            out_specs=pl.BlockSpec((tok, H * HD // 2), lambda i, core: (0, i)),
        ),
        name="gather",
    )(core, mine, other)


def shards(queries, keys, values, stem_kv, seg_ids, seg_parent, stem_owner):
    tok = queries.shape[1]
    x = lax.axis_index("x")
    core = lax.axis_index("core")
    spot = lax.axis_index(SEQ)
    pack_len = tok * 16
    core_row = core[None].astype(jnp.int32)
    here = jnp.stack([x, core]).astype(jnp.int32)

    raw = (queries[0], keys[0], values[0])
    rows = jnp.concatenate([seg_ids[0], seg_parent[0]])
    rows_mate = lax.ppermute(rows, "core", FLIP)
    raw_mate = tuple(lax.ppermute(part, "core", FLIP) for part in raw)

    stem = stem_kv[0]
    own = lax.dynamic_index_in_dim(stem, core, 0, keepdims=False)
    given = lax.dynamic_index_in_dim(stem, 1 - core, 0, keepdims=False)
    same = lax.ppermute(own, ("x", "core"), joint(0, 0))
    cross = lax.ppermute(given, ("x", "core"), joint(0, 1))
    flip = lax.ppermute(given, "core", FLIP)

    both = jnp.stack([rows, rows_mate])
    linked = jax.vmap(ancestry)(both[:, pack_len:])
    places = jax.vmap(token_places)(both[:, :pack_len], linked)
    places = lax.dynamic_slice_in_dim(places, spot * tok, tok, axis=1)
    angles = places[:, :, None] * rotary_table()[None, None, :]
    cosine, sine = jnp.cos(angles), jnp.sin(angles)
    sent = turn(
        here,
        raw,
        raw_mate,
        jnp.concatenate([cosine, cosine], axis=2),
        jnp.concatenate([-sine, sine], axis=2),
    )
    arrived = lax.all_to_all(
        sent.reshape(16, tok, 3 * HD), SEQ, split_axis=0, concat_axis=0, tiled=True
    ).reshape(pack_len, 3 * HD)
    same, cross, flip, sent = lax.optimization_barrier((same, cross, flip, sent))

    held = (own, same, flip, cross)
    wanted = moved(relay_kernel, stem.shape, (2,), (here, stem_owner), held)
    two = lax.ppermute(wanted, ("x", "core"), joint(1, 0))
    both, linked, _ = lax.optimization_barrier((both, linked, wanted))
    pair = lax.ppermute(arrived[:, 2 * HD :], "core", FLIP)

    ours = spot // KVH == core
    seg_row = jnp.where(ours, both[0, :pack_len], both[1, :pack_len])
    reach = jnp.where(ours, linked[0], linked[1])
    onehot = (seg_row[:, None] == jnp.arange(HD, dtype=jnp.int32)[None, :]).astype(jnp.float32)
    barred = jnp.pad(BARRED * (1.0 - reach), ((0, HD - SEGS), (0, HD - SEGS)))
    q_side = jnp.dot(onehot, barred, precision=lax.Precision.HIGHEST).astype(jnp.bfloat16)
    k_side = jnp.where(jnp.arange(HD)[None, :] == SEGS, -1.0, onehot).astype(jnp.bfloat16)
    q_has = onehot.reshape(pack_len // BQ, BQ, HD).max(axis=1)[:, :SEGS]
    seen = (q_has @ reach @ q_has.T > 0.5).astype(jnp.int32)

    stems = moved(
        settle_kernel,
        (2, KVH, stem.shape[1], HD),
        (2, KVH),
        (here, stem_owner),
        held + (two,),
    ).reshape(16, stem.shape[1], HD)
    mine = lax.all_to_all(stems, SEQ, split_axis=0, concat_axis=0, tiled=True).reshape(STEM, HD)
    arrived, pair, _ = lax.optimization_barrier((arrived, pair, stems))
    partial = pack_part(core_row, seen, arrived, pair, q_side, k_side)
    mine, partial = lax.optimization_barrier((mine, partial))
    other = lax.ppermute(mine, "core", FLIP)
    mixed = stem_part(core_row, arrived, mine, other, partial)

    back = lax.all_to_all(
        mixed.reshape(16, tok, 2 * HD), SEQ, split_axis=0, concat_axis=0, tiled=True
    ).reshape(2, KVH, tok, 2 * HD)
    away = lax.dynamic_index_in_dim(back, 1 - core, 0, keepdims=False)
    return gather(core_row, back, lax.ppermute(away, "core", FLIP))[None]


def solution(mesh):
    grid = Mesh(mesh.devices.reshape(4, 2, 4, 4), ("x", "core", "z", "y"))
    dp, seq = ("x", "core"), SEQ
    placed = (
        P(dp, seq, None),
        P(dp, seq, None),
        P(dp, seq, None),
        P(dp, None, seq, None),
        P(dp, None),
        P(dp, None),
        P(),
    )
    return jax.shard_map(
        shards, mesh=grid, in_specs=placed, out_specs=P(dp, seq, None), check_vma=False
    )
```

```python
import math

import jax
import jax.numpy as jnp
import numpy as np
from jax import lax
from jax.experimental import pallas as pl
from jax.experimental.pallas import tpu as pltpu
from jax.sharding import Mesh
from jax.sharding import PartitionSpec as P

H = 32
KVH = 8
HD = 128
STEM = 4096
SEGS = 16
BARRED = -1e30
BQ = 512
CK = 256
WIDE = 1024
SCALE = HD**-0.5 * math.log2(math.e)
SHIFT = 70.0 / SCALE
TINY = 2.0**-16
FLIP = [(0, 1), (1, 0)]
NEAR = [(0, 1), (1, 0), (2, 3), (3, 2)]
FAR = [(0, 3), (3, 0), (1, 2), (2, 1)]
SEQ = ("z", "y")


def joint(step, crossed):
    keys, values = (NEAR, FAR) if step == 0 else (FAR, NEAR)
    return [(2 * i + crossed, 2 * j) for i, j in keys] + [
        (2 * i + 1 - crossed, 2 * j + 1) for i, j in values
    ]


NT = (((1,), (1,)), ((), ()))
ROOM = 127 * 512 * 1024


def rotary_table():
    halves = np.arange(0, HD, 2) / HD
    inverse = 1.0 / 500000.0**halves
    wavelen = 2.0 * np.pi / inverse
    smooth = (8192.0 / wavelen - 1.0) / 3.0
    blended = (1.0 - smooth) * inverse / 8.0 + smooth * inverse
    scaled = np.where(wavelen < 2048.0, inverse, np.where(wavelen > 8192.0, inverse / 8.0, blended))
    return jnp.asarray(scaled, dtype=jnp.float32)


def ancestry(parents):
    seg_count = parents.shape[0]
    indices = jnp.arange(seg_count, dtype=jnp.int32)
    linked = (
        (indices[:, None] == indices[None, :]) | (parents[:, None] == indices[None, :])
    ).astype(jnp.float32)
    for sweep in range(max(1, (seg_count - 1).bit_length())):
        linked = (
            jnp.dot(
                linked, linked, precision=lax.Precision.HIGHEST, preferred_element_type=jnp.float32
            )
            > 0.5
        ).astype(jnp.float32)
    return linked


def token_places(seg_row, linked):
    seg_count = linked.shape[0]
    onehot = (seg_row[:, None] == jnp.arange(seg_count, dtype=jnp.int32)[None, :]).astype(
        jnp.float32
    )
    lengths = jnp.sum(onehot, axis=0)
    starts = jnp.cumsum(lengths) - lengths
    before = jnp.sum(linked * lengths[None, :], axis=1) - lengths
    token_ids = jnp.arange(seg_row.shape[0], dtype=jnp.int32).astype(jnp.float32)
    return (
        STEM
        + token_ids
        - jnp.sum(onehot * starts[None, :], axis=1)
        + jnp.sum(onehot * before[None, :], axis=1)
    )


def turn_kernel(
    spot, q_own, k_own, v_own, q_mate, k_mate, v_mate, cos_ref, sin_ref, o_ref
):
    core = spot[1]
    pack = pl.program_id(0)

    def run(place, q_ref, k_ref, v_ref):
        cosine = cos_ref[place]
        sine = sin_ref[place]

        def turned(part):
            wide = part.astype(jnp.float32)
            return (wide * cosine + pltpu.roll(wide, HD // 2, 1) * sine).astype(jnp.bfloat16)

        for e in range(KVH):
            for head in range(2):
                at = pl.multiple_of((4 * e + head + 2 * core) * HD, HD)
                o_ref[0, e, :, head * HD : head * HD + HD] = turned(q_ref[:, pl.ds(at, HD)])
            at = e * HD
            o_ref[0, e, :, 2 * HD :] = jnp.where(
                core == 0, turned(k_ref[:, at : at + HD]), v_ref[:, at : at + HD]
            )

    @pl.when(pack == core)
    def _():
        run(0, q_own, k_own, v_own)

    @pl.when(pack != core)
    def _():
        run(1, q_mate, k_mate, v_mate)


def turn(here, own, mate, cosine, sine):
    tok = own[0].shape[0]
    whole = [
        pl.BlockSpec(part.shape, lambda i, here: (0, 0), pipeline_mode=pl.Buffered(1))
        for part in own + mate
    ]
    table = pl.BlockSpec(cosine.shape, lambda i, here: (0, 0, 0), pipeline_mode=pl.Buffered(1))
    return pl.pallas_call(
        turn_kernel,
        out_shape=jax.ShapeDtypeStruct((2, KVH, tok, 3 * HD), jnp.bfloat16),
        grid_spec=pltpu.PrefetchScalarGridSpec(
            num_scalar_prefetch=1,
            grid=(2,),
            in_specs=whole + [table, table],
            out_specs=pl.BlockSpec((1, KVH, tok, 3 * HD), lambda i, here: (i, 0, 0, 0)),
        ),
        compiler_params=pltpu.CompilerParams(vmem_limit_bytes=32 * 1024 * 1024),
        name="turn",
    )(here, *own, *mate, cosine, sine)


def held_at(x, core, group):
    chip = lax.div(group, 2)
    other = jnp.where(core == 0, near_of(x), far_of(x))
    found = jnp.where(lax.rem(group, 2) == core, 0, 2) + jnp.where(chip == x, 0, 1)
    return jnp.where((chip == x) | (chip == other), found, 4)


def near_of(x):
    return x + 1 - 2 * lax.rem(x, 2)


def far_of(x):
    return 3 - x


def relay_kernel(spot, owner, own, same, flip, cross, out, hold, sems):
    x, core = spot[0], spot[1]
    to = jnp.where(core == 0, far_of(x), near_of(x))
    half = own.shape[0] // 2
    parts = [(item, pl.ds(side * half, half), 2 * item + side) for item in range(2) for side in range(2)]
    codes = [held_at(x, core, owner[2 * to + item]) for item in range(2)]
    for item, rows, place in parts:
        for at, source in enumerate((own, same, flip, cross)):
            chosen = codes[item] == at if at else (codes[item] == 0) | (codes[item] == 4)

            @pl.when(chosen)
            def _(source=source):
                pltpu.make_async_copy(source.at[rows], hold.at[item, rows], sems.at[0, place]).start()

    for item, rows, place in parts:
        pltpu.make_async_copy(own.at[rows], hold.at[item, rows], sems.at[0, place]).wait()
        pltpu.make_async_copy(hold.at[item, rows], out.at[item, rows], sems.at[1, place]).start()
    for item, rows, place in parts:
        pltpu.make_async_copy(hold.at[item, rows], out.at[item, rows], sems.at[1, place]).wait()


def settle_kernel(spot, owner, own, same, flip, cross, two, out, hold, sems):
    x, core = spot[0], spot[1]
    parts = [(pack, e) for pack in range(2) for e in range(KVH)]
    for pack in range(2):
        code = held_at(x, core, owner[2 * x + pack])
        for at, source in enumerate((own, same, flip, cross, two.at[pack])):

            @pl.when(code == at)
            def _(source=source):
                for e in range(KVH):
                    pltpu.make_async_copy(
                        source.at[:, pl.ds(e * HD, HD)], hold.at[pack, e], sems.at[0, pack, e]
                    ).start()

    for pack, e in parts:
        pltpu.make_async_copy(
            own.at[:, pl.ds(0, HD)], hold.at[pack, e], sems.at[0, pack, e]
        ).wait()
        pltpu.make_async_copy(hold.at[pack, e], out.at[pack, e], sems.at[1, pack, e]).start()
    for pack, e in parts:
        pltpu.make_async_copy(hold.at[pack, e], out.at[pack, e], sems.at[1, pack, e]).wait()


def moved(kernel, shape, sems, scalars, arrays):
    whole = pl.BlockSpec(memory_space=pl.ANY)
    return pl.pallas_call(
        kernel,
        out_shape=jax.ShapeDtypeStruct(shape, jnp.bfloat16),
        grid_spec=pltpu.PrefetchScalarGridSpec(
            num_scalar_prefetch=len(scalars),
            grid=(1,),
            in_specs=[whole] * len(arrays),
            out_specs=whole,
            scratch_shapes=[pltpu.VMEM(shape, jnp.bfloat16), pltpu.SemaphoreType.DMA(sems)],
        ),
        compiler_params=pltpu.CompilerParams(vmem_limit_bytes=ROOM),
        name=kernel.__name__,
    )(*scalars, *arrays)


def flipped_dot(left, right):
    return lax.dot_general(left, right, NT, preferred_element_type=jnp.float32)


def fill(core, mine_ref, other_ref, ka, vt, top):
    first = core == 0
    best = jnp.zeros((8, BQ), jnp.float32)
    for at in range(0, mine_ref.shape[0], BQ):
        mine = mine_ref[at : at + BQ, :]
        other = other_ref[at : at + BQ, :]
        key = jnp.where(first, mine, other)
        ka[at : at + BQ, :HD] = key
        vt[:HD, at : at + BQ] = jnp.where(first, other, mine).T
        wide = key.astype(jnp.float32)
        squares = (wide * wide).astype(jnp.bfloat16)
        best = jnp.maximum(best, flipped_dot(jnp.ones((8, HD), jnp.bfloat16), squares))
    vt[HD:, :] = jnp.ones_like(vt[HD:, :])
    longest = jnp.max(jnp.max(best, axis=1, keepdims=True), axis=0, keepdims=True)
    top[...] = jnp.broadcast_to(jnp.sqrt(longest), (8, HD))


def stacked(ref):
    return jnp.concatenate([ref[:, :HD], ref[:, HD : 2 * HD]], axis=0)


def ceiling(rows, top):
    wide = rows.astype(jnp.float32)
    squares = (wide * wide).astype(jnp.bfloat16)
    norms = jnp.dot(squares, jnp.ones((HD, HD), jnp.bfloat16), preferred_element_type=jnp.float32)
    return jnp.sqrt(norms) * top * 1.02 - SHIFT


def shift_row(qa):
    pick = lax.broadcasted_iota(jnp.int32, (8, 2 * HD), 1) == HD + SEGS
    return flipped_dot(pick.astype(jnp.float32).astype(jnp.bfloat16), qa[...])


def down(row):
    return jnp.broadcast_to(row, (HD, row.shape[1])).T


def pack_kernel(
    core, seen, q_ref, mine_ref, other_ref, qb_ref, kb_ref, o_ref, qa, ka, vt, top, acc
):
    qi = pl.program_id(0)
    rows = 2 * BQ
    lane = lax.broadcasted_iota(jnp.int32, (1, HD), 1)

    @pl.when(qi == 0)
    def _():
        fill(core[0], mine_ref, other_ref, ka, vt, top)
        ka[:, HD:] = kb_ref[...]

    q_rows = stacked(q_ref)
    qa[:, :HD] = q_rows
    side = jnp.concatenate([qb_ref[...], qb_ref[...]], axis=0).astype(jnp.float32)
    query = lax.broadcasted_iota(jnp.int32, (BQ, rows), 1)
    ahead = lax.broadcasted_iota(jnp.int32, (BQ, rows), 0) > jnp.where(
        query >= BQ, query - BQ, query
    )
    here = pl.multiple_of(qi * BQ, BQ)

    def scores(at):
        return flipped_dot(ka[pl.ds(at, BQ), :], qa[...])

    def mixed(at, weights):
        return jnp.dot(
            vt[:, pl.ds(at, BQ)],
            weights.astype(jnp.bfloat16),
            preferred_element_type=jnp.float32,
        )

    def run(shift):
        qa[:, HD:] = jnp.where(lane == SEGS, shift, side).astype(jnp.bfloat16)
        acc[...] = mixed(here, jnp.where(ahead, 0.0, jnp.exp2(scores(here) * SCALE)))

        def body(kj, carry):
            @pl.when(seen[qi, kj] > 0)
            def _():
                at = pl.multiple_of(kj * BQ, BQ)
                acc[...] += mixed(at, jnp.exp2(scores(at) * SCALE))

            return carry

        lax.fori_loop(0, qi, body, 0)
        o_ref[0, : HD + 8] = acc[...]
        o_ref[0, HD + 8 :] = shift_row(qa)

    run(ceiling(q_rows, top[0:1, 0:1]))

    @pl.when(jnp.min(acc[HD:, :]) < TINY)
    def _():
        qa[:, HD:] = side.astype(jnp.bfloat16)
        most = jnp.max(jnp.where(ahead, BARRED, scores(here)), axis=0, keepdims=True)

        def body(kj, most):
            part = scores(pl.multiple_of(kj * BQ, BQ))
            return jnp.maximum(most, jnp.max(part, axis=0, keepdims=True))

        run(down(lax.fori_loop(0, qi, body, most)))


def pack_part(core, seen, arrived, other, q_side, k_side):
    pack = arrived.shape[0]
    once = dict(pipeline_mode=pl.Buffered(1))
    return pl.pallas_call(
        pack_kernel,
        out_shape=jax.ShapeDtypeStruct((pack // BQ, HD + 16, 2 * BQ), jnp.float32),
        grid_spec=pltpu.PrefetchScalarGridSpec(
            num_scalar_prefetch=2,
            grid=(pack // BQ,),
            in_specs=[
                pl.BlockSpec((BQ, 2 * HD), lambda i, *_: (i, 0)),
                pl.BlockSpec((pack, HD), lambda i, *_: (0, 2), **once),
                pl.BlockSpec((pack, HD), lambda i, *_: (0, 0), **once),
                pl.BlockSpec((BQ, HD), lambda i, *_: (i, 0)),
                pl.BlockSpec((pack, HD), lambda i, *_: (0, 0), **once),
            ],
            out_specs=pl.BlockSpec((1, HD + 16, 2 * BQ), lambda i, *_: (i, 0, 0)),
            scratch_shapes=[
                pltpu.VMEM((2 * BQ, 2 * HD), jnp.bfloat16),
                pltpu.VMEM((pack, 2 * HD), jnp.bfloat16),
                pltpu.VMEM((HD + 8, pack), jnp.bfloat16),
                pltpu.VMEM((8, HD), jnp.float32),
                pltpu.VMEM((HD + 8, 2 * BQ), jnp.float32),
            ],
        ),
        compiler_params=pltpu.CompilerParams(vmem_limit_bytes=ROOM),
        cost_estimate=pl.CostEstimate(
            flops=8 * pack * pack * HD, bytes_accessed=8 << 20, transcendentals=pack * pack
        ),
        name="pack_part",
    )(core, seen, arrived, arrived, other, q_side, k_side)


def stem_kernel(core, q_ref, mine_ref, other_ref, part_ref, o_ref, qa, ka, vt, top, acc):
    stem = ka.shape[0]
    lane = lax.broadcasted_iota(jnp.int32, (1, HD), 1)
    side = jnp.broadcast_to(jnp.where(lane == SEGS, -1.0, 0.0).astype(jnp.bfloat16), (CK, HD))

    @pl.when(pl.program_id(0) == 0)
    def _():
        fill(core[0], mine_ref, other_ref, ka, vt, top)

    q_rows = stacked(q_ref)
    qa[:, :HD] = q_rows

    def scores(at):
        return flipped_dot(jnp.concatenate([ka[pl.ds(at, CK), :], side], axis=1), qa[...])

    def run(shift):
        qa[:, HD:] = jnp.where(lane == SEGS, shift, 0.0).astype(jnp.bfloat16)
        total, weights = None, []
        held = scores(0)
        for at in range(0, stem, CK):
            ahead = scores(at + CK) if at + CK < stem else None
            weights.append(jnp.exp2(held * SCALE).astype(jnp.bfloat16))
            if len(weights) * CK == WIDE:
                part = jnp.dot(
                    vt[:, at + CK - WIDE : at + CK],
                    jnp.concatenate(weights, axis=0),
                    preferred_element_type=jnp.float32,
                )
                total = part if total is None else total + part
                weights = []
            held = ahead
        acc[...] = total

    def finish():
        shift = shift_row(qa)[:1]
        before = part_ref[0, HD + 8 : HD + 9]
        most = jnp.maximum(shift, before)
        new = jnp.exp2((shift - most) * SCALE)
        old = jnp.exp2((before - most) * SCALE)
        total = acc[HD : HD + 1] * new + part_ref[0, HD : HD + 1] * old
        out = (acc[:HD] * (new / total) + part_ref[0, :HD] * (old / total)).T
        o_ref[:, :HD] = out[:BQ].astype(jnp.bfloat16)
        o_ref[:, HD:] = out[BQ:].astype(jnp.bfloat16)

    run(ceiling(q_rows, top[0:1, 0:1]))
    finish()

    @pl.when(jnp.min(acc[HD:, :]) < TINY)
    def _():
        qa[:, HD:] = jnp.zeros_like(q_rows)

        def body(step, most):
            part = scores(pl.multiple_of(step * CK, CK))
            return jnp.maximum(most, jnp.max(part, axis=0, keepdims=True))

        low = jnp.full((1, 2 * BQ), BARRED, jnp.float32)
        run(down(lax.fori_loop(0, stem // CK, body, low)))
        finish()


def stem_part(core, arrived, mine, other, before):
    pack = arrived.shape[0]
    stem = mine.shape[0]
    once = dict(pipeline_mode=pl.Buffered(1))
    return pl.pallas_call(
        stem_kernel,
        out_shape=jax.ShapeDtypeStruct((pack, 2 * HD), jnp.bfloat16),
        grid_spec=pltpu.PrefetchScalarGridSpec(
            num_scalar_prefetch=1,
            grid=(pack // BQ,),
            in_specs=[
                pl.BlockSpec((BQ, 2 * HD), lambda i, *_: (i, 0)),
                pl.BlockSpec((stem, HD), lambda i, *_: (0, 0), **once),
                pl.BlockSpec((stem, HD), lambda i, *_: (0, 0), **once),
                pl.BlockSpec((1, HD + 16, 2 * BQ), lambda i, *_: (i, 0, 0)),
            ],
            out_specs=pl.BlockSpec((BQ, 2 * HD), lambda i, *_: (i, 0)),
            scratch_shapes=[
                pltpu.VMEM((2 * BQ, 2 * HD), jnp.bfloat16),
                pltpu.VMEM((stem, HD), jnp.bfloat16),
                pltpu.VMEM((HD + 8, stem), jnp.bfloat16),
                pltpu.VMEM((8, HD), jnp.float32),
                pltpu.VMEM((HD + 8, 2 * BQ), jnp.float32),
            ],
        ),
        compiler_params=pltpu.CompilerParams(vmem_limit_bytes=ROOM),
        cost_estimate=pl.CostEstimate(
            flops=8 * pack * stem * HD, bytes_accessed=8 << 20, transcendentals=2 * pack * stem
        ),
        name="stem_part",
    )(core, arrived, mine, other, before)


def gather_kernel(core, mine_ref, other_ref, o_ref):
    first = core[0] == 0
    for e in range(mine_ref.shape[1]):
        mine = mine_ref[0, e]
        other = other_ref[e]
        at = 4 * HD * e
        o_ref[:, at : at + 2 * HD] = jnp.where(first, mine, other)
        o_ref[:, at + 2 * HD : at + 4 * HD] = jnp.where(first, other, mine)


def gather(core, mine, other):
    tok = mine.shape[2]
    heads = KVH // 2
    return pl.pallas_call(
        gather_kernel,
        out_shape=jax.ShapeDtypeStruct((tok, H * HD), jnp.bfloat16),
        grid_spec=pltpu.PrefetchScalarGridSpec(
            num_scalar_prefetch=1,
            grid=(2,),
            in_specs=[
                pl.BlockSpec((1, heads, tok, 2 * HD), lambda i, core: (core[0], i, 0, 0)),
                pl.BlockSpec((heads, tok, 2 * HD), lambda i, core: (i, 0, 0)),
            ],
            out_specs=pl.BlockSpec((tok, H * HD // 2), lambda i, core: (0, i)),
        ),
        compiler_params=pltpu.CompilerParams(vmem_limit_bytes=ROOM),
        name="gather",
    )(core, mine, other)


def shards(queries, keys, values, stem_kv, seg_ids, seg_parent, stem_owner):
    tok = queries.shape[1]
    x = lax.axis_index("x")
    core = lax.axis_index("core")
    spot = lax.axis_index(SEQ)
    pack_len = tok * 16
    core_row = core[None].astype(jnp.int32)
    here = jnp.stack([x, core]).astype(jnp.int32)

    raw = (queries[0], keys[0], values[0])
    rows = jnp.concatenate([seg_ids[0], seg_parent[0]])
    rows_mate = lax.ppermute(rows, "core", FLIP)
    raw_mate = tuple(lax.ppermute(part, "core", FLIP) for part in raw)

    stem = stem_kv[0]
    own = lax.dynamic_index_in_dim(stem, core, 0, keepdims=False)
    given = lax.dynamic_index_in_dim(stem, 1 - core, 0, keepdims=False)
    same = lax.ppermute(own, ("x", "core"), joint(0, 0))
    cross = lax.ppermute(given, ("x", "core"), joint(0, 1))
    flip = lax.ppermute(given, "core", FLIP)

    both = jnp.stack([rows, rows_mate])
    linked = jax.vmap(ancestry)(both[:, pack_len:])
    places = jax.vmap(token_places)(both[:, :pack_len], linked)
    places = lax.dynamic_slice_in_dim(places, spot * tok, tok, axis=1)
    angles = places[:, :, None] * rotary_table()[None, None, :]
    cosine, sine = jnp.cos(angles), jnp.sin(angles)
    sent = turn(
        here,
        raw,
        raw_mate,
        jnp.concatenate([cosine, cosine], axis=2),
        jnp.concatenate([-sine, sine], axis=2),
    )
    arrived = lax.all_to_all(
        sent.reshape(16, tok, 3 * HD), SEQ, split_axis=0, concat_axis=0, tiled=True
    ).reshape(pack_len, 3 * HD)
    same, cross, flip, sent = lax.optimization_barrier((same, cross, flip, sent))

    held = (own, same, flip, cross)
    wanted = moved(relay_kernel, stem.shape, (2, 4), (here, stem_owner), held)
    two = lax.ppermute(wanted, ("x", "core"), joint(1, 0))
    both, linked, _ = lax.optimization_barrier((both, linked, wanted))
    pair = lax.ppermute(arrived[:, 2 * HD :], "core", FLIP)

    ours = spot // KVH == core
    seg_row = jnp.where(ours, both[0, :pack_len], both[1, :pack_len])
    reach = jnp.where(ours, linked[0], linked[1])
    onehot = (seg_row[:, None] == jnp.arange(HD, dtype=jnp.int32)[None, :]).astype(jnp.float32)
    barred = jnp.pad(BARRED * (1.0 - reach), ((0, HD - SEGS), (0, HD - SEGS)))
    q_side = jnp.dot(onehot, barred, precision=lax.Precision.HIGHEST).astype(jnp.bfloat16)
    k_side = jnp.where(jnp.arange(HD)[None, :] == SEGS, -1.0, onehot).astype(jnp.bfloat16)
    q_has = onehot.reshape(pack_len // BQ, BQ, HD).max(axis=1)[:, :SEGS]
    seen = (q_has @ reach @ q_has.T > 0.5).astype(jnp.int32)

    stems = moved(
        settle_kernel,
        (2, KVH, stem.shape[1], HD),
        (2, 2, KVH),
        (here, stem_owner),
        held + (two,),
    ).reshape(16, stem.shape[1], HD)
    mine = lax.all_to_all(stems, SEQ, split_axis=0, concat_axis=0, tiled=True).reshape(STEM, HD)
    arrived, pair, _ = lax.optimization_barrier((arrived, pair, stems))
    partial = pack_part(core_row, seen, arrived, pair, q_side, k_side)
    mine, partial = lax.optimization_barrier((mine, partial))
    other = lax.ppermute(mine, "core", FLIP)
    mixed = stem_part(core_row, arrived, mine, other, partial)

    back = lax.all_to_all(
        mixed.reshape(16, tok, 2 * HD), SEQ, split_axis=0, concat_axis=0, tiled=True
    ).reshape(2, KVH, tok, 2 * HD)
    away = lax.dynamic_index_in_dim(back, 1 - core, 0, keepdims=False)
    return gather(core_row, back, lax.ppermute(away, "core", FLIP))[None]


def solution(mesh):
    grid = Mesh(mesh.devices.reshape(4, 2, 4, 4), ("x", "core", "z", "y"))
    dp, seq = ("x", "core"), SEQ
    placed = (
        P(dp, seq, None),
        P(dp, seq, None),
        P(dp, seq, None),
        P(dp, None, seq, None),
        P(dp, None),
        P(dp, None),
        P(),
    )
    return jax.shard_map(
        shards, mesh=grid, in_specs=placed, out_specs=P(dp, seq, None), check_vma=False
    )
```

```python
import functools
import math

import jax
import jax.numpy as jnp
import numpy as np
from jax import lax
from jax.experimental import pallas as pl
from jax.experimental.pallas import tpu as pltpu
from jax.sharding import Mesh
from jax.sharding import PartitionSpec as P

H = 32
KVH = 8
HD = 128
STEM = 4096
SEGS = 16
BARRED = -1e30
BQ = 512
CK = 256
WIDE = 1024
SCALE = HD**-0.5 * math.log2(math.e)
SHIFT = 70.0 / SCALE
TINY = 2.0**-16
FLIP = [(0, 1), (1, 0)]
NEAR = [(0, 1), (1, 0), (2, 3), (3, 2)]
FAR = [(0, 3), (3, 0), (1, 2), (2, 1)]
SEQ = ("z", "y")


def joint(step, crossed):
    keys, values = (NEAR, FAR) if step == 0 else (FAR, NEAR)
    return [(2 * i + crossed, 2 * j) for i, j in keys] + [
        (2 * i + 1 - crossed, 2 * j + 1) for i, j in values
    ]


NT = (((1,), (1,)), ((), ()))
ROOM = 127 * 512 * 1024


def rotary_table():
    halves = np.arange(0, HD, 2) / HD
    inverse = 1.0 / 500000.0**halves
    wavelen = 2.0 * np.pi / inverse
    smooth = (8192.0 / wavelen - 1.0) / 3.0
    blended = (1.0 - smooth) * inverse / 8.0 + smooth * inverse
    scaled = np.where(wavelen < 2048.0, inverse, np.where(wavelen > 8192.0, inverse / 8.0, blended))
    return jnp.asarray(scaled, dtype=jnp.float32)


def ancestry(parents):
    seg_count = parents.shape[0]
    indices = jnp.arange(seg_count, dtype=jnp.int32)
    linked = (
        (indices[:, None] == indices[None, :]) | (parents[:, None] == indices[None, :])
    ).astype(jnp.float32)
    for sweep in range(max(1, (seg_count - 1).bit_length())):
        linked = (
            jnp.dot(
                linked, linked, precision=lax.Precision.HIGHEST, preferred_element_type=jnp.float32
            )
            > 0.5
        ).astype(jnp.float32)
    return linked


def token_places(seg_row, linked):
    seg_count = linked.shape[0]
    onehot = (seg_row[:, None] == jnp.arange(seg_count, dtype=jnp.int32)[None, :]).astype(
        jnp.float32
    )
    lengths = jnp.sum(onehot, axis=0)
    starts = jnp.cumsum(lengths) - lengths
    before = jnp.sum(linked * lengths[None, :], axis=1) - lengths
    token_ids = jnp.arange(seg_row.shape[0], dtype=jnp.int32).astype(jnp.float32)
    return (
        STEM
        + token_ids
        - jnp.sum(onehot * starts[None, :], axis=1)
        + jnp.sum(onehot * before[None, :], axis=1)
    )


def turn_kernel(
    spot, q_own, k_own, v_own, q_mate, k_mate, v_mate, cos_ref, sin_ref, o_ref
):
    core = spot[1]
    pack = pl.program_id(0)

    def run(place, q_ref, k_ref, v_ref):
        cosine = cos_ref[place]
        sine = sin_ref[place]

        def turned(part):
            wide = part.astype(jnp.float32)
            return (wide * cosine + pltpu.roll(wide, HD // 2, 1) * sine).astype(jnp.bfloat16)

        for e in range(KVH):
            for head in range(2):
                at = pl.multiple_of((4 * e + head + 2 * core) * HD, HD)
                o_ref[0, e, :, head * HD : head * HD + HD] = turned(q_ref[:, pl.ds(at, HD)])
            at = e * HD
            o_ref[0, e, :, 2 * HD :] = jnp.where(
                core == 0, turned(k_ref[:, at : at + HD]), v_ref[:, at : at + HD]
            )

    @pl.when(pack == core)
    def _():
        run(0, q_own, k_own, v_own)

    @pl.when(pack != core)
    def _():
        run(1, q_mate, k_mate, v_mate)


def turn(here, own, mate, cosine, sine):
    tok = own[0].shape[0]
    whole = [
        pl.BlockSpec(part.shape, lambda i, here: (0, 0), pipeline_mode=pl.Buffered(1))
        for part in own + mate
    ]
    table = pl.BlockSpec(cosine.shape, lambda i, here: (0, 0, 0), pipeline_mode=pl.Buffered(1))
    return pl.pallas_call(
        turn_kernel,
        out_shape=jax.ShapeDtypeStruct((2, KVH, tok, 3 * HD), jnp.bfloat16),
        grid_spec=pltpu.PrefetchScalarGridSpec(
            num_scalar_prefetch=1,
            grid=(2,),
            in_specs=whole + [table, table],
            out_specs=pl.BlockSpec((1, KVH, tok, 3 * HD), lambda i, here: (i, 0, 0, 0)),
        ),
        compiler_params=pltpu.CompilerParams(vmem_limit_bytes=32 * 1024 * 1024),
        name="turn",
    )(here, *own, *mate, cosine, sine)


def held_at(x, core, group):
    chip = lax.div(group, 2)
    other = jnp.where(core == 0, near_of(x), far_of(x))
    found = jnp.where(lax.rem(group, 2) == core, 0, 2) + jnp.where(chip == x, 0, 1)
    return jnp.where((chip == x) | (chip == other), found, 4)


def near_of(x):
    return x + 1 - 2 * lax.rem(x, 2)


def far_of(x):
    return 3 - x


def relay_kernel(spot, owner, own, same, flip, cross, out, hold, sems):
    x, core = spot[0], spot[1]
    to = jnp.where(core == 0, far_of(x), near_of(x))
    parts = [(item, side, 2 * item + side) for item in range(2) for side in range(2)]
    codes = [held_at(x, core, owner[2 * to + item]) for item in range(2)]
    for item, rows, place in parts:
        for at, source in enumerate((own, same, flip, cross)):
            chosen = codes[item] == at if at else (codes[item] == 0) | (codes[item] == 4)

            @pl.when(chosen)
            def _(source=source):
                pltpu.make_async_copy(source.at[rows], hold.at[item, rows], sems.at[0, place]).start()

    for item, rows, place in parts:
        pltpu.make_async_copy(own.at[rows], hold.at[item, rows], sems.at[0, place]).wait()
        pltpu.make_async_copy(hold.at[item, rows], out.at[item, rows], sems.at[1, place]).start()
    for item, rows, place in parts:
        pltpu.make_async_copy(hold.at[item, rows], out.at[item, rows], sems.at[1, place]).wait()


def settle_kernel(spot, owner, own, same, flip, cross, two, out, hold, sems):
    x, core = spot[0], spot[1]
    parts = [(pack, e) for pack in range(2) for e in range(KVH)]
    for pack in range(2):
        code = held_at(x, core, owner[2 * x + pack])
        for at, source in enumerate((own, same, flip, cross, two.at[pack])):

            @pl.when(code == at)
            def _(source=source):
                for e in range(KVH):
                    pltpu.make_async_copy(
                        source.at[:, :, pl.ds(e * HD, HD)], hold.at[pack, e], sems.at[0, pack, e]
                    ).start()

    for pack, e in parts:
        pltpu.make_async_copy(
            own.at[:, :, pl.ds(0, HD)], hold.at[pack, e], sems.at[0, pack, e]
        ).wait()
        pltpu.make_async_copy(hold.at[pack, e], out.at[pack, e], sems.at[1, pack, e]).start()
    for pack, e in parts:
        pltpu.make_async_copy(hold.at[pack, e], out.at[pack, e], sems.at[1, pack, e]).wait()


def moved(kernel, shape, sems, scalars, arrays):
    whole = pl.BlockSpec(memory_space=pl.ANY)
    return pl.pallas_call(
        kernel,
        out_shape=jax.ShapeDtypeStruct(shape, jnp.bfloat16),
        grid_spec=pltpu.PrefetchScalarGridSpec(
            num_scalar_prefetch=len(scalars),
            grid=(1,),
            in_specs=[whole] * len(arrays),
            out_specs=whole,
            scratch_shapes=[pltpu.VMEM(shape, jnp.bfloat16), pltpu.SemaphoreType.DMA(sems)],
        ),
        compiler_params=pltpu.CompilerParams(vmem_limit_bytes=ROOM),
        name=kernel.__name__,
    )(*scalars, *arrays)


def flipped_dot(left, right):
    return lax.dot_general(left, right, NT, preferred_element_type=jnp.float32)


def norms_of(key):
    wide = key.astype(jnp.float32)
    return flipped_dot(jnp.ones((8, HD), jnp.bfloat16), (wide * wide).astype(jnp.bfloat16))


def longest(best):
    most = jnp.max(jnp.max(best, axis=1, keepdims=True), axis=0, keepdims=True)
    return jnp.broadcast_to(jnp.sqrt(most), (8, HD))


def fill(core, mine_ref, other_ref, ka, vt, top):
    first = core == 0
    best = jnp.zeros((8, BQ), jnp.float32)
    for at in range(0, mine_ref.shape[0], BQ):
        mine = mine_ref[at : at + BQ, :]
        other = other_ref[at : at + BQ, :]
        key = jnp.where(first, mine, other)
        ka[at : at + BQ, :HD] = key
        vt[:HD, at : at + BQ] = jnp.where(first, other, mine).T
        best = jnp.maximum(best, norms_of(key))
    vt[HD:, :] = jnp.ones_like(vt[HD:, :])
    top[...] = longest(best)


def stacked(ref):
    return jnp.concatenate([ref[:, :HD], ref[:, HD : 2 * HD]], axis=0)


def ceiling(rows, top):
    wide = rows.astype(jnp.float32)
    squares = (wide * wide).astype(jnp.bfloat16)
    norms = jnp.dot(squares, jnp.ones((HD, HD), jnp.bfloat16), preferred_element_type=jnp.float32)
    return jnp.sqrt(norms) * top * 1.02 - SHIFT


def shift_row(qa):
    pick = lax.broadcasted_iota(jnp.int32, (8, 2 * HD), 1) == HD + SEGS
    return flipped_dot(pick.astype(jnp.float32).astype(jnp.bfloat16), qa[...])


def down(row):
    return jnp.broadcast_to(row, (HD, row.shape[1])).T


def pack_kernel(
    core, seen, q_ref, mine_ref, other_ref, qb_ref, kb_ref, o_ref, qa, ka, vt, top, acc
):
    qi = pl.program_id(0)
    rows = 2 * BQ
    lane = lax.broadcasted_iota(jnp.int32, (1, HD), 1)

    @pl.when(qi == 0)
    def _():
        fill(core[0], mine_ref, other_ref, ka, vt, top)
        ka[:, HD:] = kb_ref[...]

    q_rows = stacked(q_ref)
    qa[:, :HD] = q_rows
    side = jnp.concatenate([qb_ref[...], qb_ref[...]], axis=0).astype(jnp.float32)
    query = lax.broadcasted_iota(jnp.int32, (BQ, rows), 1)
    ahead = lax.broadcasted_iota(jnp.int32, (BQ, rows), 0) > jnp.where(
        query >= BQ, query - BQ, query
    )
    here = pl.multiple_of(qi * BQ, BQ)

    def scores(at):
        return flipped_dot(ka[pl.ds(at, BQ), :], qa[...])

    def mixed(at, weights):
        return jnp.dot(
            vt[:, pl.ds(at, BQ)],
            weights.astype(jnp.bfloat16),
            preferred_element_type=jnp.float32,
        )

    def run(shift):
        qa[:, HD:] = jnp.where(lane == SEGS, shift, side).astype(jnp.bfloat16)
        acc[...] = mixed(here, jnp.where(ahead, 0.0, jnp.exp2(scores(here) * SCALE)))

        def body(kj, carry):
            @pl.when(seen[qi, kj] > 0)
            def _():
                at = pl.multiple_of(kj * BQ, BQ)
                acc[...] += mixed(at, jnp.exp2(scores(at) * SCALE))

            return carry

        lax.fori_loop(0, qi, body, 0)
        o_ref[0, : HD + 8] = acc[...]
        o_ref[0, HD + 8 :] = shift_row(qa)

    run(ceiling(q_rows, top[0:1, 0:1]))

    @pl.when(jnp.min(acc[HD:, :]) < TINY)
    def _():
        qa[:, HD:] = side.astype(jnp.bfloat16)
        most = jnp.max(jnp.where(ahead, BARRED, scores(here)), axis=0, keepdims=True)

        def body(kj, most):
            part = scores(pl.multiple_of(kj * BQ, BQ))
            return jnp.maximum(most, jnp.max(part, axis=0, keepdims=True))

        run(down(lax.fori_loop(0, qi, body, most)))


def pack_part(core, seen, arrived, other, q_side, k_side):
    pack = arrived.shape[0]
    once = dict(pipeline_mode=pl.Buffered(1))
    return pl.pallas_call(
        pack_kernel,
        out_shape=jax.ShapeDtypeStruct((pack // BQ, HD + 16, 2 * BQ), jnp.float32),
        grid_spec=pltpu.PrefetchScalarGridSpec(
            num_scalar_prefetch=2,
            grid=(pack // BQ,),
            in_specs=[
                pl.BlockSpec((BQ, 2 * HD), lambda i, *_: (i, 0)),
                pl.BlockSpec((pack, HD), lambda i, *_: (0, 2), **once),
                pl.BlockSpec((pack, HD), lambda i, *_: (0, 0), **once),
                pl.BlockSpec((BQ, HD), lambda i, *_: (i, 0)),
                pl.BlockSpec((pack, HD), lambda i, *_: (0, 0), **once),
            ],
            out_specs=pl.BlockSpec((1, HD + 16, 2 * BQ), lambda i, *_: (i, 0, 0)),
            scratch_shapes=[
                pltpu.VMEM((2 * BQ, 2 * HD), jnp.bfloat16),
                pltpu.VMEM((pack, 2 * HD), jnp.bfloat16),
                pltpu.VMEM((HD + 8, pack), jnp.bfloat16),
                pltpu.VMEM((8, HD), jnp.float32),
                pltpu.VMEM((HD + 8, 2 * BQ), jnp.float32),
            ],
        ),
        compiler_params=pltpu.CompilerParams(vmem_limit_bytes=ROOM),
        cost_estimate=pl.CostEstimate(
            flops=8 * pack * pack * HD, bytes_accessed=8 << 20, transcendentals=pack * pack
        ),
        name="pack_part",
    )(core, seen, arrived, arrived, other, q_side, k_side)


def stem_kernel(last, q_ref, kv_ref, part_ref, o_ref, qa, ka, vt, top, acc):
    stem = ka.shape[0]
    lane = lax.broadcasted_iota(jnp.int32, (1, HD), 1)
    side = jnp.broadcast_to(jnp.where(lane == SEGS, -1.0, 0.0).astype(jnp.bfloat16), (CK, HD))

    @pl.when(pl.program_id(0) == 0)
    def _():
        owners, _, rows, _ = kv_ref.shape
        best = jnp.zeros((8, rows), jnp.float32)
        for owner in range(owners):
            here = slice(owner * rows, owner * rows + rows)
            key = kv_ref[owner, 0]
            ka[here, :] = key
            vt[:HD, here] = kv_ref[owner, 1].T
            best = jnp.maximum(best, norms_of(key))
        vt[HD:, :] = jnp.ones_like(vt[HD:, :])
        top[...] = longest(best)

    q_rows = stacked(q_ref)
    qa[:, :HD] = q_rows

    def scores(at):
        return flipped_dot(jnp.concatenate([ka[pl.ds(at, CK), :], side], axis=1), qa[...])

    def run(shift):
        qa[:, HD:] = jnp.where(lane == SEGS, shift, 0.0).astype(jnp.bfloat16)
        total, weights = None, []
        held = scores(0)
        for at in range(0, stem, CK):
            ahead = scores(at + CK) if at + CK < stem else None
            weights.append(jnp.exp2(held * SCALE).astype(jnp.bfloat16))
            if len(weights) * CK == WIDE:
                part = jnp.dot(
                    vt[:, at + CK - WIDE : at + CK],
                    jnp.concatenate(weights, axis=0),
                    preferred_element_type=jnp.float32,
                )
                total = part if total is None else total + part
                weights = []
            held = ahead
        acc[...] = total

    def finish():
        shift = shift_row(qa)[:1]
        before = part_ref[0, HD + 8 : HD + 9]
        most = jnp.maximum(shift, before)
        new = jnp.exp2((shift - most) * SCALE)
        old = jnp.exp2((before - most) * SCALE)
        if last:
            total = acc[HD : HD + 1] * new + part_ref[0, HD : HD + 1] * old
            out = (acc[:HD] * (new / total) + part_ref[0, :HD] * (old / total)).T
            o_ref[:, :HD] = out[:BQ].astype(jnp.bfloat16)
            o_ref[:, HD:] = out[BQ:].astype(jnp.bfloat16)
        else:
            o_ref[0, : HD + 8] = acc[...] * new + part_ref[0, : HD + 8] * old
            o_ref[0, HD + 8 :] = jnp.broadcast_to(most, (8, 2 * BQ))

    run(ceiling(q_rows, top[0:1, 0:1]))
    finish()

    @pl.when(jnp.min(acc[HD:, :]) < TINY)
    def _():
        qa[:, HD:] = jnp.zeros_like(q_rows)

        def body(step, most):
            part = scores(pl.multiple_of(step * CK, CK))
            return jnp.maximum(most, jnp.max(part, axis=0, keepdims=True))

        low = jnp.full((1, 2 * BQ), BARRED, jnp.float32)
        run(down(lax.fori_loop(0, stem // CK, body, low)))
        finish()


def stem_part(last, arrived, kv, before):
    pack = arrived.shape[0]
    stem = kv.shape[0] * kv.shape[2]
    part = pl.BlockSpec((1, HD + 16, 2 * BQ), lambda i: (i, 0, 0))
    rows = pl.BlockSpec((BQ, 2 * HD), lambda i: (i, 0))
    return pl.pallas_call(
        functools.partial(stem_kernel, last),
        out_shape=jax.ShapeDtypeStruct((pack, 2 * HD), jnp.bfloat16)
        if last
        else jax.ShapeDtypeStruct(before.shape, jnp.float32),
        grid=(pack // BQ,),
        in_specs=[
            rows,
            pl.BlockSpec(kv.shape, lambda i: (0, 0, 0, 0), pipeline_mode=pl.Buffered(1)),
            part,
        ],
        out_specs=rows if last else part,
        scratch_shapes=[
            pltpu.VMEM((2 * BQ, 2 * HD), jnp.bfloat16),
            pltpu.VMEM((stem, HD), jnp.bfloat16),
            pltpu.VMEM((HD + 8, stem), jnp.bfloat16),
            pltpu.VMEM((8, HD), jnp.float32),
            pltpu.VMEM((HD + 8, 2 * BQ), jnp.float32),
        ],
        compiler_params=pltpu.CompilerParams(vmem_limit_bytes=ROOM),
        cost_estimate=pl.CostEstimate(
            flops=8 * pack * stem * HD, bytes_accessed=8 << 20, transcendentals=2 * pack * stem
        ),
        name="stem_part",
    )(arrived, kv, before)


def gather_kernel(slot, part_ref, *rest):
    out, sems = rest[-2:]
    part = part_ref.at[0]
    spots = [
        out.at[:, pl.ds(pl.multiple_of((2 * e + slot[1]) * 2 * HD, 2 * HD), 2 * HD)]
        for e in range(KVH)
    ]
    for e, spot in enumerate(spots):
        pltpu.make_async_copy(part.at[e], spot, sems.at[e]).start()
    for e, spot in enumerate(spots):
        pltpu.make_async_copy(part.at[e], spot, sems.at[e]).wait()


def gather(slot, part, done=None):
    tok = part.shape[2]
    whole = pl.BlockSpec(memory_space=pl.ANY)
    return pl.pallas_call(
        gather_kernel,
        out_shape=jax.ShapeDtypeStruct((tok, H * HD), jnp.bfloat16),
        grid_spec=pltpu.PrefetchScalarGridSpec(
            num_scalar_prefetch=1,
            grid=(1,),
            in_specs=[
                pl.BlockSpec((1, KVH, tok, 2 * HD), lambda i, slot: (slot[0], 0, 0, 0)),
            ]
            + ([] if done is None else [whole]),
            out_specs=whole,
            scratch_shapes=[pltpu.SemaphoreType.DMA((KVH,))],
        ),
        input_output_aliases={} if done is None else {2: 0},
        name="gather",
    )(slot, part, *(() if done is None else (done,)))


def shards(queries, keys, values, stem_kv, seg_ids, seg_parent, stem_owner):
    tok = queries.shape[1]
    x = lax.axis_index("x")
    core = lax.axis_index("core")
    spot = lax.axis_index(SEQ)
    pack_len = tok * 16
    core_row = core[None].astype(jnp.int32)
    here = jnp.stack([x, core]).astype(jnp.int32)

    raw = (queries[0], keys[0], values[0])
    rows = jnp.concatenate([seg_ids[0], seg_parent[0]])
    rows_mate = lax.ppermute(rows, "core", FLIP)
    raw_mate = tuple(lax.ppermute(part, "core", FLIP) for part in raw)

    stem = stem_kv[0]
    half = stem.shape[1] // 2
    own = lax.dynamic_slice_in_dim(stem, core * half, half, axis=1)
    given = lax.dynamic_slice_in_dim(stem, (1 - core) * half, half, axis=1)
    same = lax.ppermute(own, ("x", "core"), joint(0, 0))
    cross = lax.ppermute(given, ("x", "core"), joint(0, 1))
    flip = lax.ppermute(given, "core", FLIP)

    both = jnp.stack([rows, rows_mate])
    linked = jax.vmap(ancestry)(both[:, pack_len:])
    places = jax.vmap(token_places)(both[:, :pack_len], linked)
    places = lax.dynamic_slice_in_dim(places, spot * tok, tok, axis=1)
    angles = places[:, :, None] * rotary_table()[None, None, :]
    cosine, sine = jnp.cos(angles), jnp.sin(angles)
    sent = turn(
        here,
        raw,
        raw_mate,
        jnp.concatenate([cosine, cosine], axis=2),
        jnp.concatenate([-sine, sine], axis=2),
    )
    arrived = lax.all_to_all(
        sent.reshape(16, tok, 3 * HD), SEQ, split_axis=0, concat_axis=0, tiled=True
    ).reshape(pack_len, 3 * HD)
    same, cross, flip, sent = lax.optimization_barrier((same, cross, flip, sent))

    held = (own, same, flip, cross)
    wanted = moved(relay_kernel, (2,) + own.shape, (2, 4), (here, stem_owner), held)
    two = lax.ppermute(wanted, ("x", "core"), joint(1, 0))
    both, linked, _ = lax.optimization_barrier((both, linked, wanted))
    pair = lax.ppermute(arrived[:, 2 * HD :], "core", FLIP)

    ours = spot // KVH == core
    seg_row = jnp.where(ours, both[0, :pack_len], both[1, :pack_len])
    reach = jnp.where(ours, linked[0], linked[1])
    onehot = (seg_row[:, None] == jnp.arange(HD, dtype=jnp.int32)[None, :]).astype(jnp.float32)
    barred = jnp.pad(BARRED * (1.0 - reach), ((0, HD - SEGS), (0, HD - SEGS)))
    q_side = jnp.dot(onehot, barred, precision=lax.Precision.HIGHEST).astype(jnp.bfloat16)
    k_side = jnp.where(jnp.arange(HD)[None, :] == SEGS, -1.0, onehot).astype(jnp.bfloat16)
    q_has = onehot.reshape(pack_len // BQ, BQ, HD).max(axis=1)[:, :SEGS]
    seen = (q_has @ reach @ q_has.T > 0.5).astype(jnp.int32)

    stems = moved(
        settle_kernel,
        (2, KVH, 2, half, HD),
        (2, 2, KVH),
        (here, stem_owner),
        held + (two,),
    ).reshape(16, 2, half, HD)
    mine = lax.all_to_all(stems, SEQ, split_axis=0, concat_axis=0, tiled=True)
    arrived, pair, _ = lax.optimization_barrier((arrived, pair, stems))
    partial = pack_part(core_row, seen, arrived, pair, q_side, k_side)
    mine, partial = lax.optimization_barrier((mine, partial))
    other = lax.ppermute(mine, "core", FLIP)
    partial = stem_part(False, arrived, mine, partial)
    mixed = stem_part(True, arrived, other, partial)

    back = lax.all_to_all(
        mixed.reshape(16, tok, 2 * HD), SEQ, split_axis=0, concat_axis=0, tiled=True
    ).reshape(2, KVH, tok, 2 * HD)
    away = lax.ppermute(lax.dynamic_slice_in_dim(back, 1 - core, 1), "core", FLIP)
    out = gather(jnp.stack([core, core]).astype(jnp.int32), back)
    return gather(jnp.stack([0 * core, 1 - core]).astype(jnp.int32), away, out)[None]


def solution(mesh):
    grid = Mesh(mesh.devices.reshape(4, 2, 4, 4), ("x", "core", "z", "y"))
    dp, seq = ("x", "core"), SEQ
    placed = (
        P(dp, seq, None),
        P(dp, seq, None),
        P(dp, seq, None),
        P(dp, None, seq, None),
        P(dp, None),
        P(dp, None),
        P(),
    )
    return jax.shard_map(
        shards, mesh=grid, in_specs=placed, out_specs=P(dp, seq, None), check_vma=False
    )
```

```python
import math

import jax
import jax.numpy as jnp
import numpy as np
from jax import lax
from jax.experimental import pallas as pl
from jax.experimental.pallas import tpu as pltpu
from jax.sharding import Mesh
from jax.sharding import PartitionSpec as P

H = 32
KVH = 8
HD = 128
STEM = 4096
SEGS = 16
BARRED = -1e30
BQ = 512
SPAN = 2
CK = 256
WIDE = 1024
SCALE = HD**-0.5 * math.log2(math.e)
SHIFT = 70.0 / SCALE
TINY = 2.0**-16
FLIP = [(0, 1), (1, 0)]
NEAR = [(0, 1), (1, 0), (2, 3), (3, 2)]
FAR = [(0, 3), (3, 0), (1, 2), (2, 1)]
SEQ = ("z", "y")


def joint(step, crossed):
    keys, values = (NEAR, FAR) if step == 0 else (FAR, NEAR)
    return [(2 * i + crossed, 2 * j) for i, j in keys] + [
        (2 * i + 1 - crossed, 2 * j + 1) for i, j in values
    ]


NT = (((1,), (1,)), ((), ()))
ROOM = 56 * 1024 * 1024
FULL = 127 * 512 * 1024


def rotary_table():
    halves = np.arange(0, HD, 2) / HD
    inverse = 1.0 / 500000.0**halves
    wavelen = 2.0 * np.pi / inverse
    smooth = (8192.0 / wavelen - 1.0) / 3.0
    blended = (1.0 - smooth) * inverse / 8.0 + smooth * inverse
    scaled = np.where(wavelen < 2048.0, inverse, np.where(wavelen > 8192.0, inverse / 8.0, blended))
    return jnp.asarray(scaled, dtype=jnp.float32)


def ancestry(parents):
    seg_count = parents.shape[0]
    indices = jnp.arange(seg_count, dtype=jnp.int32)
    linked = (
        (indices[:, None] == indices[None, :]) | (parents[:, None] == indices[None, :])
    ).astype(jnp.float32)
    for sweep in range(max(1, (seg_count - 1).bit_length())):
        linked = (
            jnp.dot(
                linked, linked, precision=lax.Precision.HIGHEST, preferred_element_type=jnp.float32
            )
            > 0.5
        ).astype(jnp.float32)
    return linked


def token_places(seg_row, linked):
    seg_count = linked.shape[0]
    onehot = (seg_row[:, None] == jnp.arange(seg_count, dtype=jnp.int32)[None, :]).astype(
        jnp.float32
    )
    lengths = jnp.sum(onehot, axis=0)
    starts = jnp.cumsum(lengths) - lengths
    before = jnp.sum(linked * lengths[None, :], axis=1) - lengths
    token_ids = jnp.arange(seg_row.shape[0], dtype=jnp.int32).astype(jnp.float32)
    return (
        STEM
        + token_ids
        - jnp.sum(onehot * starts[None, :], axis=1)
        + jnp.sum(onehot * before[None, :], axis=1)
    )


def turn_kernel(
    spot, q_own, k_own, v_own, q_mate, k_mate, v_mate, cos_ref, sin_ref, o_ref
):
    core = spot[1]
    pack = pl.program_id(0)

    def run(place, q_ref, k_ref, v_ref):
        cosine = cos_ref[place]
        sine = sin_ref[place]

        def turned(part):
            wide = part.astype(jnp.float32)
            return (wide * cosine + pltpu.roll(wide, HD // 2, 1) * sine).astype(jnp.bfloat16)

        for e in range(KVH):
            for head in range(2):
                at = pl.multiple_of((4 * e + head + 2 * core) * HD, HD)
                o_ref[0, e, :, head * HD : head * HD + HD] = turned(q_ref[:, pl.ds(at, HD)])
            at = e * HD
            o_ref[0, e, :, 2 * HD :] = jnp.where(
                core == 0, turned(k_ref[:, at : at + HD]), v_ref[:, at : at + HD]
            )

    @pl.when(pack == core)
    def _():
        run(0, q_own, k_own, v_own)

    @pl.when(pack != core)
    def _():
        run(1, q_mate, k_mate, v_mate)


def turn(here, own, mate, cosine, sine):
    tok = own[0].shape[0]
    whole = [
        pl.BlockSpec(part.shape, lambda i, here: (0, 0), pipeline_mode=pl.Buffered(1))
        for part in own + mate
    ]
    table = pl.BlockSpec(cosine.shape, lambda i, here: (0, 0, 0), pipeline_mode=pl.Buffered(1))
    return pl.pallas_call(
        turn_kernel,
        out_shape=jax.ShapeDtypeStruct((2, KVH, tok, 3 * HD), jnp.bfloat16),
        grid_spec=pltpu.PrefetchScalarGridSpec(
            num_scalar_prefetch=1,
            grid=(2,),
            in_specs=whole + [table, table],
            out_specs=pl.BlockSpec((1, KVH, tok, 3 * HD), lambda i, here: (i, 0, 0, 0)),
        ),
        compiler_params=pltpu.CompilerParams(vmem_limit_bytes=32 * 1024 * 1024),
        name="turn",
    )(here, *own, *mate, cosine, sine)


def held_at(x, core, group):
    chip = lax.div(group, 2)
    other = jnp.where(core == 0, near_of(x), far_of(x))
    found = jnp.where(lax.rem(group, 2) == core, 0, 2) + jnp.where(chip == x, 0, 1)
    return jnp.where((chip == x) | (chip == other), found, 4)


def near_of(x):
    return x + 1 - 2 * lax.rem(x, 2)


def far_of(x):
    return 3 - x


def relay_kernel(spot, owner, own, same, flip, cross, out, hold, sems):
    x, core = spot[0], spot[1]
    to = jnp.where(core == 0, far_of(x), near_of(x))
    half = own.shape[0] // 2
    parts = [(item, pl.ds(side * half, half), 2 * item + side) for item in range(2) for side in range(2)]
    codes = [held_at(x, core, owner[2 * to + item]) for item in range(2)]
    for item, rows, place in parts:
        for at, source in enumerate((own, same, flip, cross)):
            chosen = codes[item] == at if at else (codes[item] == 0) | (codes[item] == 4)

            @pl.when(chosen)
            def _(source=source):
                pltpu.make_async_copy(source.at[rows], hold.at[item, rows], sems.at[0, place]).start()

    for item, rows, place in parts:
        pltpu.make_async_copy(own.at[rows], hold.at[item, rows], sems.at[0, place]).wait()
        pltpu.make_async_copy(hold.at[item, rows], out.at[item, rows], sems.at[1, place]).start()
    for item, rows, place in parts:
        pltpu.make_async_copy(hold.at[item, rows], out.at[item, rows], sems.at[1, place]).wait()


def settle_kernel(spot, owner, own, same, flip, cross, two, out, hold, sems):
    x, core = spot[0], spot[1]
    parts = [(pack, e) for pack in range(2) for e in range(KVH)]
    for pack in range(2):
        code = held_at(x, core, owner[2 * x + pack])
        for at, source in enumerate((own, same, flip, cross, two.at[pack])):

            @pl.when(code == at)
            def _(source=source):
                for e in range(KVH):
                    pltpu.make_async_copy(
                        source.at[:, pl.ds(e * HD, HD)], hold.at[pack, e], sems.at[0, pack, e]
                    ).start()

    for pack, e in parts:
        pltpu.make_async_copy(
            own.at[:, pl.ds(0, HD)], hold.at[pack, e], sems.at[0, pack, e]
        ).wait()
        pltpu.make_async_copy(hold.at[pack, e], out.at[pack, e], sems.at[1, pack, e]).start()
    for pack, e in parts:
        pltpu.make_async_copy(hold.at[pack, e], out.at[pack, e], sems.at[1, pack, e]).wait()


def moved(kernel, shape, sems, scalars, arrays):
    whole = pl.BlockSpec(memory_space=pl.ANY)
    return pl.pallas_call(
        kernel,
        out_shape=jax.ShapeDtypeStruct(shape, jnp.bfloat16),
        grid_spec=pltpu.PrefetchScalarGridSpec(
            num_scalar_prefetch=len(scalars),
            grid=(1,),
            in_specs=[whole] * len(arrays),
            out_specs=whole,
            scratch_shapes=[pltpu.VMEM(shape, jnp.bfloat16), pltpu.SemaphoreType.DMA(sems)],
        ),
        compiler_params=pltpu.CompilerParams(vmem_limit_bytes=FULL),
        name=kernel.__name__,
    )(*scalars, *arrays)


def flipped_dot(left, right):
    return lax.dot_general(left, right, NT, preferred_element_type=jnp.float32)


def fill(core, mine_ref, other_ref, ka, vt, top):
    first = core == 0
    best = jnp.zeros((8, BQ), jnp.float32)
    for at in range(0, mine_ref.shape[0], BQ):
        mine = mine_ref[at : at + BQ, :]
        other = other_ref[at : at + BQ, :]
        key = jnp.where(first, mine, other)
        ka[at : at + BQ, :HD] = key
        vt[:HD, at : at + BQ] = jnp.where(first, other, mine).T
        wide = key.astype(jnp.float32)
        squares = (wide * wide).astype(jnp.bfloat16)
        best = jnp.maximum(best, flipped_dot(jnp.ones((8, HD), jnp.bfloat16), squares))
    vt[HD:, :] = jnp.ones_like(vt[HD:, :])
    longest = jnp.max(jnp.max(best, axis=1, keepdims=True), axis=0, keepdims=True)
    top[...] = jnp.broadcast_to(jnp.sqrt(longest), (8, HD))


def stacked(ref):
    return jnp.concatenate([ref[:, :HD], ref[:, HD : 2 * HD]], axis=0)


def ceiling(rows, top):
    wide = rows.astype(jnp.float32)
    squares = (wide * wide).astype(jnp.bfloat16)
    norms = jnp.dot(squares, jnp.ones((HD, HD), jnp.bfloat16), preferred_element_type=jnp.float32)
    return jnp.sqrt(norms) * top * 1.02 - SHIFT


def shift_row(qa):
    pick = lax.broadcasted_iota(jnp.int32, (8, 2 * HD), 1) == HD + SEGS
    return flipped_dot(pick.astype(jnp.float32).astype(jnp.bfloat16), qa[...])


def down(row):
    return jnp.broadcast_to(row, (HD, row.shape[1])).T


def pack_kernel(
    core, seen, q_ref, mine_ref, other_ref, qb_ref, kb_ref, o_ref, qa, ka, vt, top, acc
):
    qi = pl.program_id(0)
    rows = 2 * BQ
    lane = lax.broadcasted_iota(jnp.int32, (1, HD), 1)

    @pl.when(qi == 0)
    def _():
        fill(core[0], mine_ref, other_ref, ka, vt, top)
        ka[:, HD:] = kb_ref[...]

    q_rows = stacked(q_ref)
    qa[:, :HD] = q_rows
    side = jnp.concatenate([qb_ref[...], qb_ref[...]], axis=0).astype(jnp.float32)
    query = lax.broadcasted_iota(jnp.int32, (BQ, rows), 1)
    ahead = lax.broadcasted_iota(jnp.int32, (BQ, rows), 0) > jnp.where(
        query >= BQ, query - BQ, query
    )
    here = pl.multiple_of(qi * BQ, BQ)

    def scores(at):
        return flipped_dot(ka[pl.ds(at, BQ), :], qa[...])

    def mixed(at, weights):
        return jnp.dot(
            vt[:, pl.ds(at, BQ)],
            weights.astype(jnp.bfloat16),
            preferred_element_type=jnp.float32,
        )

    def run(shift):
        qa[:, HD:] = jnp.where(lane == SEGS, shift, side).astype(jnp.bfloat16)
        acc[...] = mixed(here, jnp.where(ahead, 0.0, jnp.exp2(scores(here) * SCALE)))

        def body(kj, carry):
            @pl.when(seen[qi, kj] > 0)
            def _():
                at = pl.multiple_of(kj * BQ, BQ)
                acc[...] += mixed(at, jnp.exp2(scores(at) * SCALE))

            return carry

        lax.fori_loop(0, qi, body, 0)
        o_ref[0, : HD + 8] = acc[...]
        o_ref[0, HD + 8 :] = shift_row(qa)

    run(ceiling(q_rows, top[0:1, 0:1]))

    @pl.when(jnp.min(acc[HD:, :]) < TINY)
    def _():
        qa[:, HD:] = side.astype(jnp.bfloat16)
        most = jnp.max(jnp.where(ahead, BARRED, scores(here)), axis=0, keepdims=True)

        def body(kj, most):
            part = scores(pl.multiple_of(kj * BQ, BQ))
            return jnp.maximum(most, jnp.max(part, axis=0, keepdims=True))

        run(down(lax.fori_loop(0, qi, body, most)))


def pack_part(core, seen, arrived, other, q_side, k_side):
    pack = arrived.shape[0]
    once = dict(pipeline_mode=pl.Buffered(1))
    return pl.pallas_call(
        pack_kernel,
        out_shape=jax.ShapeDtypeStruct((pack // BQ, HD + 16, 2 * BQ), jnp.float32),
        grid_spec=pltpu.PrefetchScalarGridSpec(
            num_scalar_prefetch=2,
            grid=(pack // BQ,),
            in_specs=[
                pl.BlockSpec((BQ, 2 * HD), lambda i, *_: (i, 0)),
                pl.BlockSpec((pack, HD), lambda i, *_: (0, 2), **once),
                pl.BlockSpec((pack, HD), lambda i, *_: (0, 0), **once),
                pl.BlockSpec((BQ, HD), lambda i, *_: (i, 0)),
                pl.BlockSpec((pack, HD), lambda i, *_: (0, 0), **once),
            ],
            out_specs=pl.BlockSpec((1, HD + 16, 2 * BQ), lambda i, *_: (i, 0, 0)),
            scratch_shapes=[
                pltpu.VMEM((2 * BQ, 2 * HD), jnp.bfloat16),
                pltpu.VMEM((pack, 2 * HD), jnp.bfloat16),
                pltpu.VMEM((HD + 8, pack), jnp.bfloat16),
                pltpu.VMEM((8, HD), jnp.float32),
                pltpu.VMEM((HD + 8, 2 * BQ), jnp.float32),
            ],
        ),
        compiler_params=pltpu.CompilerParams(vmem_limit_bytes=ROOM),
        cost_estimate=pl.CostEstimate(
            flops=8 * pack * pack * HD, bytes_accessed=8 << 20, transcendentals=pack * pack
        ),
        name="pack_part",
    )(core, seen, arrived, arrived, other, q_side, k_side)


def stem_kernel(core, q_ref, mine_ref, other_ref, part_ref, o_ref, qa, ka, vt, top, acc):
    stem = ka.shape[0]
    lane = lax.broadcasted_iota(jnp.int32, (1, HD), 1)
    side = jnp.broadcast_to(jnp.where(lane == SEGS, -1.0, 0.0).astype(jnp.bfloat16), (CK, HD))

    @pl.when(pl.program_id(0) == 0)
    def _():
        fill(core[0], mine_ref, other_ref, ka, vt, top)

    blocks = part_ref.shape[0]
    q_rows = jnp.concatenate([stacked(q_ref.at[pl.ds(b * BQ, BQ)]) for b in range(blocks)], axis=0)
    qa[:, :HD] = q_rows

    def scores(at):
        return flipped_dot(jnp.concatenate([ka[pl.ds(at, CK), :], side], axis=1), qa[...])

    def run(shift):
        qa[:, HD:] = jnp.where(lane == SEGS, shift, 0.0).astype(jnp.bfloat16)
        total, weights = None, []
        held = scores(0)
        for at in range(0, stem, CK):
            ahead = scores(at + CK) if at + CK < stem else None
            weights.append(jnp.exp2(held * SCALE).astype(jnp.bfloat16))
            if len(weights) * CK == WIDE:
                part = jnp.dot(
                    vt[:, at + CK - WIDE : at + CK],
                    jnp.concatenate(weights, axis=0),
                    preferred_element_type=jnp.float32,
                )
                total = part if total is None else total + part
                weights = []
            held = ahead
        acc[...] = total

    def finish():
        shifts = shift_row(qa)[:1]
        for b in range(blocks):
            here = slice(b * 2 * BQ, (b + 1) * 2 * BQ)
            shift = shifts[:, here]
            before = part_ref[b, HD + 8 : HD + 9]
            most = jnp.maximum(shift, before)
            new = jnp.exp2((shift - most) * SCALE)
            old = jnp.exp2((before - most) * SCALE)
            total = acc[HD : HD + 1, here] * new + part_ref[b, HD : HD + 1] * old
            out = (acc[:HD, here] * (new / total) + part_ref[b, :HD] * (old / total)).T
            o_ref[b * BQ : (b + 1) * BQ, :HD] = out[:BQ].astype(jnp.bfloat16)
            o_ref[b * BQ : (b + 1) * BQ, HD:] = out[BQ:].astype(jnp.bfloat16)

    run(ceiling(q_rows, top[0:1, 0:1]))
    finish()

    @pl.when(jnp.min(acc[HD:, :]) < TINY)
    def _():
        qa[:, HD:] = jnp.zeros_like(q_rows)

        def body(step, most):
            part = scores(pl.multiple_of(step * CK, CK))
            return jnp.maximum(most, jnp.max(part, axis=0, keepdims=True))

        low = jnp.full((1, q_rows.shape[0]), BARRED, jnp.float32)
        run(down(lax.fori_loop(0, stem // CK, body, low)))
        finish()


def stem_part(core, arrived, mine, other, before):
    pack = arrived.shape[0]
    stem = mine.shape[0]
    once = dict(pipeline_mode=pl.Buffered(1))
    return pl.pallas_call(
        stem_kernel,
        out_shape=jax.ShapeDtypeStruct((pack, 2 * HD), jnp.bfloat16),
        grid_spec=pltpu.PrefetchScalarGridSpec(
            num_scalar_prefetch=1,
            grid=(pack // (SPAN * BQ),),
            in_specs=[
                pl.BlockSpec((SPAN * BQ, 2 * HD), lambda i, *_: (i, 0)),
                pl.BlockSpec((stem, HD), lambda i, *_: (0, 0), **once),
                pl.BlockSpec((stem, HD), lambda i, *_: (0, 0), **once),
                pl.BlockSpec((SPAN, HD + 16, 2 * BQ), lambda i, *_: (i, 0, 0)),
            ],
            out_specs=pl.BlockSpec((SPAN * BQ, 2 * HD), lambda i, *_: (i, 0)),
            scratch_shapes=[
                pltpu.VMEM((2 * SPAN * BQ, 2 * HD), jnp.bfloat16),
                pltpu.VMEM((stem, HD), jnp.bfloat16),
                pltpu.VMEM((HD + 8, stem), jnp.bfloat16),
                pltpu.VMEM((8, HD), jnp.float32),
                pltpu.VMEM((HD + 8, 2 * SPAN * BQ), jnp.float32),
            ],
        ),
        compiler_params=pltpu.CompilerParams(vmem_limit_bytes=FULL),
        cost_estimate=pl.CostEstimate(
            flops=8 * pack * stem * HD, bytes_accessed=8 << 20, transcendentals=2 * pack * stem
        ),
        name="stem_part",
    )(core, arrived, mine, other, before)


def gather_kernel(core, mine_ref, other_ref, o_ref, mine, other, sems):
    step = pl.program_id(0)
    heads = KVH // 2

    def copies(part):
        rows = pl.ds(part * heads, heads)
        return (
            pltpu.make_async_copy(mine_ref.at[core[0], rows], mine.at[rows], sems.at[0, part]),
            pltpu.make_async_copy(other_ref.at[rows], other.at[rows], sems.at[1, part]),
        )

    @pl.when(step == 0)
    def _():
        for copy in copies(0) + copies(1):
            copy.start()

    for copy in copies(step):
        copy.wait()
    first = core[0] == 0
    for e in range(heads):
        own, got = mine[step * heads + e], other[step * heads + e]
        at = 4 * HD * e
        o_ref[:, at : at + 2 * HD] = jnp.where(first, own, got)
        o_ref[:, at + 2 * HD : at + 4 * HD] = jnp.where(first, got, own)


def gather(core, mine, other):
    tok = mine.shape[2]
    whole = pl.BlockSpec(memory_space=pl.ANY)
    return pl.pallas_call(
        gather_kernel,
        out_shape=jax.ShapeDtypeStruct((tok, H * HD), jnp.bfloat16),
        grid_spec=pltpu.PrefetchScalarGridSpec(
            num_scalar_prefetch=1,
            grid=(2,),
            in_specs=[whole, whole],
            out_specs=pl.BlockSpec((tok, H * HD // 2), lambda i, core: (0, i)),
            scratch_shapes=[
                pltpu.VMEM(other.shape, jnp.bfloat16),
                pltpu.VMEM(other.shape, jnp.bfloat16),
                pltpu.SemaphoreType.DMA((2, 2)),
            ],
        ),
        name="gather",
    )(core, mine, other)


def shards(queries, keys, values, stem_kv, seg_ids, seg_parent, stem_owner):
    tok = queries.shape[1]
    x = lax.axis_index("x")
    core = lax.axis_index("core")
    spot = lax.axis_index(SEQ)
    pack_len = tok * 16
    core_row = core[None].astype(jnp.int32)
    here = jnp.stack([x, core]).astype(jnp.int32)

    raw = (queries[0], keys[0], values[0])
    rows = jnp.concatenate([seg_ids[0], seg_parent[0]])
    rows_mate = lax.ppermute(rows, "core", FLIP)
    raw_mate = tuple(lax.ppermute(part, "core", FLIP) for part in raw)

    stem = stem_kv[0]
    own = lax.dynamic_index_in_dim(stem, core, 0, keepdims=False)
    given = lax.dynamic_index_in_dim(stem, 1 - core, 0, keepdims=False)
    same = lax.ppermute(own, ("x", "core"), joint(0, 0))
    cross = lax.ppermute(given, ("x", "core"), joint(0, 1))
    flip = lax.ppermute(given, "core", FLIP)

    both = jnp.stack([rows, rows_mate])
    linked = jax.vmap(ancestry)(both[:, pack_len:])
    places = jax.vmap(token_places)(both[:, :pack_len], linked)
    places = lax.dynamic_slice_in_dim(places, spot * tok, tok, axis=1)
    angles = places[:, :, None] * rotary_table()[None, None, :]
    cosine, sine = jnp.cos(angles), jnp.sin(angles)
    sent = turn(
        here,
        raw,
        raw_mate,
        jnp.concatenate([cosine, cosine], axis=2),
        jnp.concatenate([-sine, sine], axis=2),
    )
    arrived = lax.all_to_all(
        sent.reshape(16, tok, 3 * HD), SEQ, split_axis=0, concat_axis=0, tiled=True
    ).reshape(pack_len, 3 * HD)
    same, cross, flip, sent = lax.optimization_barrier((same, cross, flip, sent))

    held = (own, same, flip, cross)
    wanted = moved(relay_kernel, stem.shape, (2, 4), (here, stem_owner), held)
    two = lax.ppermute(wanted, ("x", "core"), joint(1, 0))
    both, linked, _ = lax.optimization_barrier((both, linked, wanted))
    pair = lax.ppermute(arrived[:, 2 * HD :], "core", FLIP)

    ours = spot // KVH == core
    seg_row = jnp.where(ours, both[0, :pack_len], both[1, :pack_len])
    reach = jnp.where(ours, linked[0], linked[1])
    onehot = (seg_row[:, None] == jnp.arange(HD, dtype=jnp.int32)[None, :]).astype(jnp.float32)
    barred = jnp.pad(BARRED * (1.0 - reach), ((0, HD - SEGS), (0, HD - SEGS)))
    q_side = jnp.dot(onehot, barred, precision=lax.Precision.HIGHEST).astype(jnp.bfloat16)
    k_side = jnp.where(jnp.arange(HD)[None, :] == SEGS, -1.0, onehot).astype(jnp.bfloat16)
    q_has = onehot.reshape(pack_len // BQ, BQ, HD).max(axis=1)[:, :SEGS]
    seen = (q_has @ reach @ q_has.T > 0.5).astype(jnp.int32)

    stems = moved(
        settle_kernel,
        (2, KVH, stem.shape[1], HD),
        (2, 2, KVH),
        (here, stem_owner),
        held + (two,),
    ).reshape(16, stem.shape[1], HD)
    mine = lax.all_to_all(stems, SEQ, split_axis=0, concat_axis=0, tiled=True).reshape(STEM, HD)
    arrived, pair, _ = lax.optimization_barrier((arrived, pair, stems))
    partial = pack_part(core_row, seen, arrived, pair, q_side, k_side)
    mine, partial = lax.optimization_barrier((mine, partial))
    other = lax.ppermute(mine, "core", FLIP)
    mixed = stem_part(core_row, arrived, mine, other, partial)

    back = lax.all_to_all(
        mixed.reshape(16, tok, 2 * HD), SEQ, split_axis=0, concat_axis=0, tiled=True
    ).reshape(2, KVH, tok, 2 * HD)
    away = lax.dynamic_index_in_dim(back, 1 - core, 0, keepdims=False)
    return gather(core_row, back, lax.ppermute(away, "core", FLIP))[None]


def solution(mesh):
    grid = Mesh(mesh.devices.reshape(4, 2, 4, 4), ("x", "core", "z", "y"))
    dp, seq = ("x", "core"), SEQ
    placed = (
        P(dp, seq, None),
        P(dp, seq, None),
        P(dp, seq, None),
        P(dp, None, seq, None),
        P(dp, None),
        P(dp, None),
        P(),
    )
    return jax.shard_map(
        shards, mesh=grid, in_specs=placed, out_specs=P(dp, seq, None), check_vma=False
    )
```

```python
import math

import jax
import jax.numpy as jnp
import numpy as np
from jax import lax
from jax.experimental import pallas as pl
from jax.experimental.pallas import tpu as pltpu
from jax.sharding import Mesh
from jax.sharding import PartitionSpec as P

H = 32
KVH = 8
HD = 128
STEM = 4096
SEGS = 16
BARRED = -1e30
BQ = 512
CK = 256
WIDE = 1024
SCALE = HD**-0.5 * math.log2(math.e)
SHIFT = 70.0 / SCALE
TINY = 2.0**-16
FLIP = [(0, 1), (1, 0)]
NEAR = [(0, 1), (1, 0), (2, 3), (3, 2)]
FAR = [(0, 3), (3, 0), (1, 2), (2, 1)]
SEQ = ("z", "y")


def joint(step, crossed):
    keys, values = (NEAR, FAR) if step == 0 else (FAR, NEAR)
    return [(2 * i + crossed, 2 * j) for i, j in keys] + [
        (2 * i + 1 - crossed, 2 * j + 1) for i, j in values
    ]


NT = (((1,), (1,)), ((), ()))
ROOM = 56 * 1024 * 1024
FULL = 127 * 512 * 1024


def rotary_table():
    halves = np.arange(0, HD, 2) / HD
    inverse = 1.0 / 500000.0**halves
    wavelen = 2.0 * np.pi / inverse
    smooth = (8192.0 / wavelen - 1.0) / 3.0
    blended = (1.0 - smooth) * inverse / 8.0 + smooth * inverse
    scaled = np.where(wavelen < 2048.0, inverse, np.where(wavelen > 8192.0, inverse / 8.0, blended))
    return jnp.asarray(scaled, dtype=jnp.float32)


def ancestry(parents):
    seg_count = parents.shape[0]
    indices = jnp.arange(seg_count, dtype=jnp.int32)
    linked = (
        (indices[:, None] == indices[None, :]) | (parents[:, None] == indices[None, :])
    ).astype(jnp.float32)
    for sweep in range(max(1, (seg_count - 1).bit_length())):
        linked = (
            jnp.dot(
                linked, linked, precision=lax.Precision.HIGHEST, preferred_element_type=jnp.float32
            )
            > 0.5
        ).astype(jnp.float32)
    return linked


def token_places(seg_row, linked):
    seg_count = linked.shape[0]
    onehot = (seg_row[:, None] == jnp.arange(seg_count, dtype=jnp.int32)[None, :]).astype(
        jnp.float32
    )
    lengths = jnp.sum(onehot, axis=0)
    starts = jnp.cumsum(lengths) - lengths
    before = jnp.sum(linked * lengths[None, :], axis=1) - lengths
    token_ids = jnp.arange(seg_row.shape[0], dtype=jnp.int32).astype(jnp.float32)
    return (
        STEM
        + token_ids
        - jnp.sum(onehot * starts[None, :], axis=1)
        + jnp.sum(onehot * before[None, :], axis=1)
    )


def turn_kernel(
    spot, q_own, k_own, v_own, q_mate, k_mate, v_mate, cos_ref, sin_ref, o_ref
):
    core = spot[1]
    pack = pl.program_id(0)

    def run(place, q_ref, k_ref, v_ref):
        cosine = cos_ref[place]
        sine = sin_ref[place]

        def turned(part):
            wide = part.astype(jnp.float32)
            return (wide * cosine + pltpu.roll(wide, HD // 2, 1) * sine).astype(jnp.bfloat16)

        for e in range(KVH):
            for head in range(2):
                at = pl.multiple_of((4 * e + head + 2 * core) * HD, HD)
                o_ref[0, e, :, head * HD : head * HD + HD] = turned(q_ref[:, pl.ds(at, HD)])
            at = e * HD
            o_ref[0, e, :, 2 * HD :] = jnp.where(
                core == 0, turned(k_ref[:, at : at + HD]), v_ref[:, at : at + HD]
            )

    @pl.when(pack == core)
    def _():
        run(0, q_own, k_own, v_own)

    @pl.when(pack != core)
    def _():
        run(1, q_mate, k_mate, v_mate)


def turn(here, own, mate, cosine, sine):
    tok = own[0].shape[0]
    whole = [
        pl.BlockSpec(part.shape, lambda i, here: (0, 0), pipeline_mode=pl.Buffered(1))
        for part in own + mate
    ]
    table = pl.BlockSpec(cosine.shape, lambda i, here: (0, 0, 0), pipeline_mode=pl.Buffered(1))
    return pl.pallas_call(
        turn_kernel,
        out_shape=jax.ShapeDtypeStruct((2, KVH, tok, 3 * HD), jnp.bfloat16),
        grid_spec=pltpu.PrefetchScalarGridSpec(
            num_scalar_prefetch=1,
            grid=(2,),
            in_specs=whole + [table, table],
            out_specs=pl.BlockSpec((1, KVH, tok, 3 * HD), lambda i, here: (i, 0, 0, 0)),
        ),
        compiler_params=pltpu.CompilerParams(vmem_limit_bytes=32 * 1024 * 1024),
        name="turn",
    )(here, *own, *mate, cosine, sine)


def held_at(x, core, group):
    chip = lax.div(group, 2)
    other = jnp.where(core == 0, near_of(x), far_of(x))
    found = jnp.where(lax.rem(group, 2) == core, 0, 2) + jnp.where(chip == x, 0, 1)
    return jnp.where((chip == x) | (chip == other), found, 4)


def near_of(x):
    return x + 1 - 2 * lax.rem(x, 2)


def far_of(x):
    return 3 - x


def relay_kernel(spot, owner, own, same, flip, cross, out, hold, sems):
    x, core = spot[0], spot[1]
    to = jnp.where(core == 0, far_of(x), near_of(x))
    half = own.shape[0] // 2
    parts = [(item, pl.ds(side * half, half), 2 * item + side) for item in range(2) for side in range(2)]
    codes = [held_at(x, core, owner[2 * to + item]) for item in range(2)]
    for item, rows, place in parts:
        for at, source in enumerate((own, same, flip, cross)):
            chosen = codes[item] == at if at else (codes[item] == 0) | (codes[item] == 4)

            @pl.when(chosen)
            def _(source=source):
                pltpu.make_async_copy(source.at[rows], hold.at[item, rows], sems.at[0, place]).start()

    for item, rows, place in parts:
        pltpu.make_async_copy(own.at[rows], hold.at[item, rows], sems.at[0, place]).wait()
        pltpu.make_async_copy(hold.at[item, rows], out.at[item, rows], sems.at[1, place]).start()
    for item, rows, place in parts:
        pltpu.make_async_copy(hold.at[item, rows], out.at[item, rows], sems.at[1, place]).wait()


def settle_kernel(spot, owner, own, same, flip, cross, two, out, hold, sems):
    x, core = spot[0], spot[1]
    parts = [(pack, e) for pack in range(2) for e in range(KVH)]
    for pack in range(2):
        code = held_at(x, core, owner[2 * x + pack])
        for at, source in enumerate((own, same, flip, cross, two.at[pack])):

            @pl.when(code == at)
            def _(source=source):
                for e in range(KVH):
                    pltpu.make_async_copy(
                        source.at[:, pl.ds(e * HD, HD)], hold.at[pack, e], sems.at[0, pack, e]
                    ).start()

    for pack, e in parts:
        pltpu.make_async_copy(
            own.at[:, pl.ds(0, HD)], hold.at[pack, e], sems.at[0, pack, e]
        ).wait()
        pltpu.make_async_copy(hold.at[pack, e], out.at[pack, e], sems.at[1, pack, e]).start()
    for pack, e in parts:
        pltpu.make_async_copy(hold.at[pack, e], out.at[pack, e], sems.at[1, pack, e]).wait()


def moved(kernel, shape, sems, scalars, arrays):
    whole = pl.BlockSpec(memory_space=pl.ANY)
    return pl.pallas_call(
        kernel,
        out_shape=jax.ShapeDtypeStruct(shape, jnp.bfloat16),
        grid_spec=pltpu.PrefetchScalarGridSpec(
            num_scalar_prefetch=len(scalars),
            grid=(1,),
            in_specs=[whole] * len(arrays),
            out_specs=whole,
            scratch_shapes=[pltpu.VMEM(shape, jnp.bfloat16), pltpu.SemaphoreType.DMA(sems)],
        ),
        compiler_params=pltpu.CompilerParams(vmem_limit_bytes=FULL),
        name=kernel.__name__,
    )(*scalars, *arrays)


def flipped_dot(left, right):
    return lax.dot_general(left, right, NT, preferred_element_type=jnp.float32)


def fill(core, mine_ref, other_ref, ka, vt, top):
    first = core == 0
    best = jnp.zeros((8, BQ), jnp.float32)
    for at in range(0, mine_ref.shape[0], BQ):
        mine = mine_ref[at : at + BQ, :]
        other = other_ref[at : at + BQ, :]
        key = jnp.where(first, mine, other)
        ka[at : at + BQ, :HD] = key
        vt[:HD, at : at + BQ] = jnp.where(first, other, mine).T
        wide = key.astype(jnp.float32)
        squares = (wide * wide).astype(jnp.bfloat16)
        best = jnp.maximum(best, flipped_dot(jnp.ones((8, HD), jnp.bfloat16), squares))
    vt[HD:, :] = jnp.ones_like(vt[HD:, :])
    longest = jnp.max(jnp.max(best, axis=1, keepdims=True), axis=0, keepdims=True)
    top[...] = jnp.broadcast_to(jnp.sqrt(longest), (8, HD))


def stacked(ref):
    return jnp.concatenate([ref[:, :HD], ref[:, HD : 2 * HD]], axis=0)


def ceiling(rows, top):
    wide = rows.astype(jnp.float32)
    squares = (wide * wide).astype(jnp.bfloat16)
    norms = jnp.dot(squares, jnp.ones((HD, HD), jnp.bfloat16), preferred_element_type=jnp.float32)
    return jnp.sqrt(norms) * top * 1.02 - SHIFT


def shift_row(qa):
    pick = lax.broadcasted_iota(jnp.int32, (8, 2 * HD), 1) == HD + SEGS
    return flipped_dot(pick.astype(jnp.float32).astype(jnp.bfloat16), qa[...])


def down(row):
    return jnp.broadcast_to(row, (HD, row.shape[1])).T


def pack_kernel(
    core, seen, q_ref, mine_ref, other_ref, qb_ref, kb_ref, o_ref, qa, ka, vt, top, acc
):
    qi = pl.program_id(0)
    rows = 2 * BQ
    lane = lax.broadcasted_iota(jnp.int32, (1, HD), 1)

    @pl.when(qi == 0)
    def _():
        fill(core[0], mine_ref, other_ref, ka, vt, top)
        ka[:, HD:] = kb_ref[...]

    q_rows = stacked(q_ref)
    qa[:, :HD] = q_rows
    side = jnp.concatenate([qb_ref[...], qb_ref[...]], axis=0).astype(jnp.float32)
    query = lax.broadcasted_iota(jnp.int32, (BQ, rows), 1)
    ahead = lax.broadcasted_iota(jnp.int32, (BQ, rows), 0) > jnp.where(
        query >= BQ, query - BQ, query
    )
    here = pl.multiple_of(qi * BQ, BQ)

    def scores(at):
        return flipped_dot(ka[pl.ds(at, BQ), :], qa[...])

    def mixed(at, weights):
        return jnp.dot(
            vt[:, pl.ds(at, BQ)],
            weights.astype(jnp.bfloat16),
            preferred_element_type=jnp.float32,
        )

    def run(shift):
        qa[:, HD:] = jnp.where(lane == SEGS, shift, side).astype(jnp.bfloat16)
        acc[...] = mixed(here, jnp.where(ahead, 0.0, jnp.exp2(scores(here) * SCALE)))

        def body(kj, carry):
            @pl.when(seen[qi, kj] > 0)
            def _():
                at = pl.multiple_of(kj * BQ, BQ)
                acc[...] += mixed(at, jnp.exp2(scores(at) * SCALE))

            return carry

        lax.fori_loop(0, qi, body, 0)
        o_ref[0, : HD + 8] = acc[...]
        o_ref[0, HD + 8 :] = shift_row(qa)

    run(ceiling(q_rows, top[0:1, 0:1]))

    @pl.when(jnp.min(acc[HD:, :]) < TINY)
    def _():
        qa[:, HD:] = side.astype(jnp.bfloat16)
        most = jnp.max(jnp.where(ahead, BARRED, scores(here)), axis=0, keepdims=True)

        def body(kj, most):
            part = scores(pl.multiple_of(kj * BQ, BQ))
            return jnp.maximum(most, jnp.max(part, axis=0, keepdims=True))

        run(down(lax.fori_loop(0, qi, body, most)))


def pack_part(core, seen, arrived, other, q_side, k_side):
    pack = arrived.shape[0]
    once = dict(pipeline_mode=pl.Buffered(1))
    return pl.pallas_call(
        pack_kernel,
        out_shape=jax.ShapeDtypeStruct((pack // BQ, HD + 16, 2 * BQ), jnp.float32),
        grid_spec=pltpu.PrefetchScalarGridSpec(
            num_scalar_prefetch=2,
            grid=(pack // BQ,),
            in_specs=[
                pl.BlockSpec((BQ, 2 * HD), lambda i, *_: (i, 0)),
                pl.BlockSpec((pack, HD), lambda i, *_: (0, 2), **once),
                pl.BlockSpec((pack, HD), lambda i, *_: (0, 0), **once),
                pl.BlockSpec((BQ, HD), lambda i, *_: (i, 0)),
                pl.BlockSpec((pack, HD), lambda i, *_: (0, 0), **once),
            ],
            out_specs=pl.BlockSpec((1, HD + 16, 2 * BQ), lambda i, *_: (i, 0, 0)),
            scratch_shapes=[
                pltpu.VMEM((2 * BQ, 2 * HD), jnp.bfloat16),
                pltpu.VMEM((pack, 2 * HD), jnp.bfloat16),
                pltpu.VMEM((HD + 8, pack), jnp.bfloat16),
                pltpu.VMEM((8, HD), jnp.float32),
                pltpu.VMEM((HD + 8, 2 * BQ), jnp.float32),
            ],
        ),
        compiler_params=pltpu.CompilerParams(vmem_limit_bytes=ROOM),
        cost_estimate=pl.CostEstimate(
            flops=8 * pack * pack * HD, bytes_accessed=8 << 20, transcendentals=pack * pack
        ),
        name="pack_part",
    )(core, seen, arrived, arrived, other, q_side, k_side)


def stem_kernel(core, q_ref, mine_ref, other_ref, part_ref, o_ref, qa, ka, vt, top, acc):
    stem = ka.shape[0]
    lane = lax.broadcasted_iota(jnp.int32, (1, HD), 1)
    side = jnp.broadcast_to(jnp.where(lane == SEGS, -1.0, 0.0).astype(jnp.bfloat16), (CK, HD))

    @pl.when(pl.program_id(0) == 0)
    def _():
        fill(core[0], mine_ref, other_ref, ka, vt, top)

    q_rows = stacked(q_ref)
    qa[:, :HD] = q_rows

    def scores(at):
        return flipped_dot(jnp.concatenate([ka[pl.ds(at, CK), :], side], axis=1), qa[...])

    def run(shift):
        qa[:, HD:] = jnp.where(lane == SEGS, shift, 0.0).astype(jnp.bfloat16)
        total, weights = None, []
        held = scores(0)
        for at in range(0, stem, CK):
            ahead = scores(at + CK) if at + CK < stem else None
            weights.append(jnp.exp2(held * SCALE).astype(jnp.bfloat16))
            if len(weights) * CK == WIDE:
                part = jnp.dot(
                    vt[:, at + CK - WIDE : at + CK],
                    jnp.concatenate(weights, axis=0),
                    preferred_element_type=jnp.float32,
                )
                total = part if total is None else total + part
                weights = []
            held = ahead
        acc[...] = total

    def finish():
        shift = shift_row(qa)[:1]
        before = part_ref[0, HD + 8 : HD + 9]
        most = jnp.maximum(shift, before)
        new = jnp.exp2((shift - most) * SCALE)
        old = jnp.exp2((before - most) * SCALE)
        total = acc[HD : HD + 1] * new + part_ref[0, HD : HD + 1] * old
        out = (acc[:HD] * (new / total) + part_ref[0, :HD] * (old / total)).T
        o_ref[:, :HD] = out[:BQ].astype(jnp.bfloat16)
        o_ref[:, HD:] = out[BQ:].astype(jnp.bfloat16)

    run(ceiling(q_rows, top[0:1, 0:1]))
    finish()

    @pl.when(jnp.min(acc[HD:, :]) < TINY)
    def _():
        qa[:, HD:] = jnp.zeros_like(q_rows)

        def body(step, most):
            part = scores(pl.multiple_of(step * CK, CK))
            return jnp.maximum(most, jnp.max(part, axis=0, keepdims=True))

        low = jnp.full((1, 2 * BQ), BARRED, jnp.float32)
        run(down(lax.fori_loop(0, stem // CK, body, low)))
        finish()


def stem_part(core, arrived, mine, other, before):
    pack = arrived.shape[0]
    stem = mine.shape[0]
    return pl.pallas_call(
        stem_kernel,
        out_shape=jax.ShapeDtypeStruct((pack, 2 * HD), jnp.bfloat16),
        grid_spec=pltpu.PrefetchScalarGridSpec(
            num_scalar_prefetch=1,
            grid=(pack // BQ,),
            in_specs=[
                pl.BlockSpec((BQ, 2 * HD), lambda i, *_: (i, 0)),
                pl.BlockSpec(memory_space=pltpu.VMEM),
                pl.BlockSpec(memory_space=pltpu.VMEM),
                pl.BlockSpec((1, HD + 16, 2 * BQ), lambda i, *_: (i, 0, 0)),
            ],
            out_specs=pl.BlockSpec((BQ, 2 * HD), lambda i, *_: (i, 0)),
            scratch_shapes=[
                pltpu.VMEM((2 * BQ, 2 * HD), jnp.bfloat16),
                pltpu.VMEM((stem, HD), jnp.bfloat16),
                pltpu.VMEM((HD + 8, stem), jnp.bfloat16),
                pltpu.VMEM((8, HD), jnp.float32),
                pltpu.VMEM((HD + 8, 2 * BQ), jnp.float32),
            ],
        ),
        compiler_params=pltpu.CompilerParams(vmem_limit_bytes=48 * 1024 * 1024),
        cost_estimate=pl.CostEstimate(
            flops=8 * pack * stem * HD, bytes_accessed=8 << 20, transcendentals=2 * pack * stem
        ),
        name="stem_part",
    )(core, arrived, inside(mine), inside(other), before)


def gather_kernel(core, mine_ref, other_ref, o_ref):
    step = pl.program_id(0)
    heads = KVH // 2
    first = core[0] == 0
    for e in range(heads):
        own, got = mine_ref[core[0], step * heads + e], other_ref[step * heads + e]
        at = 4 * HD * e
        o_ref[:, at : at + 2 * HD] = jnp.where(first, own, got)
        o_ref[:, at + 2 * HD : at + 4 * HD] = jnp.where(first, got, own)


def inside(part):
    return pltpu.with_memory_space_constraint(part, pltpu.VMEM)


def gather(core, mine, other):
    tok = mine.shape[2]
    whole = pl.BlockSpec(memory_space=pltpu.VMEM)
    return pl.pallas_call(
        gather_kernel,
        out_shape=jax.ShapeDtypeStruct((tok, H * HD), jnp.bfloat16),
        grid_spec=pltpu.PrefetchScalarGridSpec(
            num_scalar_prefetch=1,
            grid=(2,),
            in_specs=[whole, whole],
            out_specs=pl.BlockSpec((tok, H * HD // 2), lambda i, core: (0, i)),
        ),
        name="gather",
    )(core, inside(mine), inside(other))


def shards(queries, keys, values, stem_kv, seg_ids, seg_parent, stem_owner):
    tok = queries.shape[1]
    x = lax.axis_index("x")
    core = lax.axis_index("core")
    spot = lax.axis_index(SEQ)
    pack_len = tok * 16
    core_row = core[None].astype(jnp.int32)
    here = jnp.stack([x, core]).astype(jnp.int32)

    raw = (queries[0], keys[0], values[0])
    rows = jnp.concatenate([seg_ids[0], seg_parent[0]])
    rows_mate = lax.ppermute(rows, "core", FLIP)
    raw_mate = tuple(lax.ppermute(part, "core", FLIP) for part in raw)

    stem = stem_kv[0]
    own = lax.dynamic_index_in_dim(stem, core, 0, keepdims=False)
    given = lax.dynamic_index_in_dim(stem, 1 - core, 0, keepdims=False)
    same = lax.ppermute(own, ("x", "core"), joint(0, 0))
    cross = lax.ppermute(given, ("x", "core"), joint(0, 1))
    flip = lax.ppermute(given, "core", FLIP)

    both = jnp.stack([rows, rows_mate])
    linked = jax.vmap(ancestry)(both[:, pack_len:])
    places = jax.vmap(token_places)(both[:, :pack_len], linked)
    places = lax.dynamic_slice_in_dim(places, spot * tok, tok, axis=1)
    angles = places[:, :, None] * rotary_table()[None, None, :]
    cosine, sine = jnp.cos(angles), jnp.sin(angles)
    sent = turn(
        here,
        raw,
        raw_mate,
        jnp.concatenate([cosine, cosine], axis=2),
        jnp.concatenate([-sine, sine], axis=2),
    )
    arrived = lax.all_to_all(
        sent.reshape(16, tok, 3 * HD), SEQ, split_axis=0, concat_axis=0, tiled=True
    ).reshape(pack_len, 3 * HD)
    same, cross, flip, sent = lax.optimization_barrier((same, cross, flip, sent))

    held = (own, same, flip, cross)
    wanted = moved(relay_kernel, stem.shape, (2, 4), (here, stem_owner), held)
    two = lax.ppermute(wanted, ("x", "core"), joint(1, 0))
    both, linked, _ = lax.optimization_barrier((both, linked, wanted))
    pair = lax.ppermute(arrived[:, 2 * HD :], "core", FLIP)

    ours = spot // KVH == core
    seg_row = jnp.where(ours, both[0, :pack_len], both[1, :pack_len])
    reach = jnp.where(ours, linked[0], linked[1])
    onehot = (seg_row[:, None] == jnp.arange(HD, dtype=jnp.int32)[None, :]).astype(jnp.float32)
    barred = jnp.pad(BARRED * (1.0 - reach), ((0, HD - SEGS), (0, HD - SEGS)))
    q_side = jnp.dot(onehot, barred, precision=lax.Precision.HIGHEST).astype(jnp.bfloat16)
    k_side = jnp.where(jnp.arange(HD)[None, :] == SEGS, -1.0, onehot).astype(jnp.bfloat16)
    q_has = onehot.reshape(pack_len // BQ, BQ, HD).max(axis=1)[:, :SEGS]
    seen = (q_has @ reach @ q_has.T > 0.5).astype(jnp.int32)

    stems = moved(
        settle_kernel,
        (2, KVH, stem.shape[1], HD),
        (2, 2, KVH),
        (here, stem_owner),
        held + (two,),
    ).reshape(16, stem.shape[1], HD)
    mine = lax.all_to_all(stems, SEQ, split_axis=0, concat_axis=0, tiled=True).reshape(STEM, HD)
    arrived, pair, _ = lax.optimization_barrier((arrived, pair, stems))
    partial = pack_part(core_row, seen, arrived, pair, q_side, k_side)
    mine, partial = lax.optimization_barrier((mine, partial))
    other = lax.ppermute(mine, "core", FLIP)
    mixed = stem_part(core_row, arrived, mine, other, partial)

    back = lax.all_to_all(
        mixed.reshape(16, tok, 2 * HD), SEQ, split_axis=0, concat_axis=0, tiled=True
    ).reshape(2, KVH, tok, 2 * HD)
    away = lax.dynamic_index_in_dim(back, 1 - core, 0, keepdims=False)
    return gather(core_row, back, lax.ppermute(away, "core", FLIP))[None]


def solution(mesh):
    grid = Mesh(mesh.devices.reshape(4, 2, 4, 4), ("x", "core", "z", "y"))
    dp, seq = ("x", "core"), SEQ
    placed = (
        P(dp, seq, None),
        P(dp, seq, None),
        P(dp, seq, None),
        P(dp, None, seq, None),
        P(dp, None),
        P(dp, None),
        P(),
    )
    return jax.shard_map(
        shards, mesh=grid, in_specs=placed, out_specs=P(dp, seq, None), check_vma=False
    )
```

```python
import math

import jax
import jax.numpy as jnp
import numpy as np
from jax import lax
from jax.experimental import pallas as pl
from jax.experimental.pallas import tpu as pltpu
from jax.sharding import Mesh
from jax.sharding import PartitionSpec as P

H = 32
KVH = 8
HD = 128
STEM = 4096
SEGS = 16
BARRED = -1e30
BQ = 512
CK = 256
WIDE = 1024
SCALE = HD**-0.5 * math.log2(math.e)
SHIFT = 70.0 / SCALE
TINY = 2.0**-16
FLIP = [(0, 1), (1, 0)]
NEAR = [(0, 1), (1, 0), (2, 3), (3, 2)]
FAR = [(0, 3), (3, 0), (1, 2), (2, 1)]
SEQ = ("z", "y")


def joint(step, crossed):
    keys, values = (NEAR, FAR) if step == 0 else (FAR, NEAR)
    return [(2 * i + crossed, 2 * j) for i, j in keys] + [
        (2 * i + 1 - crossed, 2 * j + 1) for i, j in values
    ]


NT = (((1,), (1,)), ((), ()))
ROOM = 56 * 1024 * 1024


def rotary_table():
    halves = np.arange(0, HD, 2) / HD
    inverse = 1.0 / 500000.0**halves
    wavelen = 2.0 * np.pi / inverse
    smooth = (8192.0 / wavelen - 1.0) / 3.0
    blended = (1.0 - smooth) * inverse / 8.0 + smooth * inverse
    scaled = np.where(wavelen < 2048.0, inverse, np.where(wavelen > 8192.0, inverse / 8.0, blended))
    return jnp.asarray(scaled, dtype=jnp.float32)


def ancestry(parents):
    seg_count = parents.shape[0]
    indices = jnp.arange(seg_count, dtype=jnp.int32)
    linked = (
        (indices[:, None] == indices[None, :]) | (parents[:, None] == indices[None, :])
    ).astype(jnp.float32)
    for sweep in range(max(1, (seg_count - 1).bit_length())):
        linked = (
            jnp.dot(
                linked, linked, precision=lax.Precision.HIGHEST, preferred_element_type=jnp.float32
            )
            > 0.5
        ).astype(jnp.float32)
    return linked


def token_places(seg_row, linked):
    seg_count = linked.shape[0]
    onehot = (seg_row[:, None] == jnp.arange(seg_count, dtype=jnp.int32)[None, :]).astype(
        jnp.float32
    )
    lengths = jnp.sum(onehot, axis=0)
    starts = jnp.cumsum(lengths) - lengths
    before = jnp.sum(linked * lengths[None, :], axis=1) - lengths
    token_ids = jnp.arange(seg_row.shape[0], dtype=jnp.int32).astype(jnp.float32)
    return (
        STEM
        + token_ids
        - jnp.sum(onehot * starts[None, :], axis=1)
        + jnp.sum(onehot * before[None, :], axis=1)
    )


def turn_kernel(
    spot, q_own, k_own, v_own, q_mate, k_mate, v_mate, cos_ref, sin_ref, o_ref
):
    core = spot[1]
    pack = pl.program_id(0)

    def run(place, q_ref, k_ref, v_ref):
        cosine = cos_ref[place]
        sine = sin_ref[place]

        def turned(part):
            wide = part.astype(jnp.float32)
            return (wide * cosine + pltpu.roll(wide, HD // 2, 1) * sine).astype(jnp.bfloat16)

        for e in range(KVH):
            for head in range(2):
                at = pl.multiple_of((4 * e + head + 2 * core) * HD, HD)
                o_ref[0, e, :, head * HD : head * HD + HD] = turned(q_ref[:, pl.ds(at, HD)])
            at = e * HD
            o_ref[0, e, :, 2 * HD :] = jnp.where(
                core == 0, turned(k_ref[:, at : at + HD]), v_ref[:, at : at + HD]
            )

    @pl.when(pack == core)
    def _():
        run(0, q_own, k_own, v_own)

    @pl.when(pack != core)
    def _():
        run(1, q_mate, k_mate, v_mate)


def turn(here, own, mate, cosine, sine):
    tok = own[0].shape[0]
    whole = [pl.BlockSpec(memory_space=pltpu.VMEM)] * 6
    table = pl.BlockSpec(cosine.shape, lambda i, here: (0, 0, 0), pipeline_mode=pl.Buffered(1))
    return pl.pallas_call(
        turn_kernel,
        out_shape=jax.ShapeDtypeStruct((2, KVH, tok, 3 * HD), jnp.bfloat16),
        grid_spec=pltpu.PrefetchScalarGridSpec(
            num_scalar_prefetch=1,
            grid=(2,),
            in_specs=whole + [table, table],
            out_specs=pl.BlockSpec((1, KVH, tok, 3 * HD), lambda i, here: (i, 0, 0, 0)),
        ),
        compiler_params=pltpu.CompilerParams(vmem_limit_bytes=32 * 1024 * 1024),
        name="turn",
    )(here, *[inside(part) for part in own + mate], cosine, sine)


def held_at(x, core, group):
    chip = lax.div(group, 2)
    other = jnp.where(core == 0, near_of(x), far_of(x))
    found = jnp.where(lax.rem(group, 2) == core, 0, 2) + jnp.where(chip == x, 0, 1)
    return jnp.where((chip == x) | (chip == other), found, 4)


def near_of(x):
    return x + 1 - 2 * lax.rem(x, 2)


def far_of(x):
    return 3 - x


def relay_kernel(spot, owner, own, same, flip, cross, out, sems):
    x, core = spot[0], spot[1]
    to = jnp.where(core == 0, far_of(x), near_of(x))
    for item in range(2):
        code = held_at(x, core, owner[2 * to + item])
        for place, source in enumerate((own, same, flip, cross)):
            chosen = code == place if place else (code == 0) | (code == 4)

            @pl.when(chosen)
            def _(source=source):
                pltpu.make_async_copy(source, out.at[item], sems.at[item]).start()

    for item in range(2):
        pltpu.make_async_copy(own, out.at[item], sems.at[item]).wait()


def settle_kernel(spot, owner, own, same, flip, cross, two, out, sems):
    x, core = spot[0], spot[1]
    for pack in range(2):
        code = held_at(x, core, owner[2 * x + pack])
        for place, source in enumerate((own, same, flip, cross, two.at[pack])):

            @pl.when(code == place)
            def _(source=source):
                for e in range(KVH):
                    pltpu.make_async_copy(
                        source.at[:, pl.ds(e * HD, HD)], out.at[pack, e], sems.at[pack, e]
                    ).start()

    for pack in range(2):
        for e in range(KVH):
            pltpu.make_async_copy(
                own.at[:, pl.ds(0, HD)], out.at[pack, e], sems.at[pack, e]
            ).wait()


def inside(part):
    return pltpu.with_memory_space_constraint(part, pltpu.VMEM)


def moved(kernel, shape, sems, scalars, arrays):
    return pl.pallas_call(
        kernel,
        out_shape=jax.ShapeDtypeStruct(shape, jnp.bfloat16),
        grid_spec=pltpu.PrefetchScalarGridSpec(
            num_scalar_prefetch=len(scalars),
            grid=(1,),
            in_specs=[pl.BlockSpec(memory_space=pltpu.VMEM)] * len(arrays),
            out_specs=pl.BlockSpec(memory_space=pl.ANY),
            scratch_shapes=[pltpu.SemaphoreType.DMA(sems)],
        ),
        compiler_params=pltpu.CompilerParams(vmem_limit_bytes=16 * 1024 * 1024),
        name=kernel.__name__,
    )(*scalars, *[inside(part) for part in arrays])


def flipped_dot(left, right):
    return lax.dot_general(left, right, NT, preferred_element_type=jnp.float32)


def fill(core, mine_ref, other_ref, ka, vt, top):
    first = core == 0
    best = jnp.zeros((8, BQ), jnp.float32)
    for at in range(0, mine_ref.shape[0], BQ):
        mine = mine_ref[at : at + BQ, :]
        other = other_ref[at : at + BQ, :]
        key = jnp.where(first, mine, other)
        ka[at : at + BQ, :HD] = key
        vt[:HD, at : at + BQ] = jnp.where(first, other, mine).T
        wide = key.astype(jnp.float32)
        squares = (wide * wide).astype(jnp.bfloat16)
        best = jnp.maximum(best, flipped_dot(jnp.ones((8, HD), jnp.bfloat16), squares))
    vt[HD:, :] = jnp.ones_like(vt[HD:, :])
    longest = jnp.max(jnp.max(best, axis=1, keepdims=True), axis=0, keepdims=True)
    top[...] = jnp.broadcast_to(jnp.sqrt(longest), (8, HD))


def stacked(ref):
    return jnp.concatenate([ref[:, :HD], ref[:, HD : 2 * HD]], axis=0)


def ceiling(rows, top):
    wide = rows.astype(jnp.float32)
    squares = (wide * wide).astype(jnp.bfloat16)
    norms = jnp.dot(squares, jnp.ones((HD, HD), jnp.bfloat16), preferred_element_type=jnp.float32)
    return jnp.sqrt(norms) * top * 1.02 - SHIFT


def shift_row(qa):
    pick = lax.broadcasted_iota(jnp.int32, (8, 2 * HD), 1) == HD + SEGS
    return flipped_dot(pick.astype(jnp.float32).astype(jnp.bfloat16), qa[...])


def down(row):
    return jnp.broadcast_to(row, (HD, row.shape[1])).T


def pack_kernel(
    core, seen, q_ref, mine_ref, other_ref, qb_ref, kb_ref, o_ref, qa, ka, vt, top, acc
):
    qi = pl.program_id(0)
    rows = 2 * BQ
    lane = lax.broadcasted_iota(jnp.int32, (1, HD), 1)

    @pl.when(qi == 0)
    def _():
        fill(core[0], mine_ref, other_ref, ka, vt, top)
        ka[:, HD:] = kb_ref[...]

    q_rows = stacked(q_ref)
    qa[:, :HD] = q_rows
    side = jnp.concatenate([qb_ref[...], qb_ref[...]], axis=0).astype(jnp.float32)
    query = lax.broadcasted_iota(jnp.int32, (BQ, rows), 1)
    ahead = lax.broadcasted_iota(jnp.int32, (BQ, rows), 0) > jnp.where(
        query >= BQ, query - BQ, query
    )
    here = pl.multiple_of(qi * BQ, BQ)

    def scores(at):
        return flipped_dot(ka[pl.ds(at, BQ), :], qa[...])

    def mixed(at, weights):
        return jnp.dot(
            vt[:, pl.ds(at, BQ)],
            weights.astype(jnp.bfloat16),
            preferred_element_type=jnp.float32,
        )

    def run(shift):
        qa[:, HD:] = jnp.where(lane == SEGS, shift, side).astype(jnp.bfloat16)
        acc[...] = mixed(here, jnp.where(ahead, 0.0, jnp.exp2(scores(here) * SCALE)))

        def body(kj, carry):
            @pl.when(seen[qi, kj] > 0)
            def _():
                at = pl.multiple_of(kj * BQ, BQ)
                acc[...] += mixed(at, jnp.exp2(scores(at) * SCALE))

            return carry

        lax.fori_loop(0, qi, body, 0)
        o_ref[0, : HD + 8] = acc[...]
        o_ref[0, HD + 8 :] = shift_row(qa)

    run(ceiling(q_rows, top[0:1, 0:1]))

    @pl.when(jnp.min(acc[HD:, :]) < TINY)
    def _():
        qa[:, HD:] = side.astype(jnp.bfloat16)
        most = jnp.max(jnp.where(ahead, BARRED, scores(here)), axis=0, keepdims=True)

        def body(kj, most):
            part = scores(pl.multiple_of(kj * BQ, BQ))
            return jnp.maximum(most, jnp.max(part, axis=0, keepdims=True))

        run(down(lax.fori_loop(0, qi, body, most)))


def pack_part(core, seen, arrived, other, q_side, k_side):
    pack = arrived.shape[0]
    once = dict(pipeline_mode=pl.Buffered(1))
    return pl.pallas_call(
        pack_kernel,
        out_shape=jax.ShapeDtypeStruct((pack // BQ, HD + 16, 2 * BQ), jnp.float32),
        grid_spec=pltpu.PrefetchScalarGridSpec(
            num_scalar_prefetch=2,
            grid=(pack // BQ,),
            in_specs=[
                pl.BlockSpec((BQ, 2 * HD), lambda i, *_: (i, 0)),
                pl.BlockSpec((pack, HD), lambda i, *_: (0, 2), **once),
                pl.BlockSpec((pack, HD), lambda i, *_: (0, 0), **once),
                pl.BlockSpec((BQ, HD), lambda i, *_: (i, 0)),
                pl.BlockSpec((pack, HD), lambda i, *_: (0, 0), **once),
            ],
            out_specs=pl.BlockSpec((1, HD + 16, 2 * BQ), lambda i, *_: (i, 0, 0)),
            scratch_shapes=[
                pltpu.VMEM((2 * BQ, 2 * HD), jnp.bfloat16),
                pltpu.VMEM((pack, 2 * HD), jnp.bfloat16),
                pltpu.VMEM((HD + 8, pack), jnp.bfloat16),
                pltpu.VMEM((8, HD), jnp.float32),
                pltpu.VMEM((HD + 8, 2 * BQ), jnp.float32),
            ],
        ),
        compiler_params=pltpu.CompilerParams(vmem_limit_bytes=ROOM),
        cost_estimate=pl.CostEstimate(
            flops=8 * pack * pack * HD, bytes_accessed=8 << 20, transcendentals=pack * pack
        ),
        name="pack_part",
    )(core, seen, arrived, arrived, other, q_side, k_side)


def stem_kernel(core, q_ref, mine_ref, other_ref, part_ref, o_ref, qa, ka, vt, top, acc):
    stem = ka.shape[0]
    lane = lax.broadcasted_iota(jnp.int32, (1, HD), 1)
    side = jnp.broadcast_to(jnp.where(lane == SEGS, -1.0, 0.0).astype(jnp.bfloat16), (CK, HD))

    @pl.when(pl.program_id(0) == 0)
    def _():
        fill(core[0], mine_ref, other_ref, ka, vt, top)

    q_rows = stacked(q_ref)
    qa[:, :HD] = q_rows

    def scores(at):
        return flipped_dot(jnp.concatenate([ka[pl.ds(at, CK), :], side], axis=1), qa[...])

    def run(shift):
        qa[:, HD:] = jnp.where(lane == SEGS, shift, 0.0).astype(jnp.bfloat16)
        total, weights = None, []
        held = scores(0)
        for at in range(0, stem, CK):
            ahead = scores(at + CK) if at + CK < stem else None
            weights.append(jnp.exp2(held * SCALE).astype(jnp.bfloat16))
            if len(weights) * CK == WIDE:
                part = jnp.dot(
                    vt[:, at + CK - WIDE : at + CK],
                    jnp.concatenate(weights, axis=0),
                    preferred_element_type=jnp.float32,
                )
                total = part if total is None else total + part
                weights = []
            held = ahead
        acc[...] = total

    def finish():
        shift = shift_row(qa)[:1]
        before = part_ref[0, HD + 8 : HD + 9]
        most = jnp.maximum(shift, before)
        new = jnp.exp2((shift - most) * SCALE)
        old = jnp.exp2((before - most) * SCALE)
        total = acc[HD : HD + 1] * new + part_ref[0, HD : HD + 1] * old
        out = (acc[:HD] * (new / total) + part_ref[0, :HD] * (old / total)).T
        o_ref[:, :HD] = out[:BQ].astype(jnp.bfloat16)
        o_ref[:, HD:] = out[BQ:].astype(jnp.bfloat16)

    run(ceiling(q_rows, top[0:1, 0:1]))
    finish()

    @pl.when(jnp.min(acc[HD:, :]) < TINY)
    def _():
        qa[:, HD:] = jnp.zeros_like(q_rows)

        def body(step, most):
            part = scores(pl.multiple_of(step * CK, CK))
            return jnp.maximum(most, jnp.max(part, axis=0, keepdims=True))

        low = jnp.full((1, 2 * BQ), BARRED, jnp.float32)
        run(down(lax.fori_loop(0, stem // CK, body, low)))
        finish()


def stem_part(core, arrived, mine, other, before):
    pack = arrived.shape[0]
    stem = mine.shape[0]
    return pl.pallas_call(
        stem_kernel,
        out_shape=jax.ShapeDtypeStruct((pack, 2 * HD), jnp.bfloat16),
        grid_spec=pltpu.PrefetchScalarGridSpec(
            num_scalar_prefetch=1,
            grid=(pack // BQ,),
            in_specs=[
                pl.BlockSpec((BQ, 2 * HD), lambda i, *_: (i, 0)),
                pl.BlockSpec(memory_space=pltpu.VMEM),
                pl.BlockSpec(memory_space=pltpu.VMEM),
                pl.BlockSpec((1, HD + 16, 2 * BQ), lambda i, *_: (i, 0, 0)),
            ],
            out_specs=pl.BlockSpec((BQ, 2 * HD), lambda i, *_: (i, 0)),
            scratch_shapes=[
                pltpu.VMEM((2 * BQ, 2 * HD), jnp.bfloat16),
                pltpu.VMEM((stem, HD), jnp.bfloat16),
                pltpu.VMEM((HD + 8, stem), jnp.bfloat16),
                pltpu.VMEM((8, HD), jnp.float32),
                pltpu.VMEM((HD + 8, 2 * BQ), jnp.float32),
            ],
        ),
        compiler_params=pltpu.CompilerParams(vmem_limit_bytes=48 * 1024 * 1024),
        cost_estimate=pl.CostEstimate(
            flops=8 * pack * stem * HD, bytes_accessed=8 << 20, transcendentals=2 * pack * stem
        ),
        name="stem_part",
    )(core, arrived, inside(mine), inside(other), before)


def gather_kernel(core, mine_ref, other_ref, o_ref):
    step = pl.program_id(0)
    heads = KVH // 2
    first = core[0] == 0
    for e in range(heads):
        own, got = mine_ref[core[0], step * heads + e], other_ref[step * heads + e]
        at = 4 * HD * e
        o_ref[:, at : at + 2 * HD] = jnp.where(first, own, got)
        o_ref[:, at + 2 * HD : at + 4 * HD] = jnp.where(first, got, own)


def gather(core, mine, other):
    tok = mine.shape[2]
    whole = pl.BlockSpec(memory_space=pltpu.VMEM)
    return pl.pallas_call(
        gather_kernel,
        out_shape=jax.ShapeDtypeStruct((tok, H * HD), jnp.bfloat16),
        grid_spec=pltpu.PrefetchScalarGridSpec(
            num_scalar_prefetch=1,
            grid=(2,),
            in_specs=[whole, whole],
            out_specs=pl.BlockSpec((tok, H * HD // 2), lambda i, core: (0, i)),
        ),
        name="gather",
    )(core, inside(mine), inside(other))


def shards(queries, keys, values, stem_kv, seg_ids, seg_parent, stem_owner):
    tok = queries.shape[1]
    x = lax.axis_index("x")
    core = lax.axis_index("core")
    spot = lax.axis_index(SEQ)
    pack_len = tok * 16
    core_row = core[None].astype(jnp.int32)
    here = jnp.stack([x, core]).astype(jnp.int32)

    raw = (queries[0], keys[0], values[0])
    rows = jnp.concatenate([seg_ids[0], seg_parent[0]])
    rows_mate = lax.ppermute(rows, "core", FLIP)
    raw_mate = tuple(lax.ppermute(part, "core", FLIP) for part in raw)

    stem = stem_kv[0]
    own = lax.dynamic_index_in_dim(stem, core, 0, keepdims=False)
    given = lax.dynamic_index_in_dim(stem, 1 - core, 0, keepdims=False)
    same = lax.ppermute(own, ("x", "core"), joint(0, 0))
    cross = lax.ppermute(given, ("x", "core"), joint(0, 1))
    flip = lax.ppermute(given, "core", FLIP)

    both = jnp.stack([rows, rows_mate])
    linked = jax.vmap(ancestry)(both[:, pack_len:])
    places = jax.vmap(token_places)(both[:, :pack_len], linked)
    places = lax.dynamic_slice_in_dim(places, spot * tok, tok, axis=1)
    angles = places[:, :, None] * rotary_table()[None, None, :]
    cosine, sine = jnp.cos(angles), jnp.sin(angles)
    sent = turn(
        here,
        raw,
        raw_mate,
        jnp.concatenate([cosine, cosine], axis=2),
        jnp.concatenate([-sine, sine], axis=2),
    )
    arrived = lax.all_to_all(
        sent.reshape(16, tok, 3 * HD), SEQ, split_axis=0, concat_axis=0, tiled=True
    ).reshape(pack_len, 3 * HD)
    same, cross, flip, sent = lax.optimization_barrier((same, cross, flip, sent))

    held = (own, same, flip, cross)
    wanted = moved(relay_kernel, stem.shape, (2,), (here, stem_owner), held)
    two = lax.ppermute(wanted, ("x", "core"), joint(1, 0))
    both, linked, _ = lax.optimization_barrier((both, linked, wanted))
    pair = lax.ppermute(arrived[:, 2 * HD :], "core", FLIP)

    ours = spot // KVH == core
    seg_row = jnp.where(ours, both[0, :pack_len], both[1, :pack_len])
    reach = jnp.where(ours, linked[0], linked[1])
    onehot = (seg_row[:, None] == jnp.arange(HD, dtype=jnp.int32)[None, :]).astype(jnp.float32)
    barred = jnp.pad(BARRED * (1.0 - reach), ((0, HD - SEGS), (0, HD - SEGS)))
    q_side = jnp.dot(onehot, barred, precision=lax.Precision.HIGHEST).astype(jnp.bfloat16)
    k_side = jnp.where(jnp.arange(HD)[None, :] == SEGS, -1.0, onehot).astype(jnp.bfloat16)
    q_has = onehot.reshape(pack_len // BQ, BQ, HD).max(axis=1)[:, :SEGS]
    seen = (q_has @ reach @ q_has.T > 0.5).astype(jnp.int32)

    stems = moved(
        settle_kernel,
        (2, KVH, stem.shape[1], HD),
        (2, KVH),
        (here, stem_owner),
        held + (two,),
    ).reshape(16, stem.shape[1], HD)
    mine = lax.all_to_all(stems, SEQ, split_axis=0, concat_axis=0, tiled=True).reshape(STEM, HD)
    arrived, pair, _ = lax.optimization_barrier((arrived, pair, stems))
    partial = pack_part(core_row, seen, arrived, pair, q_side, k_side)
    mine, partial = lax.optimization_barrier((mine, partial))
    other = lax.ppermute(mine, "core", FLIP)
    mixed = stem_part(core_row, arrived, mine, other, partial)

    back = lax.all_to_all(
        mixed.reshape(16, tok, 2 * HD), SEQ, split_axis=0, concat_axis=0, tiled=True
    ).reshape(2, KVH, tok, 2 * HD)
    away = lax.dynamic_index_in_dim(back, 1 - core, 0, keepdims=False)
    return gather(core_row, back, lax.ppermute(away, "core", FLIP))[None]


def solution(mesh):
    grid = Mesh(mesh.devices.reshape(4, 2, 4, 4), ("x", "core", "z", "y"))
    dp, seq = ("x", "core"), SEQ
    placed = (
        P(dp, seq, None),
        P(dp, seq, None),
        P(dp, seq, None),
        P(dp, None, seq, None),
        P(dp, None),
        P(dp, None),
        P(),
    )
    return jax.shard_map(
        shards, mesh=grid, in_specs=placed, out_specs=P(dp, seq, None), check_vma=False
    )
```

```python
import math

import jax
import jax.numpy as jnp
import numpy as np
from jax import lax
from jax.experimental import pallas as pl
from jax.experimental.pallas import tpu as pltpu
from jax.sharding import Mesh
from jax.sharding import PartitionSpec as P

H = 32
KVH = 8
HD = 128
STEM = 4096
SEGS = 16
BARRED = -1e30
BQ = 512
CK = 256
WIDE = 1024
SCALE = HD**-0.5 * math.log2(math.e)
SHIFT = 70.0 / SCALE
TINY = 2.0**-16
FLIP = [(0, 1), (1, 0)]
NEAR = [(0, 1), (1, 0), (2, 3), (3, 2)]
FAR = [(0, 3), (3, 0), (1, 2), (2, 1)]
SEQ = ("z", "y")


def joint(step, crossed):
    keys, values = (NEAR, FAR) if step == 0 else (FAR, NEAR)
    return [(2 * i + crossed, 2 * j) for i, j in keys] + [
        (2 * i + 1 - crossed, 2 * j + 1) for i, j in values
    ]


NT = (((1,), (1,)), ((), ()))
ROOM = 56 * 1024 * 1024


def rotary_table():
    halves = np.arange(0, HD, 2) / HD
    inverse = 1.0 / 500000.0**halves
    wavelen = 2.0 * np.pi / inverse
    smooth = (8192.0 / wavelen - 1.0) / 3.0
    blended = (1.0 - smooth) * inverse / 8.0 + smooth * inverse
    scaled = np.where(wavelen < 2048.0, inverse, np.where(wavelen > 8192.0, inverse / 8.0, blended))
    return jnp.asarray(scaled, dtype=jnp.float32)


def ancestry(parents):
    seg_count = parents.shape[0]
    indices = jnp.arange(seg_count, dtype=jnp.int32)
    linked = (
        (indices[:, None] == indices[None, :]) | (parents[:, None] == indices[None, :])
    ).astype(jnp.float32)
    for sweep in range(max(1, (seg_count - 1).bit_length())):
        linked = (
            jnp.dot(
                linked, linked, precision=lax.Precision.HIGHEST, preferred_element_type=jnp.float32
            )
            > 0.5
        ).astype(jnp.float32)
    return linked


def token_places(seg_row, linked):
    seg_count = linked.shape[0]
    onehot = (seg_row[:, None] == jnp.arange(seg_count, dtype=jnp.int32)[None, :]).astype(
        jnp.float32
    )
    lengths = jnp.sum(onehot, axis=0)
    starts = jnp.cumsum(lengths) - lengths
    before = jnp.sum(linked * lengths[None, :], axis=1) - lengths
    token_ids = jnp.arange(seg_row.shape[0], dtype=jnp.int32).astype(jnp.float32)
    return (
        STEM
        + token_ids
        - jnp.sum(onehot * starts[None, :], axis=1)
        + jnp.sum(onehot * before[None, :], axis=1)
    )


def turn_kernel(
    spot, q_own, k_own, v_own, q_mate, k_mate, v_mate, cos_ref, sin_ref, o_ref
):
    core = spot[1]
    pack = pl.program_id(0)

    def run(place, q_ref, k_ref, v_ref):
        cosine = cos_ref[place]
        sine = sin_ref[place]

        def turned(part):
            wide = part.astype(jnp.float32)
            return (wide * cosine + pltpu.roll(wide, HD // 2, 1) * sine).astype(jnp.bfloat16)

        for e in range(KVH):
            for head in range(2):
                at = pl.multiple_of((4 * e + head + 2 * core) * HD, HD)
                o_ref[0, e, :, head * HD : head * HD + HD] = turned(q_ref[:, pl.ds(at, HD)])
            at = e * HD
            o_ref[0, e, :, 2 * HD :] = jnp.where(
                core == 0, turned(k_ref[:, at : at + HD]), v_ref[:, at : at + HD]
            )

    @pl.when(pack == core)
    def _():
        run(0, q_own, k_own, v_own)

    @pl.when(pack != core)
    def _():
        run(1, q_mate, k_mate, v_mate)


def turn(here, own, mate, cosine, sine):
    tok = own[0].shape[0]
    whole = [
        pl.BlockSpec(part.shape, lambda i, here: (0, 0), pipeline_mode=pl.Buffered(1))
        for part in own + mate
    ]
    table = pl.BlockSpec(cosine.shape, lambda i, here: (0, 0, 0), pipeline_mode=pl.Buffered(1))
    return pl.pallas_call(
        turn_kernel,
        out_shape=jax.ShapeDtypeStruct((2, KVH, tok, 3 * HD), jnp.bfloat16),
        grid_spec=pltpu.PrefetchScalarGridSpec(
            num_scalar_prefetch=1,
            grid=(2,),
            in_specs=whole + [table, table],
            out_specs=pl.BlockSpec((1, KVH, tok, 3 * HD), lambda i, here: (i, 0, 0, 0)),
        ),
        compiler_params=pltpu.CompilerParams(vmem_limit_bytes=32 * 1024 * 1024),
        name="turn",
    )(here, *own, *mate, cosine, sine)


def held_at(x, core, group):
    chip = lax.div(group, 2)
    other = jnp.where(core == 0, near_of(x), far_of(x))
    found = jnp.where(lax.rem(group, 2) == core, 0, 2) + jnp.where(chip == x, 0, 1)
    return jnp.where((chip == x) | (chip == other), found, 4)


def near_of(x):
    return x + 1 - 2 * lax.rem(x, 2)


def far_of(x):
    return 3 - x


def relay_kernel(spot, owner, own, same, flip, cross, out, sems):
    x, core = spot[0], spot[1]
    to = jnp.where(core == 0, far_of(x), near_of(x))
    for item in range(2):
        code = held_at(x, core, owner[2 * to + item])
        for place, source in enumerate((own, same, flip, cross)):
            chosen = code == place if place else (code == 0) | (code == 4)

            @pl.when(chosen)
            def _(source=source):
                pltpu.make_async_copy(source, out.at[item], sems.at[item]).start()

    for item in range(2):
        pltpu.make_async_copy(own, out.at[item], sems.at[item]).wait()


def settle_kernel(spot, owner, own, same, flip, cross, two, out, sems):
    x, core = spot[0], spot[1]
    for pack in range(2):
        code = held_at(x, core, owner[2 * x + pack])
        for place, source in enumerate((own, same, flip, cross, two.at[pack])):

            @pl.when(code == place)
            def _(source=source):
                for e in range(KVH):
                    pltpu.make_async_copy(
                        source.at[:, pl.ds(e * HD, HD)], out.at[pack, e], sems.at[pack, e]
                    ).start()

    for pack in range(2):
        for e in range(KVH):
            pltpu.make_async_copy(
                own.at[:, pl.ds(0, HD)], out.at[pack, e], sems.at[pack, e]
            ).wait()


def inside(part):
    return pltpu.with_memory_space_constraint(part, pltpu.VMEM)


def moved(kernel, shape, sems, scalars, arrays):
    return pl.pallas_call(
        kernel,
        out_shape=jax.ShapeDtypeStruct(shape, jnp.bfloat16),
        grid_spec=pltpu.PrefetchScalarGridSpec(
            num_scalar_prefetch=len(scalars),
            grid=(1,),
            in_specs=[pl.BlockSpec(memory_space=pltpu.VMEM)] * len(arrays),
            out_specs=pl.BlockSpec(memory_space=pl.ANY),
            scratch_shapes=[pltpu.SemaphoreType.DMA(sems)],
        ),
        compiler_params=pltpu.CompilerParams(vmem_limit_bytes=16 * 1024 * 1024),
        name=kernel.__name__,
    )(*scalars, *[inside(part) for part in arrays])


def flipped_dot(left, right):
    return lax.dot_general(left, right, NT, preferred_element_type=jnp.float32)


def fill(core, mine_ref, other_ref, ka, vt, top):
    first = core == 0
    best = jnp.zeros((8, BQ), jnp.float32)
    for at in range(0, mine_ref.shape[0], BQ):
        mine = mine_ref[at : at + BQ, :]
        other = other_ref[at : at + BQ, :]
        key = jnp.where(first, mine, other)
        ka[at : at + BQ, :HD] = key
        vt[:HD, at : at + BQ] = jnp.where(first, other, mine).T
        wide = key.astype(jnp.float32)
        squares = (wide * wide).astype(jnp.bfloat16)
        best = jnp.maximum(best, flipped_dot(jnp.ones((8, HD), jnp.bfloat16), squares))
    vt[HD:, :] = jnp.ones_like(vt[HD:, :])
    longest = jnp.max(jnp.max(best, axis=1, keepdims=True), axis=0, keepdims=True)
    top[...] = jnp.broadcast_to(jnp.sqrt(longest), (8, HD))


def stacked(ref):
    return jnp.concatenate([ref[:, :HD], ref[:, HD : 2 * HD]], axis=0)


def ceiling(rows, top):
    wide = rows.astype(jnp.float32)
    squares = (wide * wide).astype(jnp.bfloat16)
    norms = jnp.dot(squares, jnp.ones((HD, HD), jnp.bfloat16), preferred_element_type=jnp.float32)
    return jnp.sqrt(norms) * top * 1.02 - SHIFT


def shift_row(qa):
    pick = lax.broadcasted_iota(jnp.int32, (8, 2 * HD), 1) == HD + SEGS
    return flipped_dot(pick.astype(jnp.float32).astype(jnp.bfloat16), qa[...])


def down(row):
    return jnp.broadcast_to(row, (HD, row.shape[1])).T


def pack_kernel(
    core, seen, q_ref, mine_ref, other_ref, qb_ref, kb_ref, o_ref, qa, ka, vt, top, acc
):
    qi = pl.program_id(0)
    rows = 2 * BQ
    lane = lax.broadcasted_iota(jnp.int32, (1, HD), 1)

    @pl.when(qi == 0)
    def _():
        fill(core[0], mine_ref, other_ref, ka, vt, top)
        ka[:, HD:] = kb_ref[...]

    q_rows = stacked(q_ref)
    qa[:, :HD] = q_rows
    side = jnp.concatenate([qb_ref[...], qb_ref[...]], axis=0).astype(jnp.float32)
    query = lax.broadcasted_iota(jnp.int32, (BQ, rows), 1)
    ahead = lax.broadcasted_iota(jnp.int32, (BQ, rows), 0) > jnp.where(
        query >= BQ, query - BQ, query
    )
    here = pl.multiple_of(qi * BQ, BQ)

    def scores(at):
        return flipped_dot(ka[pl.ds(at, BQ), :], qa[...])

    def mixed(at, weights):
        return jnp.dot(
            vt[:, pl.ds(at, BQ)],
            weights.astype(jnp.bfloat16),
            preferred_element_type=jnp.float32,
        )

    def run(shift):
        qa[:, HD:] = jnp.where(lane == SEGS, shift, side).astype(jnp.bfloat16)
        acc[...] = mixed(here, jnp.where(ahead, 0.0, jnp.exp2(scores(here) * SCALE)))

        def body(kj, carry):
            @pl.when(seen[qi, kj] > 0)
            def _():
                at = pl.multiple_of(kj * BQ, BQ)
                acc[...] += mixed(at, jnp.exp2(scores(at) * SCALE))

            return carry

        lax.fori_loop(0, qi, body, 0)
        o_ref[0, : HD + 8] = acc[...]
        o_ref[0, HD + 8 :] = shift_row(qa)

    run(ceiling(q_rows, top[0:1, 0:1]))

    @pl.when(jnp.min(acc[HD:, :]) < TINY)
    def _():
        qa[:, HD:] = side.astype(jnp.bfloat16)
        most = jnp.max(jnp.where(ahead, BARRED, scores(here)), axis=0, keepdims=True)

        def body(kj, most):
            part = scores(pl.multiple_of(kj * BQ, BQ))
            return jnp.maximum(most, jnp.max(part, axis=0, keepdims=True))

        run(down(lax.fori_loop(0, qi, body, most)))


def pack_part(core, seen, arrived, other, q_side, k_side):
    pack = arrived.shape[0]
    once = dict(pipeline_mode=pl.Buffered(1))
    return pl.pallas_call(
        pack_kernel,
        out_shape=jax.ShapeDtypeStruct((pack // BQ, HD + 16, 2 * BQ), jnp.float32),
        grid_spec=pltpu.PrefetchScalarGridSpec(
            num_scalar_prefetch=2,
            grid=(pack // BQ,),
            in_specs=[
                pl.BlockSpec((BQ, 2 * HD), lambda i, *_: (i, 0)),
                pl.BlockSpec((pack, HD), lambda i, *_: (0, 2), **once),
                pl.BlockSpec((pack, HD), lambda i, *_: (0, 0), **once),
                pl.BlockSpec((BQ, HD), lambda i, *_: (i, 0)),
                pl.BlockSpec((pack, HD), lambda i, *_: (0, 0), **once),
            ],
            out_specs=pl.BlockSpec((1, HD + 16, 2 * BQ), lambda i, *_: (i, 0, 0)),
            scratch_shapes=[
                pltpu.VMEM((2 * BQ, 2 * HD), jnp.bfloat16),
                pltpu.VMEM((pack, 2 * HD), jnp.bfloat16),
                pltpu.VMEM((HD + 8, pack), jnp.bfloat16),
                pltpu.VMEM((8, HD), jnp.float32),
                pltpu.VMEM((HD + 8, 2 * BQ), jnp.float32),
            ],
        ),
        compiler_params=pltpu.CompilerParams(vmem_limit_bytes=ROOM),
        cost_estimate=pl.CostEstimate(
            flops=8 * pack * pack * HD, bytes_accessed=8 << 20, transcendentals=pack * pack
        ),
        name="pack_part",
    )(core, seen, arrived, arrived, other, q_side, k_side)


def stem_kernel(core, q_ref, mine_ref, other_ref, part_ref, o_ref, qa, ka, vt, top, acc):
    stem = ka.shape[0]
    lane = lax.broadcasted_iota(jnp.int32, (1, HD), 1)
    side = jnp.broadcast_to(jnp.where(lane == SEGS, -1.0, 0.0).astype(jnp.bfloat16), (CK, HD))

    @pl.when(pl.program_id(0) == 0)
    def _():
        fill(core[0], mine_ref, other_ref, ka, vt, top)

    q_rows = stacked(q_ref)
    qa[:, :HD] = q_rows

    def scores(at):
        return flipped_dot(jnp.concatenate([ka[pl.ds(at, CK), :], side], axis=1), qa[...])

    def run(shift):
        qa[:, HD:] = jnp.where(lane == SEGS, shift, 0.0).astype(jnp.bfloat16)
        total, weights = None, []
        held = scores(0)
        for at in range(0, stem, CK):
            ahead = scores(at + CK) if at + CK < stem else None
            weights.append(jnp.exp2(held * SCALE).astype(jnp.bfloat16))
            if len(weights) * CK == WIDE:
                part = jnp.dot(
                    vt[:, at + CK - WIDE : at + CK],
                    jnp.concatenate(weights, axis=0),
                    preferred_element_type=jnp.float32,
                )
                total = part if total is None else total + part
                weights = []
            held = ahead
        acc[...] = total

    def finish():
        shift = shift_row(qa)[:1]
        before = part_ref[0, HD + 8 : HD + 9]
        most = jnp.maximum(shift, before)
        new = jnp.exp2((shift - most) * SCALE)
        old = jnp.exp2((before - most) * SCALE)
        total = acc[HD : HD + 1] * new + part_ref[0, HD : HD + 1] * old
        out = (acc[:HD] * (new / total) + part_ref[0, :HD] * (old / total)).T
        o_ref[:, :HD] = out[:BQ].astype(jnp.bfloat16)
        o_ref[:, HD:] = out[BQ:].astype(jnp.bfloat16)

    run(ceiling(q_rows, top[0:1, 0:1]))
    finish()

    @pl.when(jnp.min(acc[HD:, :]) < TINY)
    def _():
        qa[:, HD:] = jnp.zeros_like(q_rows)

        def body(step, most):
            part = scores(pl.multiple_of(step * CK, CK))
            return jnp.maximum(most, jnp.max(part, axis=0, keepdims=True))

        low = jnp.full((1, 2 * BQ), BARRED, jnp.float32)
        run(down(lax.fori_loop(0, stem // CK, body, low)))
        finish()


def stem_part(core, arrived, mine, other, before):
    pack = arrived.shape[0]
    stem = mine.shape[0]
    return pl.pallas_call(
        stem_kernel,
        out_shape=jax.ShapeDtypeStruct((pack, 2 * HD), jnp.bfloat16),
        grid_spec=pltpu.PrefetchScalarGridSpec(
            num_scalar_prefetch=1,
            grid=(pack // BQ,),
            in_specs=[
                pl.BlockSpec((BQ, 2 * HD), lambda i, *_: (i, 0)),
                pl.BlockSpec(memory_space=pltpu.VMEM),
                pl.BlockSpec(memory_space=pltpu.VMEM),
                pl.BlockSpec((1, HD + 16, 2 * BQ), lambda i, *_: (i, 0, 0)),
            ],
            out_specs=pl.BlockSpec((BQ, 2 * HD), lambda i, *_: (i, 0)),
            scratch_shapes=[
                pltpu.VMEM((2 * BQ, 2 * HD), jnp.bfloat16),
                pltpu.VMEM((stem, HD), jnp.bfloat16),
                pltpu.VMEM((HD + 8, stem), jnp.bfloat16),
                pltpu.VMEM((8, HD), jnp.float32),
                pltpu.VMEM((HD + 8, 2 * BQ), jnp.float32),
            ],
        ),
        compiler_params=pltpu.CompilerParams(vmem_limit_bytes=48 * 1024 * 1024),
        cost_estimate=pl.CostEstimate(
            flops=8 * pack * stem * HD, bytes_accessed=8 << 20, transcendentals=2 * pack * stem
        ),
        name="stem_part",
    )(core, arrived, inside(mine), inside(other), before)


def gather_kernel(core, mine_ref, other_ref, o_ref):
    step = pl.program_id(0)
    heads = KVH // 2
    first = core[0] == 0
    for e in range(heads):
        own, got = mine_ref[core[0], step * heads + e], other_ref[step * heads + e]
        at = 4 * HD * e
        o_ref[:, at : at + 2 * HD] = jnp.where(first, own, got)
        o_ref[:, at + 2 * HD : at + 4 * HD] = jnp.where(first, got, own)


def gather(core, mine, other):
    tok = mine.shape[2]
    whole = pl.BlockSpec(memory_space=pltpu.VMEM)
    return pl.pallas_call(
        gather_kernel,
        out_shape=jax.ShapeDtypeStruct((tok, H * HD), jnp.bfloat16),
        grid_spec=pltpu.PrefetchScalarGridSpec(
            num_scalar_prefetch=1,
            grid=(2,),
            in_specs=[whole, whole],
            out_specs=pl.BlockSpec((tok, H * HD // 2), lambda i, core: (0, i)),
        ),
        name="gather",
    )(core, inside(mine), inside(other))


def shards(queries, keys, values, stem_kv, seg_ids, seg_parent, stem_owner):
    tok = queries.shape[1]
    x = lax.axis_index("x")
    core = lax.axis_index("core")
    spot = lax.axis_index(SEQ)
    pack_len = tok * 16
    core_row = core[None].astype(jnp.int32)
    here = jnp.stack([x, core]).astype(jnp.int32)

    raw = (queries[0], keys[0], values[0])
    rows = jnp.concatenate([seg_ids[0], seg_parent[0]])
    rows_mate = lax.ppermute(rows, "core", FLIP)
    raw_mate = tuple(lax.ppermute(part, "core", FLIP) for part in raw)

    stem = stem_kv[0]
    own = lax.dynamic_index_in_dim(stem, core, 0, keepdims=False)
    given = lax.dynamic_index_in_dim(stem, 1 - core, 0, keepdims=False)
    same = lax.ppermute(own, ("x", "core"), joint(0, 0))
    cross = lax.ppermute(given, ("x", "core"), joint(0, 1))
    flip = lax.ppermute(given, "core", FLIP)

    both = jnp.stack([rows, rows_mate])
    linked = jax.vmap(ancestry)(both[:, pack_len:])
    places = jax.vmap(token_places)(both[:, :pack_len], linked)
    places = lax.dynamic_slice_in_dim(places, spot * tok, tok, axis=1)
    angles = places[:, :, None] * rotary_table()[None, None, :]
    cosine, sine = jnp.cos(angles), jnp.sin(angles)
    sent = turn(
        here,
        raw,
        raw_mate,
        jnp.concatenate([cosine, cosine], axis=2),
        jnp.concatenate([-sine, sine], axis=2),
    )
    arrived = lax.all_to_all(
        sent.reshape(16, tok, 3 * HD), SEQ, split_axis=0, concat_axis=0, tiled=True
    ).reshape(pack_len, 3 * HD)
    same, cross, flip, sent = lax.optimization_barrier((same, cross, flip, sent))

    held = (own, same, flip, cross)
    wanted = moved(relay_kernel, stem.shape, (2,), (here, stem_owner), held)
    two = lax.ppermute(wanted, ("x", "core"), joint(1, 0))
    both, linked, _ = lax.optimization_barrier((both, linked, wanted))
    pair = lax.ppermute(arrived[:, 2 * HD :], "core", FLIP)

    ours = spot // KVH == core
    seg_row = jnp.where(ours, both[0, :pack_len], both[1, :pack_len])
    reach = jnp.where(ours, linked[0], linked[1])
    onehot = (seg_row[:, None] == jnp.arange(HD, dtype=jnp.int32)[None, :]).astype(jnp.float32)
    barred = jnp.pad(BARRED * (1.0 - reach), ((0, HD - SEGS), (0, HD - SEGS)))
    q_side = jnp.dot(onehot, barred, precision=lax.Precision.HIGHEST).astype(jnp.bfloat16)
    k_side = jnp.where(jnp.arange(HD)[None, :] == SEGS, -1.0, onehot).astype(jnp.bfloat16)
    q_has = onehot.reshape(pack_len // BQ, BQ, HD).max(axis=1)[:, :SEGS]
    seen = (q_has @ reach @ q_has.T > 0.5).astype(jnp.int32)

    stems = moved(
        settle_kernel,
        (2, KVH, stem.shape[1], HD),
        (2, KVH),
        (here, stem_owner),
        held + (two,),
    ).reshape(16, stem.shape[1], HD)
    mine = lax.all_to_all(stems, SEQ, split_axis=0, concat_axis=0, tiled=True).reshape(STEM, HD)
    arrived, pair, _ = lax.optimization_barrier((arrived, pair, stems))
    partial = pack_part(core_row, seen, arrived, pair, q_side, k_side)
    mine, partial = lax.optimization_barrier((mine, partial))
    other = lax.ppermute(mine, "core", FLIP)
    mixed = stem_part(core_row, arrived, mine, other, partial)

    back = lax.all_to_all(
        mixed.reshape(16, tok, 2 * HD), SEQ, split_axis=0, concat_axis=0, tiled=True
    ).reshape(2, KVH, tok, 2 * HD)
    away = lax.dynamic_index_in_dim(back, 1 - core, 0, keepdims=False)
    return gather(core_row, back, lax.ppermute(away, "core", FLIP))[None]


def solution(mesh):
    grid = Mesh(mesh.devices.reshape(4, 2, 4, 4), ("x", "core", "z", "y"))
    dp, seq = ("x", "core"), SEQ
    placed = (
        P(dp, seq, None),
        P(dp, seq, None),
        P(dp, seq, None),
        P(dp, None, seq, None),
        P(dp, None),
        P(dp, None),
        P(),
    )
    return jax.shard_map(
        shards, mesh=grid, in_specs=placed, out_specs=P(dp, seq, None), check_vma=False
    )
```
